32 devices in a mesh: seq: 4 (over x, core), fsdp: 8 (over z, y).
Axes of the slice: x: 2, y: 2, z: 4, core: 2. Of those that a mesh axis runs over, the one named last changes fastest.
Arguments:
- tokens: bfloat16 [8, 4096, 768], P('fsdp', 'seq'), may hold values from -6 to 6
- block_ids: int32 [8, 2048], P('fsdp'), may hold values from 0 to 15, never falling along the last dimension, each value on 1 to 256 neighbouring positions
- ln1_scale: bfloat16 [768], P('fsdp'), may hold values from 0.5 to 1.5
- ln1_bias: bfloat16 [768], P('fsdp'), may hold values from -1 to 1
- qkv_weight: bfloat16 [768, 2304], P('fsdp'), may hold values from -0.21875 to 0.21875
- qkv_bias: bfloat16 [2304], P('fsdp'), may hold values from -1 to 1
- out_weight: bfloat16 [768, 768], P('fsdp'), may hold values from -3.5 to 3.5
- out_bias: bfloat16 [768], P('fsdp'), may hold values from -1 to 1
- ln2_scale: bfloat16 [768], P('fsdp'), may hold values from 0.5 to 1.5
- ln2_bias: bfloat16 [768], P('fsdp'), may hold values from -1 to 1
- up_weight: bfloat16 [768, 3072], P('fsdp'), may hold values from -0.21875 to 0.21875
- up_bias: bfloat16 [3072], P('fsdp'), may hold values from -1 to 1
- down_weight: bfloat16 [3072, 768], P('fsdp'), may hold values from -0.109375 to 0.109375
- down_bias: bfloat16 [768], P('fsdp'), may hold values from -1 to 1
- cotangent: bfloat16 [8, 4096, 768], P('fsdp', 'seq'), may hold values from -6 to 6
Outputs:
- output: bfloat16 [8, 4096, 768], P('fsdp', 'seq')
- input_grad: float32 [8, 4096, 768], P('fsdp', 'seq')
- ln1_scale_grad: float32 [768], P('fsdp')
- ln1_bias_grad: float32 [768], P('fsdp')
- qkv_weight_grad: float32 [768, 2304], P('fsdp')
- qkv_bias_grad: float32 [2304], P('fsdp')
- out_weight_grad: float32 [768, 768], P('fsdp')
- out_bias_grad: float32 [768], P('fsdp')
- ln2_scale_grad: float32 [768], P('fsdp')
- ln2_bias_grad: float32 [768], P('fsdp')
- up_weight_grad: float32 [768, 3072], P('fsdp')
- up_bias_grad: float32 [3072], P('fsdp')
- down_weight_grad: float32 [3072, 768], P('fsdp')
- down_bias_grad: float32 [768], P('fsdp')
The draws below stay inside these ranges and needn't reach their ends.
Inputs may be any that keep to these rules, and one draw needn't show every extreme that they name: `block_ids`: along each sequence the block id never falls; every id from 0 to 15 occurs, each block holds 1 to 256 positions, and some block holds exactly 256.
All inputs are finite; a program needn't handle non-finite values.
Results may differ from the reference program's by a relative error of at most 0.0095.
Values may be sent and summed in bfloat16 or wider, within the bound.
A program may use at most 192 MiB of HBM per device.

```python
import math
import jax
import jax.numpy as jnp
import numpy as np
from jax import lax

D = 768
H = 12
HD = 64
FF = 3072
LEN = 2048
BLOCK = 256
ROWS = 4096
BLOCKS = 16
SEQS = 8


def shard_levels(rng, dims, split, low, high):
    def one(dim, parts):
        draws = jax.random.uniform(jax.random.fold_in(jax.random.fold_in(rng, 6), dim), (parts,), jnp.float32, low / len(split), high / len(split))
        return jnp.repeat(jnp.exp(draws), dims[dim] // parts).reshape((-1,) + (1,) * (len(dims) - dim - 1))

    level = one(*split[0])
    for cut in split[1:]:
        level = level * one(*cut)
    return level


def profile(number_of, total, limit, lean):
    portions = [(1 << 20) // math.isqrt(grade ** lean) + 1 for grade in range(2, number_of + 1)]
    spare, counts = total - limit - (number_of - 1), [1] * (number_of - 1)
    while spare > 0:
        free = [i for i in range(number_of - 1) if counts[i] < limit]
        pool, remaining = sum([portions[i] for i in free]), spare
        for i in free:
            addition = min(limit - counts[i], max(1, remaining * portions[i] // pool), spare)
            counts[i] = counts[i] + addition
            spare = spare - addition
    return np.array([limit] + counts)


def uneven_parts(own_key, number_of, total, reach, skew):
    if number_of == 2:
        one = jax.random.randint(own_key, (), max(1, total - reach), min(reach, total - 1) + 1)
        return jnp.stack([one, total - one])
    tallies = jnp.asarray(profile(number_of, total, reach, skew), jnp.int32)
    pairs = (number_of - 1) // 2
    donor, receiver = tallies[1:1 + 2 * pairs:2], tallies[2:2 + 2 * pairs:2]
    room = jnp.minimum(donor - 1, reach - receiver)
    shifted = jax.random.randint(jax.random.fold_in(own_key, 1), (pairs,), 0, 1 << 20) % (room + 1)
    tallies = tallies.at[1:1 + 2 * pairs:2].set(donor - shifted).at[2:2 + 2 * pairs:2].set(receiver + shifted)
    return tallies[jax.random.permutation(jax.random.fold_in(own_key, 2), number_of)]


def bell_draw(stream_key, extent, scale, most, cuts=(), kind=jnp.bfloat16):
    array = jax.random.normal(stream_key, extent, jnp.float32) * scale
    if len(cuts) > 0:
        array = shard_levels(stream_key, extent, cuts, -0.22, 0.18) * array
    return jnp.clip(array, min=-most, max=most).astype(kind)


def setup_inputs(seed: int = 0) -> dict:
    key_of = jax.random.split(jax.random.key(seed), 16)
    tokens = bell_draw(key_of[0], (SEQS, ROWS, D), 1.0, 6.0, ((0, 8), (1, 4)))
    block_ids = jax.vmap(lambda own: jnp.searchsorted(jnp.cumsum(uneven_parts(own, BLOCKS, LEN, BLOCK, 2)), jnp.arange(LEN), side="right"))(jax.random.split(key_of[1], SEQS)).reshape((SEQS, LEN)).astype(jnp.int32)
    ln1_scale = jnp.clip(1.0 + 0.1 * jax.random.normal(key_of[2], (D,), jnp.float32), 0.5, 1.5).astype(jnp.bfloat16)
    ln1_bias = bell_draw(key_of[3], (D,), 0.2, 1.0, ((0, 8),))
    qkv_weight = bell_draw(key_of[4], (D, 3 * D), D ** -0.5, 0.21875, ((0, 8),))
    qkv_bias = bell_draw(key_of[5], (3 * D,), 0.2, 1.0, ((0, 8),))
    out_weight = bell_draw(key_of[6], (D, D), (max(1, D // 256)) ** -0.5, 3.5, ((0, 8),))
    out_bias = bell_draw(key_of[7], (D,), 0.2, 1.0, ((0, 8),))
    ln2_scale = jnp.clip(1.0 + 0.1 * jax.random.normal(key_of[8], (D,), jnp.float32), 0.5, 1.5).astype(jnp.bfloat16)
    ln2_bias = bell_draw(key_of[9], (D,), 0.2, 1.0, ((0, 8),))
    up_weight = bell_draw(key_of[10], (D, FF), D ** -0.5, 0.21875, ((0, 8),))
    up_bias = bell_draw(key_of[11], (FF,), 0.2, 1.0, ((0, 8),))
    down_weight = bell_draw(key_of[12], (FF, D), FF ** -0.5, 0.109375, ((0, 8),))
    down_bias = bell_draw(key_of[13], (D,), 0.2, 1.0, ((0, 8),))
    cotangent = bell_draw(key_of[14], (SEQS, ROWS, D), 1.0, 6.0, ((0, 8), (1, 4)))
    return dict(tokens=tokens, block_ids=block_ids, ln1_scale=ln1_scale, ln1_bias=ln1_bias, qkv_weight=qkv_weight, qkv_bias=qkv_bias, out_weight=out_weight, out_bias=out_bias, ln2_scale=ln2_scale, ln2_bias=ln2_bias, up_weight=up_weight, up_bias=up_bias, down_weight=down_weight, down_bias=down_bias, cotangent=cotangent)


@jax.custom_vjp
def low(v):
    return lax.optimization_barrier(v.astype(jnp.bfloat16)).astype(jnp.float32)

@jax.custom_vjp
def low_back(v):
    return v

def low_keep(v):
    return (low(v), None)

def low_pass(kept, grad):
    return (grad,)

def back_keep(v):
    return (v, None)

def back_low(kept, grad):
    return (low(grad),)
low.defvjp(low_keep, low_pass)
low_back.defvjp(back_keep, back_low)
HIGHEST_PRECISION = lax.Precision.HIGHEST
EPSILON = 1e-05

def matmul(left, right):
    return jnp.dot(left, right, precision=HIGHEST_PRECISION)

def normalize(values, scale, shift):
    mean_value = lax.optimization_barrier(jnp.mean(values, -1, keepdims=True))
    centred = values - mean_value
    variance = lax.optimization_barrier(jnp.mean(centred * centred, -1, keepdims=True))
    return centred * lax.rsqrt(variance + EPSILON) * scale + shift

def tables(positions, half_dim):
    frequency = jnp.exp(-jnp.log(10000.0) * jnp.arange(half_dim, dtype=jnp.float32) / half_dim)
    angles = positions.astype(jnp.float32)[:, None] * frequency
    return (jnp.cos(angles), jnp.sin(angles))

def rotate(values, cos_table, sin_table):
    half_dim = values.shape[-1] // 2
    first_half = values[..., :half_dim]
    second_half = values[..., half_dim:]
    return jnp.concatenate([first_half * cos_table - second_half * sin_table, first_half * sin_table + second_half * cos_table], -1)

def allowed(query_blocks, query_clean, key_blocks, key_clean):
    noisy_allowed = jnp.where(key_clean[None, :], key_blocks[None, :] < query_blocks[:, None], key_blocks[None, :] == query_blocks[:, None])
    clean_allowed = key_clean[None, :] & (key_blocks[None, :] <= query_blocks[:, None])
    return jnp.where(query_clean[:, None], clean_allowed, noisy_allowed)

def apply_layer(tokens, params, id_table):
    ln1_scale, ln1_bias, qkv_weight, qkv_bias, out_weight, out_bias, ln2_scale, ln2_bias, up_weight, up_bias, down_weight, down_bias = params
    total_rows = tokens.shape[0]
    length = id_table.shape[0]
    query_rows = min(512, total_rows)
    first_in = low(normalize(tokens, ln1_scale, ln1_bias))
    linear = low_back(matmul(first_in, qkv_weight) + qkv_bias).reshape(total_rows, H, 3, HD)
    positions = jnp.arange(total_rows, dtype=jnp.int32) % length
    cos_table, sin_table = tables(positions, HD // 2)
    queries = low(rotate(linear[:, :, 0], cos_table[:, None], sin_table[:, None]))
    key_rows = low(rotate(linear[:, :, 1], cos_table[:, None], sin_table[:, None]))
    values = low(linear[:, :, 2])
    row_blocks = jnp.concatenate([id_table, id_table]).astype(jnp.int32)
    clean_rows = jnp.arange(total_rows, dtype=jnp.int32) >= length

    def attend(offset):
        query_block = lax.dynamic_slice_in_dim(queries, offset, query_rows, 0)
        scores = low_back(jnp.einsum('qhd,khd->hqk', query_block, key_rows, precision=HIGHEST_PRECISION) * 0.125)
        allowed_mask = allowed(lax.dynamic_slice_in_dim(row_blocks, offset, query_rows, 0), lax.dynamic_slice_in_dim(clean_rows, offset, query_rows, 0), row_blocks, clean_rows)
        scores = jnp.where(allowed_mask[None], scores, -1e+30)
        probability = low(jax.nn.softmax(scores, axis=-1))
        return jnp.einsum('hqk,khd->qhd', probability, values, precision=HIGHEST_PRECISION)
    starts = jnp.arange(total_rows // query_rows, dtype=jnp.int32) * query_rows
    pieces = lax.map(jax.checkpoint(attend), starts)
    attended = low_back(low(pieces.reshape(total_rows, H * HD)))
    hidden = tokens + low_back(matmul(attended, out_weight) + out_bias)
    second_in = low(normalize(hidden, ln2_scale, ln2_bias))
    pre_act = low_back(matmul(second_in, up_weight) + up_bias)
    activated = low(jax.nn.gelu(pre_act, approximate=True))
    return hidden + low_back(matmul(activated, down_weight) + down_bias)

def reference(tokens, block_ids, ln1_scale, ln1_bias, qkv_weight, qkv_bias, out_weight, out_bias, ln2_scale, ln2_bias, up_weight, up_bias, down_weight, down_bias, cotangent):
    params = tuple((param.astype(jnp.float32) for param in (ln1_scale, ln1_bias, qkv_weight, qkv_bias, out_weight, out_bias, ln2_scale, ln2_bias, up_weight, up_bias, down_weight, down_bias)))

    def one_sequence(grad_totals, seq_item):
        rows_in, id_table, cot_rows = seq_item
        layer_out, pullback = jax.vjp(lambda rows_x, param_set: apply_layer(rows_x, param_set, id_table), rows_in.astype(jnp.float32), params)
        grad_rows, grad_params = pullback(cot_rows.astype(jnp.float32))
        grad_totals = jax.tree.map(jnp.add, grad_totals, grad_params)
        return (grad_totals, (layer_out.astype(jnp.bfloat16), grad_rows))
    zero_grads = jax.tree.map(jnp.zeros_like, params)
    totals, (outputs, input_grads) = lax.scan(one_sequence, zero_grads, (tokens, block_ids, cotangent))
    return (outputs, input_grads, totals[0], totals[1], totals[2], totals[3], totals[4], totals[5], totals[6], totals[7], totals[8], totals[9], totals[10], totals[11])
```

```python
import functools

import jax
import jax.numpy as jnp
from jax import lax
from jax.experimental import pallas as pl
from jax.experimental.pallas import tpu as pltpu
from jax.sharding import PartitionSpec as P

H = 12
HD = 64
EPSILON = 1e-05
LOG2E = 1.4426950408889634
NEG = -1e30
TQ = 256
TK = 256
TM = 128
BF = jnp.bfloat16
F32 = jnp.float32


def normalize_parts(values):
    mean_value = jnp.mean(values, -1, keepdims=True)
    centred = values - mean_value
    variance = jnp.mean(centred * centred, -1, keepdims=True)
    inverse = lax.rsqrt(variance + EPSILON)
    return (centred * inverse, inverse)


def norm_backward(grad_out, normed, inverse, scale):
    grad_norm = grad_out * scale
    return inverse * (
        grad_norm
        - jnp.mean(grad_norm, -1, keepdims=True)
        - normed * jnp.mean(grad_norm * normed, -1, keepdims=True)
    )


def rows_contract(left, right):
    return lax.dot_general(left, right, (((0,), (0,)), ((), ())), preferred_element_type=F32)


def right_transposed(left, right):
    return lax.dot_general(left, right, (((1,), (1,)), ((), ())), preferred_element_type=F32)


def dot(left, right):
    return jnp.dot(left, right, preferred_element_type=F32)


def qkv_kernel(heads, core_ref, mine, other, cmine, cother, w_ref, vec_ref, bias_ref, cos_ref,
               sin_ref, q_out, k_out, v_out, kc_out, vc_out, a_out, ac_out, wt):
    step = pl.program_id(0)
    span = heads * HD

    @pl.when(step == 0)
    def _():
        whole = jnp.transpose(w_ref[...])
        for h in range(heads):
            for part in range(3):
                wt[part * span + h * HD : part * span + (h + 1) * HD, :] = whole[
                    (3 * h + part) * HD : (3 * h + part + 1) * HD, :
                ]

    def normed(rows):
        values = rows.astype(F32)
        n, _ = normalize_parts(values)
        return (n * vec_ref[0:1, :] + vec_ref[1:2, :]).astype(BF)

    def turn(lin, base, out):
        cos_t, sin_t = cos_ref[...], sin_ref[...]
        half = HD // 2
        for h in range(heads):
            first = lin[base + h * HD : base + h * HD + half, :]
            second = lin[base + h * HD + half : base + (h + 1) * HD, :]
            out[h * HD : h * HD + half, :] = (first * cos_t - second * sin_t).astype(BF)
            out[h * HD + half : (h + 1) * HD, :] = (first * sin_t + second * cos_t).astype(BF)

    quarter = pl.num_programs(0) // 4

    @pl.when(step < 2 * quarter)
    def _():
        a = normed(jnp.where(step < quarter, mine[...], other[...]))
        a_out[...] = a
        lin = right_transposed(wt[...], a) + bias_ref[...]
        turn(lin, 0, q_out)
        turn(lin, span, k_out)
        v_out[...] = lin[2 * span :, :].astype(BF)

    @pl.when(step >= 2 * quarter)
    def _():
        a = normed(jnp.where(step < 3 * quarter, cmine[...], cother[...]))
        ac_out[...] = a
        lin = right_transposed(wt[span:, :], a) + bias_ref[span:, :]
        turn(lin, 0, kc_out)
        vc_out[...] = lin[span:, :].astype(BF)


def project(core, mine, other, cmine, cother, weight, vec, bias, cos_t, sin_t, heads):
    local, width = mine.shape
    span = heads * HD
    tile = 256
    n = local // tile

    def place(t, c):
        mine_first = jnp.where(t % (2 * n) < n, c[0], 1 - c[0])
        return mine_first * n + t % n

    def src(k):
        return pl.BlockSpec((tile, width), lambda t, c: (jnp.clip(t - k * n, 0, n - 1), 0))

    whole = lambda shape: pl.BlockSpec(shape, lambda t, c: (0, 0))
    own = pl.BlockSpec((span, tile), lambda t, c: (0, place(jnp.minimum(t, 2 * n - 1), c)))
    cln = pl.BlockSpec((span, tile), lambda t, c: (0, place(jnp.maximum(t, 2 * n), c)))
    own_a = pl.BlockSpec((tile, width), lambda t, c: (place(jnp.minimum(t, 2 * n - 1), c), 0))
    cln_a = pl.BlockSpec((tile, width), lambda t, c: (place(jnp.maximum(t, 2 * n), c), 0))
    tab = pl.BlockSpec((HD // 2, tile), lambda t, c: (0, place(t, c)))
    head_shape = jax.ShapeDtypeStruct((span, 2 * local), BF)
    row_shape = jax.ShapeDtypeStruct((2 * local, width), BF)
    return pl.pallas_call(
        functools.partial(qkv_kernel, heads),
        grid_spec=pltpu.PrefetchScalarGridSpec(
            num_scalar_prefetch=1,
            grid=(4 * n,),
            in_specs=[src(0), src(1), src(2), src(3), whole((width, 3 * span)), whole(vec.shape),
                      whole(bias.shape), tab, tab],
            out_specs=[own, own, own, cln, cln, own_a, cln_a],
            scratch_shapes=[pltpu.VMEM((3 * span, width), BF)],
        ),
        out_shape=[head_shape] * 5 + [row_shape] * 2,
        name="project",
    )(core, mine, other, cmine, cother, weight, vec, bias, cos_t, sin_t)


def attend_kernel(group, bounds, q, k, v, kc, vc, id_row, id_col, o_out, lse_out, ks, kcs, vs,
                  vcs):
    total = q.shape[1]
    scale = LOG2E * HD**-0.5
    ones = jnp.ones((16, total), BF)
    for h in range(group):
        rows = slice(h * HD, (h + 1) * HD)
        ks[h] = jnp.transpose(k[rows, :])
        kcs[h] = jnp.transpose(kc[rows, :])
        vs[h, :HD] = v[rows, :]
        vcs[h, :HD] = vc[rows, :]
        vs[h, HD:] = ones
        vcs[h, HD:] = ones
    lift = bounds[4, 0]

    def one_tile(i, _):
        at = pl.ds(pl.multiple_of(i * TQ, TQ), TQ)
        queries = [q[h * HD : (h + 1) * HD, at] for h in range(group)]
        q_ids = id_row[0:1, at]

        def update(state, key_ref, val_ref, keys, mask):
            out = []
            for h in range(group):
                m, acc = state[2 * h], state[2 * h + 1]
                s = dot(key_ref[h, keys, :], queries[h])
                if mask is not None:
                    s = jnp.where(mask, s, NEG)
                m_new = jnp.maximum(m, jnp.max(s, 0, keepdims=True))
                p = jnp.exp2((s - m_new) * scale).astype(BF)
                alpha = jnp.exp2((m - m_new) * scale)
                acc = acc * alpha + dot(val_ref[h, :, keys], p)
                out += [m_new, acc]
            return tuple(out)

        def key_ids(keys):
            col = id_col[keys, :]
            return jnp.concatenate([col] * (TQ // 128), 1)

        def band(j, state):
            keys = pl.ds(pl.multiple_of(j * TM, TM), TM)
            return update(state, ks, vs, keys, key_ids(keys) == q_ids)

        def full(j, state):
            keys = pl.ds(pl.multiple_of(j * TK, TK), TK)
            return update(state, kcs, vcs, keys, None)

        def edge(j, state):
            keys = pl.ds(pl.multiple_of(j * TM, TM), TM)
            return update(state, kcs, vcs, keys, key_ids(keys) < q_ids + lift)

        state = (jnp.full((1, TQ), NEG, F32), jnp.zeros((HD + 16, TQ), F32)) * group
        state = lax.fori_loop(bounds[2, i], bounds[3, i], band, state)
        state = lax.fori_loop(0, bounds[0, i], full, state)
        state = lax.fori_loop(bounds[0, i] * (TK // TM), bounds[1, i], edge, state)
        for h in range(group):
            m, acc = state[2 * h], state[2 * h + 1]
            total_w = acc[HD : HD + 1, :]
            o_out[h * HD : (h + 1) * HD, at] = (acc[:HD, :] / total_w).astype(BF)
            lse_out[h, :, at] = jnp.broadcast_to(m * scale + jnp.log2(total_w), (8, TQ))
        return 0

    lax.fori_loop(0, total // TQ, one_tile, 0)


def attend(bounds, q, k, v, kc, vc, id_row, id_col, heads, group):
    total = q.shape[1]
    head = pl.BlockSpec((group * HD, total), lambda g, b: (g, 0))
    whole = lambda shape: pl.BlockSpec(shape, lambda g, b: (0, 0))
    return pl.pallas_call(
        functools.partial(attend_kernel, group),
        grid_spec=pltpu.PrefetchScalarGridSpec(
            num_scalar_prefetch=1,
            grid=(heads // group,),
            in_specs=[head] * 5 + [whole(id_row.shape), whole(id_col.shape)],
            out_specs=[head, pl.BlockSpec((group, 8, total), lambda g, b: (g, 0, 0))],
            scratch_shapes=[pltpu.VMEM((group, total, HD), BF)] * 2
            + [pltpu.VMEM((group, HD + 16, total), BF)] * 2,
        ),
        out_shape=[
            jax.ShapeDtypeStruct((heads * HD, total), BF),
            jax.ShapeDtypeStruct((heads, 8, total), F32),
        ],
        name="attend",
    )(bounds, q, k, v, kc, vc, id_row, id_col)


def attend_back_kernel(group, bounds, q, k, v, kc, vc, o, lse, do_mine, do_other, id_row, id_col,
                       cos_ref, sin_ref, own_out, cln_out, ks, vs, kcs, vcs, qs, dos, dot_s,
                       dk_acc, dv_acc, dkc_acc, dvc_acc, dq_acc):
    total = q.shape[1]
    half_rows = total // 2
    scale = LOG2E * HD**-0.5
    lift = bounds[4, 0]
    core = bounds[4, 1]
    near = pl.ds(pl.multiple_of(core * half_rows, 128), half_rows)
    far = pl.ds(pl.multiple_of((1 - core) * half_rows, 128), half_rows)
    dot_s[:, near] = do_mine[...]
    dot_s[:, far] = do_other[...]
    for h in range(group):
        rows = slice(h * HD, (h + 1) * HD)
        ks[h] = jnp.transpose(k[rows, :])
        vs[h] = jnp.transpose(v[rows, :])
        kcs[h] = jnp.transpose(kc[rows, :])
        vcs[h] = jnp.transpose(vc[rows, :])
        qs[h] = jnp.transpose(q[rows, :])
        dos[h] = jnp.transpose(dot_s[rows, :])
    for ref in (dk_acc, dv_acc, dkc_acc, dvc_acc):
        ref[...] = jnp.zeros_like(ref)

    def one_tile(i, _):
        at = pl.ds(pl.multiple_of(i * TQ, TQ), TQ)
        q_ids = id_row[0:1, at]
        queries, grads, deltas, sums, q_rows, g_rows = [], [], [], [], [], []
        for h in range(group):
            rows = slice(h * HD, (h + 1) * HD)
            queries.append(q[rows, at])
            g = dot_s[rows, at]
            grads.append(g)
            deltas.append(jnp.sum(g.astype(F32) * o[rows, at].astype(F32), 0, keepdims=True))
            sums.append(lse[h, 0:1, at])
            q_rows.append(qs[h, at, :])
            g_rows.append(dos[h, at, :])

        def update(state, key_ref, val_ref, key_cols, dk, dv, keys, mask):
            out = []
            for h in range(group):
                s = dot(key_ref[h, keys, :], queries[h])
                p = jnp.exp2(s * scale - sums[h])
                if mask is not None:
                    p = jnp.where(mask, p, 0.0)
                dp = dot(val_ref[h, keys, :], grads[h])
                ds = (p * (dp - deltas[h])).astype(BF)
                dv[h, keys, :] += dot(p.astype(BF), g_rows[h])
                dk[h, keys, :] += dot(ds, q_rows[h])
                out.append(state[h] + dot(key_cols[h * HD : (h + 1) * HD, keys], ds))
            return tuple(out)

        def key_ids(keys):
            col = id_col[keys, :]
            return jnp.concatenate([col] * (TQ // 128), 1)

        def band(j, state):
            keys = pl.ds(pl.multiple_of(j * TM, TM), TM)
            return update(state, ks, vs, k, dk_acc, dv_acc, keys, key_ids(keys) == q_ids)

        def full(j, state):
            keys = pl.ds(pl.multiple_of(j * TK, TK), TK)
            return update(state, kcs, vcs, kc, dkc_acc, dvc_acc, keys, None)

        def edge(j, state):
            keys = pl.ds(pl.multiple_of(j * TM, TM), TM)
            mask = key_ids(keys) < q_ids + lift
            return update(state, kcs, vcs, kc, dkc_acc, dvc_acc, keys, mask)

        state = (jnp.zeros((HD, TQ), F32),) * group
        state = lax.fori_loop(bounds[2, i], bounds[3, i], band, state)
        state = lax.fori_loop(0, bounds[0, i], full, state)
        state = lax.fori_loop(bounds[0, i] * (TK // TM), bounds[1, i], edge, state)
        for h in range(group):
            dq_acc[h * HD : (h + 1) * HD, at] = state[h]
        return 0

    lax.fori_loop(0, total // TQ, one_tile, 0)

    half = HD // 2
    cos_t, sin_t = cos_ref[...], sin_ref[...]
    noisy = lift == 0

    def back_turn(w, out, base):
        first, second = w[:half, :], w[half:, :]
        out[base : base + half, :] = (first * cos_t + second * sin_t).astype(BF)
        out[base + half : base + HD, :] = (second * cos_t - first * sin_t).astype(BF)

    for h in range(group):
        back_turn(dq_acc[h * HD : (h + 1) * HD, :] * HD**-0.5, own_out, 3 * h * HD)
        band_k = jnp.where(noisy, dk_acc[h], dkc_acc[h])
        band_v = jnp.where(noisy, dv_acc[h], dvc_acc[h])
        back_turn(jnp.transpose(band_k) * HD**-0.5, own_out, (3 * h + 1) * HD)
        own_out[(3 * h + 2) * HD : (3 * h + 3) * HD, :] = jnp.transpose(band_v).astype(BF)
        back_turn(jnp.transpose(dkc_acc[h]) * HD**-0.5, cln_out, 2 * h * HD)
        cln_out[(2 * h + 1) * HD : (2 * h + 2) * HD, :] = jnp.transpose(dvc_acc[h]).astype(BF)


def attend_back(bounds, q, k, v, kc, vc, o, lse, do_mine, do_other, id_row, id_col, cos_t, sin_t,
                heads, group):
    total = q.shape[1]
    head = pl.BlockSpec((group * HD, total), lambda g, b: (g, 0))
    halfhead = pl.BlockSpec((group * HD, total // 2), lambda g, b: (g, 0))
    whole = lambda shape: pl.BlockSpec(shape, lambda g, b: (0, 0))
    rows16 = pltpu.VMEM((group, total, HD), BF)
    rows32 = pltpu.VMEM((group, total, HD), F32)
    return pl.pallas_call(
        functools.partial(attend_back_kernel, group),
        grid_spec=pltpu.PrefetchScalarGridSpec(
            num_scalar_prefetch=1,
            grid=(heads // group,),
            in_specs=[head] * 6
            + [pl.BlockSpec((group, 8, total), lambda g, b: (g, 0, 0)), halfhead, halfhead]
            + [whole(id_row.shape), whole(id_col.shape), whole(cos_t.shape), whole(sin_t.shape)],
            out_specs=[
                pl.BlockSpec((group * 3 * HD, total), lambda g, b: (g, 0)),
                pl.BlockSpec((group * 2 * HD, total), lambda g, b: (g, 0)),
            ],
            scratch_shapes=[rows16] * 6
            + [pltpu.VMEM((group * HD, total), BF)]
            + [rows32] * 4
            + [pltpu.VMEM((group * HD, total), F32)],
        ),
        out_shape=[
            jax.ShapeDtypeStruct((heads * 3 * HD, total), BF),
            jax.ShapeDtypeStruct((heads * 2 * HD, total), BF),
        ],
        name="attend_back",
    )(bounds, q, k, v, kc, vc, o, lse, do_mine, do_other, id_row, id_col, cos_t, sin_t)


def on_device(
    tokens,
    block_ids,
    ln1_scale,
    ln1_bias,
    qkv_weight,
    qkv_bias,
    out_weight,
    out_bias,
    ln2_scale,
    ln2_bias,
    up_weight,
    up_bias,
    down_weight,
    down_bias,
    cotangent,
):
    tok = tokens[0]
    local_rows, width = tok.shape
    ids = block_ids[0].astype(jnp.int32)
    length = ids.shape[0]
    shard = ln1_scale.shape[0]
    heads = H // 2
    span = heads * HD
    me = lax.axis_index("seq")
    core = me % 2
    noisy = me < 2
    swap = [(0, 1), (1, 0), (2, 3), (3, 2)]
    other = lax.ppermute(tok, "seq", swap)
    clean_in = lax.ppermute(tok, "seq", [(2, 0), (3, 1)])
    clean_mine = jnp.where(noisy, clean_in, tok)
    clean_other = lax.ppermute(clean_mine, "seq", swap)

    q_cols = lax.dynamic_slice_in_dim(qkv_weight, core * 3 * span, 3 * span, 1)
    small = jnp.concatenate(
        [
            ln1_scale.reshape(1, shard),
            ln1_bias.reshape(1, shard),
            out_bias.reshape(1, shard),
            ln2_scale.reshape(1, shard),
            ln2_bias.reshape(1, shard),
            down_bias.reshape(1, shard),
            qkv_bias.reshape(-1, shard),
            up_bias.reshape(-1, shard),
        ],
        0,
    )
    n_small = small.shape[0]
    small = jnp.pad(small, ((0, 128 - n_small), (0, 0))).T
    gathered = lax.all_gather(
        jnp.concatenate([q_cols, small], 1), "fsdp", axis=0, tiled=True
    )
    n_fsdp = width // shard
    vectors = gathered[:, 3 * span :].reshape(n_fsdp, shard, 128)[:, :, :n_small]
    vectors = jnp.transpose(vectors, (2, 0, 1)).astype(F32)
    flat = vectors[:6].reshape(6, width)
    qkv_b = jnp.transpose(vectors[6:9], (1, 0, 2)).reshape(-1)
    up_b = jnp.transpose(vectors[9:], (1, 0, 2)).reshape(-1)
    scale_one, shift_one, out_shift, scale_two, shift_two, down_shift = [flat[i] for i in range(6)]

    out_full = lax.all_gather(out_weight, "fsdp", axis=0, tiled=True)
    up_full = lax.all_gather(up_weight, "fsdp", axis=0, tiled=True)
    down_full = lax.all_gather(down_weight, "fsdp", axis=0, tiled=True)

    frequency = jnp.exp(-jnp.log(10000.0) * jnp.arange(HD // 2, dtype=F32) / (HD // 2))
    angles = frequency[:, None] * jnp.arange(length, dtype=F32)[None, :]
    cos_t, sin_t = jnp.cos(angles), jnp.sin(angles)

    first = ids[::TQ][:, None]
    last = ids[TQ - 1 :: TQ][:, None]
    before = lambda edge: jnp.sum((ids[None, :] < edge).astype(jnp.int32), 1)
    start_first, end_first = before(first), before(first + 1)
    start_last, end_last = before(last), before(last + 1)
    ceil_m = lambda value: (value + TM - 1) // TM
    lift = jnp.where(noisy, 0, 1)
    zero = jnp.zeros_like(start_first)
    bounds = jnp.stack(
        [
            jnp.where(noisy, start_first, end_first) // TK,
            ceil_m(jnp.where(noisy, start_last, end_last)),
            jnp.where(noisy, start_first // TM, zero),
            jnp.where(noisy, ceil_m(end_last), zero),
            zero + jnp.where(jnp.arange(zero.shape[0]) == 0, lift, core),
        ]
    ).astype(jnp.int32)
    id_row = jnp.broadcast_to(ids[None, :], (8, length))
    id_col = jnp.broadcast_to(ids[:, None], (length, 128))

    vec = jnp.concatenate([scale_one[None], shift_one[None], jnp.zeros((6, width), F32)], 0)
    bias_own = lax.dynamic_slice_in_dim(qkv_b, core * 3 * span, 3 * span, 0)
    bias_own = jnp.transpose(bias_own.reshape(heads, 3, HD), (1, 0, 2)).reshape(3 * span, 1)
    q, k, v, kc, vc, a_own, a_clean = project(
        core.reshape(1).astype(jnp.int32), tok, other, clean_mine, clean_other, gathered, vec,
        bias_own, cos_t, sin_t, heads
    )
    o, lse = attend(bounds, q, k, v, kc, vc, id_row, id_col, heads, 2)
    cut = lambda value, which: lax.dynamic_slice_in_dim(value, which * local_rows, local_rows, 1)
    o_mine = cut(o, core)
    o_in = lax.ppermute(cut(o, 1 - core), "seq", swap)
    attended = jnp.where(
        core == 0, jnp.concatenate([o_mine, o_in], 0), jnp.concatenate([o_in, o_mine], 0)
    )

    rows_in = tok.astype(F32)
    hidden = rows_in + rows_contract(attended, out_full) + out_shift
    normed_two, inverse_two = normalize_parts(hidden)
    second_in = (normed_two * scale_two + shift_two).astype(BF)
    pre_act = dot(second_in, up_full) + up_b
    activated, gelu_pull = jax.vjp(
        lambda pre_value: jax.nn.gelu(pre_value, approximate=True), pre_act
    )
    act_low = activated.astype(BF)
    result = hidden + dot(act_low, down_full) + down_shift

    grad_branch = cotangent[0]
    grad_top = grad_branch.astype(F32)
    grad_down_w = rows_contract(act_low, grad_branch)
    grad_down_b = jnp.sum(grad_top, 0)
    grad_act = right_transposed(grad_branch, down_full)
    grad_pre = gelu_pull(grad_act)[0].astype(BF)
    grad_up_w = rows_contract(second_in, grad_pre)
    grad_up_b = jnp.sum(grad_pre.astype(F32), 0)
    grad_second = right_transposed(grad_pre, up_full)
    grad_scale_two = jnp.sum(grad_second * normed_two, 0)
    grad_shift_two = jnp.sum(grad_second, 0)
    grad_hidden = grad_top + norm_backward(grad_second, normed_two, inverse_two, scale_two)

    grad_attn = grad_hidden.astype(BF)
    grad_out_w = dot(attended, grad_attn)
    grad_out_b = jnp.sum(grad_attn.astype(F32), 0)
    grad_o = right_transposed(out_full, grad_attn).astype(BF)
    cut_heads = lambda which: lax.dynamic_slice_in_dim(grad_o, which * span, span, 0)
    do_mine = cut_heads(core)
    do_in = lax.ppermute(cut_heads(1 - core), "seq", swap)
    down_part = lax.psum_scatter(grad_down_w.astype(BF), "fsdp", scatter_dimension=0, tiled=True)
    up_part = lax.psum_scatter(grad_up_w.astype(BF), "fsdp", scatter_dimension=0, tiled=True)
    out_part = lax.psum_scatter(grad_out_w.astype(BF), "fsdp", scatter_dimension=0, tiled=True)

    own_grad, clean_grad = attend_back(
        bounds, q, k, v, kc, vc, o, lse, do_mine, do_in, id_row, id_col, cos_t, sin_t, heads, 2
    )
    from_noisy = lax.ppermute(clean_grad, "seq", [(0, 2), (1, 3)])
    own_grad = own_grad.reshape(heads, 3 * HD, length)
    own_grad = own_grad.at[:, HD:].add(from_noisy.reshape(heads, 2 * HD, length))
    own_grad = own_grad.reshape(3 * span, length)
    grad_qkv_w = lax.dot_general(
        a_own, own_grad, (((0,), (1,)), ((), ())), preferred_element_type=F32
    )
    grad_qkv_b = jnp.sum(own_grad.astype(F32), 1)
    qkv_part = lax.psum_scatter(grad_qkv_w.astype(BF), "fsdp", scatter_dimension=0, tiled=True)
    grad_first = lax.dot_general(
        own_grad, gathered[:, : 3 * span], (((0,), (1,)), ((), ())), preferred_element_type=F32
    )
    cut_rows = lambda which: lax.dynamic_slice_in_dim(grad_first, which * local_rows, local_rows, 0)
    grad_first = cut_rows(core) + lax.ppermute(
        cut_rows(1 - core).astype(BF), "seq", swap
    ).astype(F32)
    normed_one, inverse_one = normalize_parts(rows_in)
    grad_scale_one = jnp.sum(grad_first * normed_one, 0)
    grad_shift_one = jnp.sum(grad_first, 0)
    grad_rows = grad_hidden + norm_backward(grad_first, normed_one, inverse_one, scale_one)

    grad_qkv_b = lax.dynamic_update_slice_in_dim(
        jnp.zeros((2 * 3 * span,), F32), grad_qkv_b, core * 3 * span, 0
    )
    pieces = [
        grad_scale_one, grad_shift_one, grad_qkv_b, grad_out_b, grad_scale_two, grad_shift_two,
        grad_up_b, grad_down_b,
    ]
    sizes = [piece.shape[0] for piece in pieces]
    packed = lax.psum(jnp.concatenate(pieces), ("fsdp", "seq"))
    index = lax.axis_index("fsdp")
    small_out, at = [], 0
    for size in sizes:
        mine = size // n_fsdp
        small_out.append(lax.dynamic_slice_in_dim(packed, at + index * mine, mine, 0))
        at += size

    qkv_wide = lax.dynamic_update_slice_in_dim(
        jnp.zeros((shard, 2 * 3 * span), F32), qkv_part.astype(F32), core * 3 * span, 1
    )
    qkv_g, out_g, up_g, down_g = lax.psum(
        (qkv_wide, out_part.astype(F32), up_part.astype(F32), down_part.astype(F32)), "seq"
    )
    return (
        result.astype(BF)[None],
        grad_rows[None],
        small_out[0],
        small_out[1],
        qkv_g,
        small_out[2],
        out_g,
        small_out[3],
        small_out[4],
        small_out[5],
        up_g,
        small_out[6],
        down_g,
        small_out[7],
    )


def solution(mesh):
    row, mat, vec = P("fsdp", "seq", None), P("fsdp", None), P("fsdp")
    in_specs = (row, mat, vec, vec, mat, vec, mat, vec, vec, vec, mat, vec, mat, vec, row)
    out_specs = (row, row, vec, vec, mat, vec, mat, vec, vec, vec, mat, vec, mat, vec)
    return jax.shard_map(
        on_device, mesh=mesh, in_specs=in_specs, out_specs=out_specs, check_vma=False
    )
```

```python
import functools

import jax
import jax.numpy as jnp
from jax import lax
from jax.experimental import pallas as pl
from jax.experimental.pallas import tpu as pltpu
from jax.sharding import PartitionSpec as P

H = 12
HD = 64
EPSILON = 1e-05
LOG2E = 1.4426950408889634
NEG = -1e30
TQ = 512
TK = 256
TM = 256
BF = jnp.bfloat16
F32 = jnp.float32


def normalize_parts(values):
    mean_value = jnp.mean(values, -1, keepdims=True)
    centred = values - mean_value
    variance = jnp.mean(centred * centred, -1, keepdims=True)
    inverse = lax.rsqrt(variance + EPSILON)
    return (centred * inverse, inverse)


def norm_backward(grad_out, normed, inverse, scale):
    grad_norm = grad_out * scale
    return inverse * (
        grad_norm
        - jnp.mean(grad_norm, -1, keepdims=True)
        - normed * jnp.mean(grad_norm * normed, -1, keepdims=True)
    )


def rows_contract(left, right):
    return lax.dot_general(left, right, (((0,), (0,)), ((), ())), preferred_element_type=F32)


def right_transposed(left, right):
    return lax.dot_general(left, right, (((1,), (1,)), ((), ())), preferred_element_type=F32)


def dot(left, right):
    return jnp.dot(left, right, preferred_element_type=F32)


def qkv_kernel(heads, core_ref, mine, other, cmine, cother, w_ref, vec_ref, bias_ref, cos_ref,
               sin_ref, q_out, k_out, v_out, kc_out, vc_out, a_out, ac_out, wt):
    step = pl.program_id(0)
    span = heads * HD

    @pl.when(step == 0)
    def _():
        whole = jnp.transpose(w_ref[...])
        for h in range(heads):
            for part in range(3):
                wt[part * span + h * HD : part * span + (h + 1) * HD, :] = whole[
                    (3 * h + part) * HD : (3 * h + part + 1) * HD, :
                ]

    def normed(rows):
        values = rows.astype(F32)
        n, _ = normalize_parts(values)
        return (n * vec_ref[0:1, :] + vec_ref[1:2, :]).astype(BF)

    def turn(lin, base, out):
        cos_t, sin_t = cos_ref[...], sin_ref[...]
        half = HD // 2
        for h in range(heads):
            first = lin[base + h * HD : base + h * HD + half, :]
            second = lin[base + h * HD + half : base + (h + 1) * HD, :]
            out[h * HD : h * HD + half, :] = (first * cos_t - second * sin_t).astype(BF)
            out[h * HD + half : (h + 1) * HD, :] = (first * sin_t + second * cos_t).astype(BF)

    quarter = pl.num_programs(0) // 4

    @pl.when(step < 2 * quarter)
    def _():
        a = normed(jnp.where(step < quarter, mine[...], other[...]))
        a_out[...] = a
        lin = right_transposed(wt[...], a) + bias_ref[...]
        turn(lin, 0, q_out)
        turn(lin, span, k_out)
        v_out[...] = lin[2 * span :, :].astype(BF)

    @pl.when(step >= 2 * quarter)
    def _():
        a = normed(jnp.where(step < 3 * quarter, cmine[...], cother[...]))
        ac_out[...] = a
        lin = right_transposed(wt[span:, :], a) + bias_ref[span:, :]
        turn(lin, 0, kc_out)
        vc_out[...] = lin[span:, :].astype(BF)


def project(core, mine, other, cmine, cother, weight, vec, bias, cos_t, sin_t, heads):
    local, width = mine.shape
    span = heads * HD
    tile = 256
    n = local // tile

    def place(t, c):
        mine_first = jnp.where(t % (2 * n) < n, c[0], 1 - c[0])
        return mine_first * n + t % n

    def src(k):
        return pl.BlockSpec((tile, width), lambda t, c: (jnp.clip(t - k * n, 0, n - 1), 0))

    whole = lambda shape: pl.BlockSpec(shape, lambda t, c: (0, 0))
    own = pl.BlockSpec((span, tile), lambda t, c: (0, place(jnp.minimum(t, 2 * n - 1), c)))
    cln = pl.BlockSpec((span, tile), lambda t, c: (0, place(jnp.maximum(t, 2 * n), c)))
    own_a = pl.BlockSpec((tile, width), lambda t, c: (place(jnp.minimum(t, 2 * n - 1), c), 0))
    cln_a = pl.BlockSpec((tile, width), lambda t, c: (place(jnp.maximum(t, 2 * n), c), 0))
    tab = pl.BlockSpec((HD // 2, tile), lambda t, c: (0, place(t, c)))
    head_shape = jax.ShapeDtypeStruct((span, 2 * local), BF)
    row_shape = jax.ShapeDtypeStruct((2 * local, width), BF)
    return pl.pallas_call(
        functools.partial(qkv_kernel, heads),
        grid_spec=pltpu.PrefetchScalarGridSpec(
            num_scalar_prefetch=1,
            grid=(4 * n,),
            in_specs=[src(0), src(1), src(2), src(3), whole((width, 3 * span)), whole(vec.shape),
                      whole(bias.shape), tab, tab],
            out_specs=[own, own, own, cln, cln, own_a, cln_a],
            scratch_shapes=[pltpu.VMEM((3 * span, width), BF)],
        ),
        out_shape=[head_shape] * 5 + [row_shape] * 2,
        name="project",
    )(core, mine, other, cmine, cother, weight, vec, bias, cos_t, sin_t)


def attend_kernel(group, bounds, q, k, v, kc, vc, id_row, id_col, o_out, lse_out, ks, kcs, vs,
                  vcs):
    total = q.shape[1]
    scale = LOG2E * HD**-0.5
    ones = jnp.ones((16, total), BF)
    for h in range(group):
        rows = slice(h * HD, (h + 1) * HD)
        ks[h] = jnp.transpose(k[rows, :])
        kcs[h] = jnp.transpose(kc[rows, :])
        vs[h, :HD] = v[rows, :]
        vcs[h, :HD] = vc[rows, :]
        vs[h, HD:] = ones
        vcs[h, HD:] = ones
    lift = bounds[4, 0]

    def one_tile(i, _):
        at = pl.ds(pl.multiple_of(i * TQ, TQ), TQ)
        queries = [q[h * HD : (h + 1) * HD, at] for h in range(group)]
        q_ids = id_row[0:1, at]

        def update(state, key_ref, val_ref, keys, mask):
            out = []
            for h in range(group):
                m, acc = state[2 * h], state[2 * h + 1]
                s = dot(key_ref[h, keys, :], queries[h])
                if mask is not None:
                    s = jnp.where(mask, s, NEG)
                m_new = jnp.maximum(m, jnp.max(s, 0, keepdims=True))
                p = jnp.exp2((s - m_new) * scale).astype(BF)
                alpha = jnp.exp2((m - m_new) * scale)
                acc = acc * alpha + dot(val_ref[h, :, keys], p)
                out += [m_new, acc]
            return tuple(out)

        def key_ids(keys):
            col = id_col[keys, :]
            return jnp.concatenate([col] * (TQ // 128), 1)

        def band(j, state):
            keys = pl.ds(pl.multiple_of(j * TM, TM), TM)
            return update(state, ks, vs, keys, key_ids(keys) == q_ids)

        def full(j, state):
            keys = pl.ds(pl.multiple_of(j * TK, TK), TK)
            return update(state, kcs, vcs, keys, None)

        def edge(j, state):
            keys = pl.ds(pl.multiple_of(j * TM, TM), TM)
            return update(state, kcs, vcs, keys, key_ids(keys) < q_ids + lift)

        state = (jnp.full((1, TQ), NEG, F32), jnp.zeros((HD + 16, TQ), F32)) * group
        state = lax.fori_loop(bounds[2, i], bounds[3, i], band, state)
        state = lax.fori_loop(0, bounds[0, i], full, state)
        state = lax.fori_loop(bounds[0, i] * (TK // TM), bounds[1, i], edge, state)
        for h in range(group):
            m, acc = state[2 * h], state[2 * h + 1]
            total_w = acc[HD : HD + 1, :]
            o_out[h * HD : (h + 1) * HD, at] = (acc[:HD, :] / total_w).astype(BF)
            lse_out[h, :, at] = jnp.broadcast_to(m * scale + jnp.log2(total_w), (8, TQ))
        return 0

    lax.fori_loop(0, total // TQ, one_tile, 0)


def attend(bounds, q, k, v, kc, vc, id_row, id_col, heads, group):
    total = q.shape[1]
    head = pl.BlockSpec((group * HD, total), lambda g, b: (g, 0))
    whole = lambda shape: pl.BlockSpec(shape, lambda g, b: (0, 0))
    return pl.pallas_call(
        functools.partial(attend_kernel, group),
        grid_spec=pltpu.PrefetchScalarGridSpec(
            num_scalar_prefetch=1,
            grid=(heads // group,),
            in_specs=[head] * 5 + [whole(id_row.shape), whole(id_col.shape)],
            out_specs=[head, pl.BlockSpec((group, 8, total), lambda g, b: (g, 0, 0))],
            scratch_shapes=[pltpu.VMEM((group, total, HD), BF)] * 2
            + [pltpu.VMEM((group, HD + 16, total), BF)] * 2,
        ),
        out_shape=[
            jax.ShapeDtypeStruct((heads * HD, total), BF),
            jax.ShapeDtypeStruct((heads, 8, total), F32),
        ],
        name="attend",
    )(bounds, q, k, v, kc, vc, id_row, id_col)


def attend_back_kernel(group, bounds, q, k, v, kc, vc, o, lse, do_mine, do_other, id_row, id_col,
                       cos_ref, sin_ref, own_out, cln_out, ks, vs, kcs, vcs, qs, dos, dot_s,
                       dk_acc, dv_acc, dkc_acc, dvc_acc, dq_acc):
    total = q.shape[1]
    half_rows = total // 2
    scale = LOG2E * HD**-0.5
    lift = bounds[4, 0]
    core = bounds[4, 1]
    near = pl.ds(pl.multiple_of(core * half_rows, 128), half_rows)
    far = pl.ds(pl.multiple_of((1 - core) * half_rows, 128), half_rows)
    dot_s[:, near] = do_mine[...]
    dot_s[:, far] = do_other[...]
    for h in range(group):
        rows = slice(h * HD, (h + 1) * HD)
        ks[h] = jnp.transpose(k[rows, :])
        vs[h] = jnp.transpose(v[rows, :])
        kcs[h] = jnp.transpose(kc[rows, :])
        vcs[h] = jnp.transpose(vc[rows, :])
        qs[h] = jnp.transpose(q[rows, :])
        dos[h] = jnp.transpose(dot_s[rows, :])
    for ref in (dk_acc, dv_acc, dkc_acc, dvc_acc):
        ref[...] = jnp.zeros_like(ref)

    def one_tile(i, _):
        at = pl.ds(pl.multiple_of(i * TQ, TQ), TQ)
        q_ids = id_row[0:1, at]
        queries, grads, deltas, sums, q_rows, g_rows = [], [], [], [], [], []
        for h in range(group):
            rows = slice(h * HD, (h + 1) * HD)
            queries.append(q[rows, at])
            g = dot_s[rows, at]
            grads.append(g)
            deltas.append(jnp.sum(g.astype(F32) * o[rows, at].astype(F32), 0, keepdims=True))
            sums.append(lse[h, 0:1, at])
            q_rows.append(qs[h, at, :])
            g_rows.append(dos[h, at, :])

        def update(state, key_ref, val_ref, key_cols, dk, dv, keys, mask):
            out = []
            for h in range(group):
                s = dot(key_ref[h, keys, :], queries[h])
                p = jnp.exp2(s * scale - sums[h])
                if mask is not None:
                    p = jnp.where(mask, p, 0.0)
                dp = dot(val_ref[h, keys, :], grads[h])
                ds = (p * (dp - deltas[h])).astype(BF)
                dv[h, keys, :] += dot(p.astype(BF), g_rows[h])
                dk[h, keys, :] += dot(ds, q_rows[h])
                out.append(state[h] + dot(key_cols[h * HD : (h + 1) * HD, keys], ds))
            return tuple(out)

        def key_ids(keys):
            col = id_col[keys, :]
            return jnp.concatenate([col] * (TQ // 128), 1)

        def band(j, state):
            keys = pl.ds(pl.multiple_of(j * TM, TM), TM)
            return update(state, ks, vs, k, dk_acc, dv_acc, keys, key_ids(keys) == q_ids)

        def full(j, state):
            keys = pl.ds(pl.multiple_of(j * TK, TK), TK)
            return update(state, kcs, vcs, kc, dkc_acc, dvc_acc, keys, None)

        def edge(j, state):
            keys = pl.ds(pl.multiple_of(j * TM, TM), TM)
            mask = key_ids(keys) < q_ids + lift
            return update(state, kcs, vcs, kc, dkc_acc, dvc_acc, keys, mask)

        state = (jnp.zeros((HD, TQ), F32),) * group
        state = lax.fori_loop(bounds[2, i], bounds[3, i], band, state)
        state = lax.fori_loop(0, bounds[0, i], full, state)
        state = lax.fori_loop(bounds[0, i] * (TK // TM), bounds[1, i], edge, state)
        for h in range(group):
            dq_acc[h * HD : (h + 1) * HD, at] = state[h]
        return 0

    lax.fori_loop(0, total // TQ, one_tile, 0)

    half = HD // 2
    cos_t, sin_t = cos_ref[...], sin_ref[...]
    noisy = lift == 0

    def back_turn(w, out, base):
        first, second = w[:half, :], w[half:, :]
        out[base : base + half, :] = (first * cos_t + second * sin_t).astype(BF)
        out[base + half : base + HD, :] = (second * cos_t - first * sin_t).astype(BF)

    for h in range(group):
        back_turn(dq_acc[h * HD : (h + 1) * HD, :] * HD**-0.5, own_out, 3 * h * HD)
        band_k = jnp.where(noisy, dk_acc[h], dkc_acc[h])
        band_v = jnp.where(noisy, dv_acc[h], dvc_acc[h])
        back_turn(jnp.transpose(band_k) * HD**-0.5, own_out, (3 * h + 1) * HD)
        own_out[(3 * h + 2) * HD : (3 * h + 3) * HD, :] = jnp.transpose(band_v).astype(BF)
        part_k = jnp.where(noisy, dkc_acc[h], 0.0)
        part_v = jnp.where(noisy, dvc_acc[h], 0.0)
        back_turn(jnp.transpose(part_k) * HD**-0.5, cln_out, 2 * h * HD)
        cln_out[(2 * h + 1) * HD : (2 * h + 2) * HD, :] = jnp.transpose(part_v).astype(BF)


def attend_back(bounds, q, k, v, kc, vc, o, lse, do_mine, do_other, id_row, id_col, cos_t, sin_t,
                heads, group):
    total = q.shape[1]
    head = pl.BlockSpec((group * HD, total), lambda g, b: (g, 0))
    halfhead = pl.BlockSpec((group * HD, total // 2), lambda g, b: (g, 0))
    whole = lambda shape: pl.BlockSpec(shape, lambda g, b: (0, 0))
    rows16 = pltpu.VMEM((group, total, HD), BF)
    rows32 = pltpu.VMEM((group, total, HD), F32)
    return pl.pallas_call(
        functools.partial(attend_back_kernel, group),
        grid_spec=pltpu.PrefetchScalarGridSpec(
            num_scalar_prefetch=1,
            grid=(heads // group,),
            in_specs=[head] * 6
            + [pl.BlockSpec((group, 8, total), lambda g, b: (g, 0, 0)), halfhead, halfhead]
            + [whole(id_row.shape), whole(id_col.shape), whole(cos_t.shape), whole(sin_t.shape)],
            out_specs=[
                pl.BlockSpec((group * 3 * HD, total), lambda g, b: (g, 0)),
                pl.BlockSpec((group * 2 * HD, total), lambda g, b: (g, 0)),
            ],
            scratch_shapes=[rows16] * 6
            + [pltpu.VMEM((group * HD, total), BF)]
            + [rows32] * 4
            + [pltpu.VMEM((group * HD, total), F32)],
        ),
        out_shape=[
            jax.ShapeDtypeStruct((heads * 3 * HD, total), BF),
            jax.ShapeDtypeStruct((heads * 2 * HD, total), BF),
        ],
        name="attend_back",
    )(bounds, q, k, v, kc, vc, o, lse, do_mine, do_other, id_row, id_col, cos_t, sin_t)


def finish_kernel(n, g, s, up, dn, ou, g_out, s_out, up_out, dn_out, ou_out, g_in, s_in, g_x,
                  s_x, up_x, dn_x, ou_x, g_t, s_t, s_c, up_t, dn_t, ou_t, send, recv, s_send,
                  s_recv, x_send, x_recv, c_send, c_recv, local):
    me = lax.axis_index("fsdp")
    seat = lax.axis_index("seq")
    core = lax.rem(seat, 2)
    across = {"seq": lax.rem(seat + 2, 4)}
    beside = {"seq": seat + 1 - 2 * core}
    mesh_id = pl.DeviceIdType.MESH
    barrier = pltpu.get_barrier_semaphore()
    peers = [{"fsdp": lax.rem(me + d, n)} for d in range(1, n)]
    for where in peers + [across, beside]:
        pl.semaphore_signal(barrier, inc=1, device_id=where, device_id_type=mesh_id)
    pl.semaphore_wait(barrier, n + 1)

    def push(src, dst, one, two, where):
        copy = pltpu.make_async_remote_copy(
            src_ref=src, dst_ref=dst, send_sem=one, recv_sem=two, device_id=where,
            device_id_type=mesh_id,
        )
        copy.start()
        return copy

    def settle(tmp, out, sem):
        copy = pltpu.make_async_copy(tmp, out, sem)
        copy.start()
        copy.wait()

    first = []
    for d in range(1, n):
        to = lax.rem(me + d, n)
        first.append(push(g.at[to], g_in.at[d - 1], send.at[d - 1], recv.at[d - 1], peers[d - 1]))
        first.append(
            push(s.at[to], s_in.at[d - 1], s_send.at[d - 1], s_recv.at[d - 1], peers[d - 1])
        )
    shards = [(up, up_x, up_t, up_out), (dn, dn_x, dn_t, dn_out), (ou, ou_x, ou_t, ou_out)]
    over = [
        push(src, land, x_send.at[i], x_recv.at[i], across)
        for i, (src, land, _, _) in enumerate(shards)
    ]
    near = []
    for i, (src, land, tmp, out) in enumerate(shards):
        over[i].wait()
        tmp[...] = (src[...].astype(F32) + land[...].astype(F32)).astype(BF)
        settle(tmp, out.at[core], local.at[i])
        near.append(push(out.at[core], out.at[core], c_send.at[i], c_recv.at[i], beside))
    for copy in first:
        copy.wait()

    rows = g.shape[1]
    block = 16 if rows % 16 == 0 else rows

    def add_rows(i, _):
        at = pl.ds(pl.multiple_of(i * block, block), block)
        total = g[me, at, :].astype(F32)
        for d in range(n - 1):
            total = total + g_in[d, at, :].astype(F32)
        g_t[at, :] = total.astype(BF)
        return 0

    lax.fori_loop(0, rows // block, add_rows, 0)
    total = s[me]
    for d in range(n - 1):
        total = total + s_in[d]
    s_t[0] = total
    settle(g_t, g_x.at[0], local.at[3])
    settle(s_t.at[0], s_x.at[0], local.at[4])
    far_g = push(g_x.at[0], g_x.at[1], x_send.at[3], x_recv.at[3], across)
    far_s = push(s_x.at[0], s_x.at[1], x_send.at[4], x_recv.at[4], across)
    far_s.wait()
    s_t[1] = s_x[0] + s_x[1]
    settle(s_t.at[1], s_c.at[0], local.at[5])
    near_s = push(s_c.at[0], s_c.at[1], c_send.at[4], c_recv.at[4], beside)
    far_g.wait()
    g_t[...] = (g_x[0].astype(F32) + g_x[1].astype(F32)).astype(BF)
    settle(g_t, g_out.at[core], local.at[6])
    near.append(push(g_out.at[core], g_out.at[core], c_send.at[3], c_recv.at[3], beside))
    near_s.wait()
    s_out[...] = s_c[0] + s_c[1]
    for copy in near:
        copy.wait()


def finish(g, s, up, dn, ou):
    n = g.shape[0]
    vm = pl.BlockSpec(memory_space=pltpu.VMEM)
    pair = lambda a: jax.ShapeDtypeStruct((2,) + a.shape, BF)
    one = lambda a: pltpu.VMEM(a.shape, a.dtype)
    dma = pltpu.SemaphoreType.DMA
    return pl.pallas_call(
        functools.partial(finish_kernel, n),
        in_specs=[vm] * 5,
        out_specs=[vm] * 5,
        out_shape=[
            jax.ShapeDtypeStruct((2,) + g.shape[1:], BF),
            jax.ShapeDtypeStruct(s.shape[1:], F32),
            pair(up),
            pair(dn),
            pair(ou),
        ],
        scratch_shapes=[
            pltpu.VMEM((n - 1,) + g.shape[1:], BF),
            pltpu.VMEM((n - 1,) + s.shape[1:], F32),
            pltpu.VMEM((2,) + g.shape[1:], BF),
            pltpu.VMEM((2,) + s.shape[1:], F32),
            one(up),
            one(dn),
            one(ou),
            pltpu.VMEM(g.shape[1:], BF),
            pltpu.VMEM((2,) + s.shape[1:], F32),
            pltpu.VMEM((2,) + s.shape[1:], F32),
            one(up),
            one(dn),
            one(ou),
            dma((n - 1,)),
            dma((n - 1,)),
            dma((n - 1,)),
            dma((n - 1,)),
            dma((5,)),
            dma((5,)),
            dma((5,)),
            dma((5,)),
            dma((7,)),
        ],
        compiler_params=pltpu.CompilerParams(collective_id=1, has_side_effects=True),
        name="finish",
    )(g, s, up, dn, ou)


def on_device(
    tokens,
    block_ids,
    ln1_scale,
    ln1_bias,
    qkv_weight,
    qkv_bias,
    out_weight,
    out_bias,
    ln2_scale,
    ln2_bias,
    up_weight,
    up_bias,
    down_weight,
    down_bias,
    cotangent,
):
    tok = tokens[0]
    local_rows, width = tok.shape
    ids = block_ids[0].astype(jnp.int32)
    length = ids.shape[0]
    shard = ln1_scale.shape[0]
    heads = H // 2
    span = heads * HD
    me = lax.axis_index("seq")
    core = me % 2
    noisy = me < 2
    swap = [(0, 1), (1, 0), (2, 3), (3, 2)]
    other = lax.ppermute(tok, "seq", swap)
    clean_in = lax.ppermute(tok, "seq", [(2, 0), (3, 1)])
    clean_mine = jnp.where(noisy, clean_in, tok)
    clean_other = lax.ppermute(clean_mine, "seq", swap)

    q_cols = lax.dynamic_slice_in_dim(qkv_weight, core * 3 * span, 3 * span, 1)
    small = jnp.concatenate(
        [
            ln1_scale.reshape(1, shard),
            ln1_bias.reshape(1, shard),
            out_bias.reshape(1, shard),
            ln2_scale.reshape(1, shard),
            ln2_bias.reshape(1, shard),
            down_bias.reshape(1, shard),
            qkv_bias.reshape(-1, shard),
            up_bias.reshape(-1, shard),
        ],
        0,
    )
    n_small = small.shape[0]
    small = jnp.pad(small, ((0, 128 - n_small), (0, 0))).T
    gathered = lax.all_gather(
        jnp.concatenate([q_cols, small], 1), "fsdp", axis=0, tiled=True
    )
    n_fsdp = width // shard
    vectors = gathered[:, 3 * span :].reshape(n_fsdp, shard, 128)[:, :, :n_small]
    vectors = jnp.transpose(vectors, (2, 0, 1)).astype(F32)
    flat = vectors[:6].reshape(6, width)
    qkv_b = jnp.transpose(vectors[6:9], (1, 0, 2)).reshape(-1)
    scale_one, shift_one, out_shift, scale_two, shift_two, down_shift = [flat[i] for i in range(6)]

    inner = up_bias.shape[0] // 2
    up_b = jnp.transpose(vectors[9:], (1, 0, 2)).reshape(n_fsdp, 2, inner)
    up_b = lax.dynamic_index_in_dim(up_b, core, 1, False).reshape(-1)
    up_cols = lax.dynamic_index_in_dim(
        up_weight.reshape(shard, n_fsdp, 2, inner), core, 2, False
    ).reshape(shard, n_fsdp * inner)
    down_rows = lax.dynamic_slice_in_dim(down_weight, core * inner, inner, 0)
    out_cols = lax.dynamic_slice_in_dim(out_weight, core * span, span, 1)
    out_near = lax.all_gather(out_cols, "fsdp", axis=0, tiled=True)
    up_own = lax.all_gather(up_cols, "fsdp", axis=0, tiled=True)
    down_own = lax.all_gather(down_rows, "fsdp", axis=0, tiled=True)
    out_far = lax.ppermute(out_near, "seq", swap)
    in_order = lambda near, far, axis: jnp.where(
        core == 0, jnp.concatenate([near, far], axis), jnp.concatenate([far, near], axis)
    )
    out_full = in_order(out_near, out_far, 1)
    cot_both = jnp.concatenate([cotangent[0], lax.ppermute(cotangent[0], "seq", swap)], 0)

    frequency = jnp.exp(-jnp.log(10000.0) * jnp.arange(HD // 2, dtype=F32) / (HD // 2))
    angles = frequency[:, None] * jnp.arange(length, dtype=F32)[None, :]
    cos_t, sin_t = jnp.cos(angles), jnp.sin(angles)

    first = ids[::TQ][:, None]
    last = ids[TQ - 1 :: TQ][:, None]
    before = lambda edge: jnp.sum((ids[None, :] < edge).astype(jnp.int32), 1)
    start_first, end_first = before(first), before(first + 1)
    start_last, end_last = before(last), before(last + 1)
    ceil_m = lambda value: (value + TM - 1) // TM
    lift = jnp.where(noisy, 0, 1)
    zero = jnp.zeros_like(start_first)
    bounds = jnp.stack(
        [
            jnp.where(noisy, start_first, end_first) // TK,
            ceil_m(jnp.where(noisy, start_last, end_last)),
            jnp.where(noisy, start_first // TM, zero),
            jnp.where(noisy, ceil_m(end_last), zero),
            zero + jnp.where(jnp.arange(zero.shape[0]) == 0, lift, core),
        ]
    ).astype(jnp.int32)
    id_row = jnp.broadcast_to(ids[None, :], (8, length))
    id_col = jnp.broadcast_to(ids[:, None], (length, 128))

    vec = jnp.concatenate([scale_one[None], shift_one[None], jnp.zeros((6, width), F32)], 0)
    bias_own = lax.dynamic_slice_in_dim(qkv_b, core * 3 * span, 3 * span, 0)
    bias_own = jnp.transpose(bias_own.reshape(heads, 3, HD), (1, 0, 2)).reshape(3 * span, 1)
    q, k, v, kc, vc, a_own, a_clean = project(
        core.reshape(1).astype(jnp.int32), tok, other, clean_mine, clean_other, gathered, vec,
        bias_own, cos_t, sin_t, heads
    )
    o, lse = attend(bounds, q, k, v, kc, vc, id_row, id_col, heads, 2)
    cut = lambda value, which: lax.dynamic_slice_in_dim(value, which * local_rows, local_rows, 1)
    o_mine = cut(o, core)
    o_in = lax.ppermute(cut(o, 1 - core), "seq", swap)
    attended = in_order(o_mine, o_in, 0)

    rows_in = tok.astype(F32)
    hidden = rows_in + rows_contract(attended, out_full) + out_shift
    normed_two, inverse_two = normalize_parts(hidden)
    second_in = (normed_two * scale_two + shift_two).astype(BF)
    both_in = jnp.concatenate([second_in, lax.ppermute(second_in, "seq", swap)], 0)

    def join(partial):
        return partial[:local_rows] + lax.ppermute(
            partial[local_rows:].astype(BF), "seq", swap
        ).astype(F32)

    pre_act = dot(both_in, up_own) + up_b
    activated, gelu_pull = jax.vjp(
        lambda pre_value: jax.nn.gelu(pre_value, approximate=True), pre_act
    )
    act_low = activated.astype(BF)
    result = hidden + join(dot(act_low, down_own)) + down_shift

    grad_top = cotangent[0].astype(F32)
    grad_down_b = jnp.sum(grad_top, 0)
    grad_pre = gelu_pull(right_transposed(cot_both, down_own))[0].astype(BF)
    grad_second = join(right_transposed(grad_pre, up_own))
    grad_up_b = jnp.sum(grad_pre.astype(F32), 0)
    grad_down_w = rows_contract(act_low, cot_both).astype(BF)
    grad_up_w = rows_contract(both_in, grad_pre).astype(BF)
    grad_scale_two = jnp.sum(grad_second * normed_two, 0)
    grad_shift_two = jnp.sum(grad_second, 0)
    grad_hidden = grad_top + norm_backward(grad_second, normed_two, inverse_two, scale_two)

    grad_attn = grad_hidden.astype(BF)
    grad_out_w = dot(attended, grad_attn).astype(BF)
    grad_out_b = jnp.sum(grad_attn.astype(F32), 0)
    grad_o = right_transposed(out_full, grad_attn).astype(BF)
    cut_heads = lambda which: lax.dynamic_slice_in_dim(grad_o, which * span, span, 0)
    do_mine = cut_heads(core)
    do_in = lax.ppermute(cut_heads(1 - core), "seq", swap)
    cut_cols = lambda which: lax.dynamic_slice_in_dim(grad_out_w, which * span, span, 1)
    out_sum = (
        cut_cols(core).astype(F32) + lax.ppermute(cut_cols(1 - core), "seq", swap).astype(F32)
    ).astype(BF)
    do_mine, do_in, grad_down_w, grad_up_w, out_sum = lax.optimization_barrier(
        (do_mine, do_in, grad_down_w, grad_up_w, out_sum)
    )
    scatter = lambda grad: lax.psum_scatter(grad, "fsdp", scatter_dimension=0, tiled=True)
    down_part = scatter(grad_down_w)
    up_out_part = scatter(jnp.concatenate([grad_up_w, out_sum], 1))
    up_part, out_part = up_out_part[:, : n_fsdp * inner], up_out_part[:, n_fsdp * inner :]

    own_grad, clean_grad = attend_back(
        bounds, q, k, v, kc, vc, o, lse, do_mine, do_in, id_row, id_col, cos_t, sin_t, heads, 2
    )
    weight = gathered[:, : 3 * span]
    weight_kv = weight.reshape(width, heads, 3 * HD)[:, :, HD:].reshape(width, 2 * span)
    back = lambda grad, w: lax.dot_general(
        grad, w, (((0,), (1,)), ((), ())), preferred_element_type=F32
    )
    first_clean = back(clean_grad, weight_kv)
    first_own = back(own_grad, weight)
    cut_rows = lambda value, which: lax.dynamic_slice_in_dim(
        value, which * local_rows, local_rows, 0
    )
    send_rows = jnp.concatenate(
        [cut_rows(first_clean, 1 - core), cut_rows(first_own, 1 - core)], 0
    ).astype(BF)
    got_rows = lax.ppermute(send_rows, "seq", swap).astype(F32)
    clean_sum = (cut_rows(first_clean, core) + got_rows[:local_rows]).astype(BF)
    from_noisy = lax.ppermute(clean_sum, "seq", [(0, 2), (1, 3)])
    grad_first = cut_rows(first_own, core) + got_rows[local_rows:]

    by_rows = lambda a, grad: lax.dot_general(
        a, grad, (((0,), (1,)), ((), ())), preferred_element_type=F32
    )
    grad_qkv_w = by_rows(a_own, own_grad).reshape(width, heads, 3 * HD)
    grad_kv = by_rows(a_clean, clean_grad).reshape(width, heads, 2 * HD)
    grad_qkv_w = grad_qkv_w.at[:, :, HD:].add(grad_kv).astype(BF)
    grad_qkv_w = grad_qkv_w.reshape(n_fsdp, shard, 3 * span)
    grad_qkv_b = jnp.sum(own_grad.astype(F32), 1).reshape(heads, 3 * HD)
    kv_b = jnp.sum(clean_grad.astype(F32), 1).reshape(heads, 2 * HD)
    grad_qkv_b = grad_qkv_b.at[:, HD:].add(kv_b).reshape(3 * span)

    normed_one, inverse_one = normalize_parts(rows_in)
    normed_clean, _ = normalize_parts(clean_mine.astype(F32))
    clean_wide = clean_sum.astype(F32)
    grad_scale_one = jnp.sum(grad_first * normed_one + clean_wide * normed_clean, 0)
    grad_shift_one = jnp.sum(grad_first + clean_wide, 0)
    grad_first = grad_first + from_noisy.astype(F32)
    grad_rows = grad_hidden + norm_backward(grad_first, normed_one, inverse_one, scale_one)

    qkv_b_wide = lax.dynamic_update_slice_in_dim(
        jnp.zeros((2 * 3 * span,), F32), grad_qkv_b, core * 3 * span, 0
    )
    up_b_wide = lax.dynamic_update_slice_in_dim(
        jnp.zeros((n_fsdp, 2, inner), F32), grad_up_b.reshape(n_fsdp, 1, inner), core, 1
    )
    pieces = [
        piece.reshape(n_fsdp, -1)
        for piece in (
            grad_scale_one, grad_shift_one, qkv_b_wide, grad_out_b, grad_scale_two,
            grad_shift_two, up_b_wide, grad_down_b,
        )
    ]
    sizes = [piece.shape[1] for piece in pieces]
    packed = jnp.concatenate(pieces, 1)
    lines = -(-packed.shape[1] // 128)
    packed = jnp.pad(packed, ((0, 0), (0, lines * 128 - packed.shape[1])))
    packed = packed.reshape(n_fsdp, lines, 128)
    qkv_g, small_sum, up_g, down_g, out_g = finish(
        grad_qkv_w, packed, up_part, down_part, out_part
    )
    small_sum = small_sum.reshape(-1)
    small_out, at = [], 0
    for size in sizes:
        small_out.append(small_sum[at : at + size])
        at += size
    side = lambda pair: jnp.concatenate([pair[0], pair[1]], 1).astype(F32)
    up_g = jnp.transpose(up_g.reshape(2, shard, n_fsdp, inner), (1, 2, 0, 3))
    return (
        result.astype(BF)[None],
        grad_rows[None],
        small_out[0],
        small_out[1],
        side(qkv_g),
        small_out[2],
        side(out_g),
        small_out[3],
        small_out[4],
        small_out[5],
        up_g.reshape(shard, -1).astype(F32),
        small_out[6],
        down_g.reshape(2 * inner, width).astype(F32),
        small_out[7],
    )


def solution(mesh):
    row, mat, vec = P("fsdp", "seq", None), P("fsdp", None), P("fsdp")
    in_specs = (row, mat, vec, vec, mat, vec, mat, vec, vec, vec, mat, vec, mat, vec, row)
    out_specs = (row, row, vec, vec, mat, vec, mat, vec, vec, vec, mat, vec, mat, vec)
    return jax.shard_map(
        on_device, mesh=mesh, in_specs=in_specs, out_specs=out_specs, check_vma=False
    )
```

```python
import functools
import math

import jax
import jax.numpy as jnp
from jax import lax
from jax.experimental import pallas as pl
from jax.experimental.pallas import tpu as pltpu
from jax.sharding import PartitionSpec as P

H = 12
HD = 64
EPSILON = 1e-05
LOG2E = 1.4426950408889634
NEG = -1e30
TQ = 512
TK = 256
TM = 256
BF = jnp.bfloat16
F32 = jnp.float32


def normalize_parts(values):
    mean_value = jnp.mean(values, -1, keepdims=True)
    centred = values - mean_value
    variance = jnp.mean(centred * centred, -1, keepdims=True)
    inverse = lax.rsqrt(variance + EPSILON)
    return (centred * inverse, inverse)


def norm_backward(grad_out, normed, inverse, scale):
    grad_norm = grad_out * scale
    return inverse * (
        grad_norm
        - jnp.mean(grad_norm, -1, keepdims=True)
        - normed * jnp.mean(grad_norm * normed, -1, keepdims=True)
    )


def rows_contract(left, right):
    return lax.dot_general(left, right, (((0,), (0,)), ((), ())), preferred_element_type=F32)


def right_transposed(left, right):
    return lax.dot_general(left, right, (((1,), (1,)), ((), ())), preferred_element_type=F32)


def dot(left, right):
    return jnp.dot(left, right, preferred_element_type=F32)


def qkv_kernel(heads, core_ref, mine, other, cmine, cother, w_ref, vec_ref, bias_ref, cos_ref,
               sin_ref, q_out, k_out, v_out, kc_out, vc_out, a_out, wt):
    step = pl.program_id(0)
    span = heads * HD

    @pl.when(step == 0)
    def _():
        whole = jnp.transpose(w_ref[...])
        for h in range(heads):
            for part in range(3):
                wt[part * span + h * HD : part * span + (h + 1) * HD, :] = whole[
                    (3 * h + part) * HD : (3 * h + part + 1) * HD, :
                ]

    def normed(rows):
        values = rows.astype(F32)
        n, _ = normalize_parts(values)
        return (n * vec_ref[0:1, :] + vec_ref[1:2, :]).astype(BF)

    def turn(lin, base, out):
        cos_t, sin_t = cos_ref[...], sin_ref[...]
        half = HD // 2
        for h in range(heads):
            first = lin[base + h * HD : base + h * HD + half, :]
            second = lin[base + h * HD + half : base + (h + 1) * HD, :]
            out[h * HD : h * HD + half, :] = (first * cos_t - second * sin_t).astype(BF)
            out[h * HD + half : (h + 1) * HD, :] = (first * sin_t + second * cos_t).astype(BF)

    quarter = pl.num_programs(0) // 4

    @pl.when(step < 2 * quarter)
    def _():
        a = normed(jnp.where(step < quarter, mine[...], other[...]))
        a_out[...] = a
        lin = right_transposed(wt[...], a) + bias_ref[...]
        turn(lin, 0, q_out)
        turn(lin, span, k_out)
        v_out[...] = lin[2 * span :, :].astype(BF)

    @pl.when(step >= 2 * quarter)
    def _():
        a = normed(jnp.where(step < 3 * quarter, cmine[...], cother[...]))
        lin = right_transposed(wt[span:, :], a) + bias_ref[span:, :]
        turn(lin, 0, kc_out)
        vc_out[...] = lin[span:, :].astype(BF)


def project(core, mine, other, cmine, cother, weight, vec, bias, cos_t, sin_t, heads):
    local, width = mine.shape
    span = heads * HD
    tile = 256
    n = local // tile

    def place(t, c):
        mine_first = jnp.where(t % (2 * n) < n, c[0], 1 - c[0])
        return mine_first * n + t % n

    def src(k):
        return pl.BlockSpec((tile, width), lambda t, c: (jnp.clip(t - k * n, 0, n - 1), 0))

    whole = lambda shape: pl.BlockSpec(shape, lambda t, c: (0, 0))
    own = pl.BlockSpec((span, tile), lambda t, c: (0, place(jnp.minimum(t, 2 * n - 1), c)))
    cln = pl.BlockSpec((span, tile), lambda t, c: (0, place(jnp.maximum(t, 2 * n), c)))
    own_a = pl.BlockSpec((tile, width), lambda t, c: (jnp.minimum(t, 2 * n - 1), 0))
    tab = pl.BlockSpec((HD // 2, tile), lambda t, c: (0, place(t, c)))
    head_shape = jax.ShapeDtypeStruct((span, 2 * local), BF)
    row_shape = jax.ShapeDtypeStruct((2 * local, width), BF)
    return pl.pallas_call(
        functools.partial(qkv_kernel, heads),
        grid_spec=pltpu.PrefetchScalarGridSpec(
            num_scalar_prefetch=1,
            grid=(4 * n,),
            in_specs=[src(0), src(1), src(2), src(3), whole((width, 3 * span)), whole(vec.shape),
                      whole(bias.shape), tab, tab],
            out_specs=[own, own, own, cln, cln, own_a],
            scratch_shapes=[pltpu.VMEM((3 * span, width), BF)],
        ),
        out_shape=[head_shape] * 5 + [row_shape],
        name="project",
    )(core, mine, other, cmine, cother, weight, vec, bias, cos_t, sin_t)


def attend_kernel(group, bounds, q, k, v, kc, vc, id_row, id_col, o_out, lse_out, ks, kcs, vs,
                  vcs):
    total = q.shape[1]
    scale = LOG2E * HD**-0.5
    ones = jnp.ones((16, total), BF)
    for h in range(group):
        rows = slice(h * HD, (h + 1) * HD)
        ks[h] = jnp.transpose(k[rows, :])
        kcs[h] = jnp.transpose(kc[rows, :])
        vs[h, :HD] = v[rows, :]
        vcs[h, :HD] = vc[rows, :]
        vs[h, HD:] = ones
        vcs[h, HD:] = ones
    lift = bounds[4, 0]

    lead = jnp.ones((8, HD), BF)
    top = lambda ref, rows: jnp.max(dot(lead, ref[rows, :] * ref[rows, :]))
    limit = jnp.float32(0.9 * (96.0 / scale) ** 2)
    small = None
    for h in range(group):
        rows = slice(h * HD, (h + 1) * HD)
        fits = top(q, rows) * jnp.maximum(top(k, rows), top(kc, rows)) < limit
        small = fits if small is None else jnp.logical_and(small, fits)

    def key_ids(keys):
        col = id_col[keys, :]
        return jnp.concatenate([col] * (TQ // 128), 1)

    def sweep(i, q_ids, update, state):
        def band(j, state):
            keys = pl.ds(pl.multiple_of(j * TM, TM), TM)
            return update(state, ks, vs, keys, key_ids(keys) == q_ids)

        def full(j, state):
            keys = pl.ds(pl.multiple_of(j * TK, TK), TK)
            return update(state, kcs, vcs, keys, None)

        def edge(j, state):
            keys = pl.ds(pl.multiple_of(j * TM, TM), TM)
            return update(state, kcs, vcs, keys, key_ids(keys) < q_ids + lift)

        state = lax.fori_loop(bounds[2, i], bounds[3, i], band, state)
        state = lax.fori_loop(0, bounds[0, i], full, state)
        return lax.fori_loop(bounds[0, i] * (TK // TM), bounds[1, i], edge, state)

    def store(h, at, acc, log_shift):
        total_w = acc[HD : HD + 1, :]
        o_out[h * HD : (h + 1) * HD, at] = (acc[:HD, :] / total_w).astype(BF)
        lse_out[h, :, at] = jnp.broadcast_to(log_shift + jnp.log2(total_w), (8, TQ))

    def plain_tile(i, _):
        at = pl.ds(pl.multiple_of(i * TQ, TQ), TQ)
        queries = [q[h * HD : (h + 1) * HD, at] for h in range(group)]

        def update(state, key_ref, val_ref, keys, mask):
            out = []
            for h in range(group):
                p = jnp.exp2(dot(key_ref[h, keys, :], queries[h]) * scale)
                if mask is not None:
                    p = jnp.where(mask, p, 0.0)
                out.append(state[h] + dot(val_ref[h, :, keys], p.astype(BF)))
            return tuple(out)

        state = (jnp.zeros((HD + 16, TQ), F32),) * group
        state = sweep(i, id_row[0:1, at], update, state)
        for h in range(group):
            store(h, at, state[h], 0.0)
        return 0

    def shifted_tile(i, _):
        at = pl.ds(pl.multiple_of(i * TQ, TQ), TQ)
        q_ids = id_row[0:1, at]
        for h in range(group):
            query = q[h * HD : (h + 1) * HD, at]

            def update(state, key_ref, val_ref, keys, mask):
                m, acc = state
                s = dot(key_ref[h, keys, :], query)
                if mask is not None:
                    s = jnp.where(mask, s, NEG)
                m_new = jnp.maximum(m, jnp.max(s, 0, keepdims=True))
                p = jnp.exp2((s - m_new) * scale).astype(BF)
                alpha = jnp.exp2((m - m_new) * scale)
                return m_new, acc * alpha + dot(val_ref[h, :, keys], p)

            state = (jnp.full((1, TQ), NEG, F32), jnp.zeros((HD + 16, TQ), F32))
            m, acc = sweep(i, q_ids, update, state)
            store(h, at, acc, m * scale)
        return 0

    @pl.when(small)
    def _():
        lax.fori_loop(0, total // TQ, plain_tile, 0)

    @pl.when(jnp.logical_not(small))
    def _():
        lax.fori_loop(0, total // TQ, shifted_tile, 0)


def attend(bounds, q, k, v, kc, vc, id_row, id_col, heads, group):
    total = q.shape[1]
    head = pl.BlockSpec((group * HD, total), lambda g, b: (g, 0))
    whole = lambda shape: pl.BlockSpec(shape, lambda g, b: (0, 0))
    return pl.pallas_call(
        functools.partial(attend_kernel, group),
        grid_spec=pltpu.PrefetchScalarGridSpec(
            num_scalar_prefetch=1,
            grid=(heads // group,),
            in_specs=[head] * 5 + [whole(id_row.shape), whole(id_col.shape)],
            out_specs=[head, pl.BlockSpec((group, 8, total), lambda g, b: (g, 0, 0))],
            scratch_shapes=[pltpu.VMEM((group, total, HD), BF)] * 2
            + [pltpu.VMEM((group, HD + 16, total), BF)] * 2,
        ),
        out_shape=[
            jax.ShapeDtypeStruct((heads * HD, total), BF),
            jax.ShapeDtypeStruct((heads, 8, total), F32),
        ],
        cost_estimate=pl.CostEstimate(
            flops=16 * heads * HD * total * total, bytes_accessed=2**24, transcendentals=0
        ),
        name="attend",
    )(bounds, q, k, v, kc, vc, id_row, id_col)


def attend_back_kernel(group, bounds, q, k, v, kc, vc, o, lse, do_mine, do_other, id_row, id_col,
                       cos_ref, sin_ref, own_out, cln_out, ks, vs, kcs, vcs, qs, dos, dot_s,
                       dk_acc, dv_acc, dkc_acc, dvc_acc, dq_acc):
    total = q.shape[1]
    half_rows = total // 2
    scale = LOG2E * HD**-0.5
    lift = bounds[4, 0]
    core = bounds[4, 1]
    near = pl.ds(pl.multiple_of(core * half_rows, 128), half_rows)
    far = pl.ds(pl.multiple_of((1 - core) * half_rows, 128), half_rows)
    dot_s[:, near] = do_mine[...]
    dot_s[:, far] = do_other[...]
    for h in range(group):
        rows = slice(h * HD, (h + 1) * HD)
        ks[h] = jnp.transpose(k[rows, :])
        vs[h] = jnp.transpose(v[rows, :])
        kcs[h] = jnp.transpose(kc[rows, :])
        vcs[h] = jnp.transpose(vc[rows, :])
        qs[h] = jnp.transpose(q[rows, :])
        dos[h] = jnp.transpose(dot_s[rows, :])
    for ref in (dk_acc, dv_acc, dkc_acc, dvc_acc):
        ref[...] = jnp.zeros_like(ref)

    def one_tile(i, _):
        at = pl.ds(pl.multiple_of(i * TQ, TQ), TQ)
        q_ids = id_row[0:1, at]
        queries, grads, deltas, sums, q_rows, g_rows = [], [], [], [], [], []
        for h in range(group):
            rows = slice(h * HD, (h + 1) * HD)
            queries.append(q[rows, at])
            g = dot_s[rows, at]
            grads.append(g)
            deltas.append(jnp.sum(g.astype(F32) * o[rows, at].astype(F32), 0, keepdims=True))
            sums.append(lse[h, 0:1, at])
            q_rows.append(qs[h, at, :])
            g_rows.append(dos[h, at, :])

        def update(state, key_ref, val_ref, key_cols, dk, dv, keys, mask):
            out = []
            for h in range(group):
                s = dot(key_ref[h, keys, :], queries[h])
                p = jnp.exp2(s * scale - sums[h])
                if mask is not None:
                    p = jnp.where(mask, p, 0.0)
                dp = dot(val_ref[h, keys, :], grads[h])
                ds = (p * (dp - deltas[h])).astype(BF)
                dv[h, keys, :] += dot(p.astype(BF), g_rows[h])
                dk[h, keys, :] += dot(ds, q_rows[h])
                out.append(state[h] + dot(key_cols[h * HD : (h + 1) * HD, keys], ds))
            return tuple(out)

        def key_ids(keys):
            col = id_col[keys, :]
            return jnp.concatenate([col] * (TQ // 128), 1)

        def band(j, state):
            keys = pl.ds(pl.multiple_of(j * TM, TM), TM)
            return update(state, ks, vs, k, dk_acc, dv_acc, keys, key_ids(keys) == q_ids)

        def full(j, state):
            keys = pl.ds(pl.multiple_of(j * TK, TK), TK)
            return update(state, kcs, vcs, kc, dkc_acc, dvc_acc, keys, None)

        def edge(j, state):
            keys = pl.ds(pl.multiple_of(j * TM, TM), TM)
            mask = key_ids(keys) < q_ids + lift
            return update(state, kcs, vcs, kc, dkc_acc, dvc_acc, keys, mask)

        state = (jnp.zeros((HD, TQ), F32),) * group
        state = lax.fori_loop(bounds[2, i], bounds[3, i], band, state)
        state = lax.fori_loop(0, bounds[0, i], full, state)
        state = lax.fori_loop(bounds[0, i] * (TK // TM), bounds[1, i], edge, state)
        for h in range(group):
            dq_acc[h * HD : (h + 1) * HD, at] = state[h]
        return 0

    lax.fori_loop(0, total // TQ, one_tile, 0)

    half = HD // 2
    cos_t, sin_t = cos_ref[...], sin_ref[...]
    noisy = lift == 0

    def spread(out, value, base):
        rows = slice(base, base + value.shape[0])
        out[rows, near] = value[:, :half_rows].astype(BF)
        out[rows, far] = value[:, half_rows:].astype(BF)

    def back_turn(out, w, base):
        first, second = w[:half, :], w[half:, :]
        spread(out, first * cos_t + second * sin_t, base)
        spread(out, second * cos_t - first * sin_t, base + half)

    for h in range(group):
        back_turn(own_out, dq_acc[h * HD : (h + 1) * HD, :] * HD**-0.5, 3 * h * HD)
        band_k = jnp.where(noisy, dk_acc[h], dkc_acc[h])
        band_v = jnp.where(noisy, dv_acc[h], dvc_acc[h])
        back_turn(own_out, jnp.transpose(band_k) * HD**-0.5, (3 * h + 1) * HD)
        spread(own_out, jnp.transpose(band_v), (3 * h + 2) * HD)
        back_turn(cln_out, jnp.transpose(dkc_acc[h]) * HD**-0.5, 2 * h * HD)
        spread(cln_out, jnp.transpose(dvc_acc[h]), (2 * h + 1) * HD)


def attend_back(bounds, q, k, v, kc, vc, o, lse, do_mine, do_other, id_row, id_col, cos_t, sin_t,
                pair, group):
    total = q.shape[1]
    head = pl.BlockSpec((group * HD, total), lambda g, b: (pair, 0))
    halfhead = pl.BlockSpec((group * HD, total // 2), lambda g, b: (pair, 0))
    whole = lambda shape: pl.BlockSpec(shape, lambda g, b: (0, 0))
    rows16 = pltpu.VMEM((group, total, HD), BF)
    rows32 = pltpu.VMEM((group, total, HD), F32)
    outs = [(group * 3 * HD, total), (group * 2 * HD, total)]
    return pl.pallas_call(
        functools.partial(attend_back_kernel, group),
        grid_spec=pltpu.PrefetchScalarGridSpec(
            num_scalar_prefetch=1,
            grid=(1,),
            in_specs=[head] * 6
            + [pl.BlockSpec((group, 8, total), lambda g, b: (pair, 0, 0)), halfhead, halfhead]
            + [whole(id_row.shape), whole(id_col.shape), whole(cos_t.shape), whole(sin_t.shape)],
            out_specs=[whole(shape) for shape in outs],
            scratch_shapes=[rows16] * 6
            + [pltpu.VMEM((group * HD, total), BF)]
            + [rows32] * 4
            + [pltpu.VMEM((group * HD, total), F32)],
        ),
        out_shape=[jax.ShapeDtypeStruct(shape, BF) for shape in outs],
        cost_estimate=pl.CostEstimate(
            flops=20 * group * HD * total * total, bytes_accessed=8 * 2**20, transcendentals=0
        ),
        name="attend_back",
    )(bounds, q, k, v, kc, vc, o, lse, do_mine, do_other, id_row, id_col, cos_t, sin_t)


def finish_kernel(n, g, w, s, g_out, s_out, w_in, s_in, g_x, w_x, s_x, g_c, s_c, g_t, w_t, s_t,
                  w_send, w_recv, s_send, s_recv, x_send, x_recv, c_send, c_recv, local):
    me = lax.axis_index("fsdp")
    seat = lax.axis_index("seq")
    core = lax.rem(seat, 2)
    across = {"seq": lax.rem(seat + 2, 4)}
    beside = {"seq": seat + 1 - 2 * core}
    mesh_id = pl.DeviceIdType.MESH
    barrier = pltpu.get_barrier_semaphore()
    peers = [{"fsdp": lax.rem(me + d, n)} for d in range(1, n)]
    for where in peers + [across, beside]:
        pl.semaphore_signal(barrier, inc=1, device_id=where, device_id_type=mesh_id)
    pl.semaphore_wait(barrier, n + 1)

    def push(src, dst, one, two, where):
        copy = pltpu.make_async_remote_copy(
            src_ref=src, dst_ref=dst, send_sem=one, recv_sem=two, device_id=where,
            device_id_type=mesh_id,
        )
        copy.start()
        return copy

    def settle(tmp, out, sem):
        copy = pltpu.make_async_copy(tmp, out, sem)
        copy.start()
        copy.wait()

    first_s, first_w = [], []
    for d in range(1, n):
        to = lax.rem(me + d, n)
        first_s.append(
            push(s.at[to], s_in.at[d - 1], s_send.at[d - 1], s_recv.at[d - 1], peers[d - 1])
        )
        first_w.append(
            push(w.at[to], w_in.at[d - 1], w_send.at[d - 1], w_recv.at[d - 1], peers[d - 1])
        )
    far_g = push(g, g_x, x_send.at[0], x_recv.at[0], across)
    for copy in first_s:
        copy.wait()
    total = s[me]
    for d in range(n - 1):
        total = total + s_in[d]
    s_t[0] = total
    settle(s_t.at[0], s_x.at[0], local.at[0])
    far_s = push(s_x.at[0], s_x.at[1], x_send.at[1], x_recv.at[1], across)
    split = g.shape[1]
    span = split + w.shape[2]
    far_g.wait()
    g_t[:, :split] = (g[...].astype(F32) + g_x[...].astype(F32)).astype(BF)
    far_s.wait()
    s_t[1] = s_x[0] + s_x[1]
    settle(s_t.at[1], s_c.at[0], local.at[1])
    near_s = push(s_c.at[0], s_c.at[1], c_send.at[1], c_recv.at[1], beside)
    for copy in first_w:
        copy.wait()
    rows = w.shape[1]
    block = 16 if rows % 16 == 0 else rows

    def add_rows(i, _):
        at = pl.ds(pl.multiple_of(i * block, block), block)
        total = w[me, at, :].astype(F32)
        for d in range(n - 1):
            total = total + w_in[d, at, :].astype(F32)
        w_t[at, :] = total.astype(BF)
        return 0

    lax.fori_loop(0, rows // block, add_rows, 0)
    settle(w_t, w_x.at[0], local.at[2])
    far_w = push(w_x.at[0], w_x.at[1], x_send.at[2], x_recv.at[2], across)
    far_w.wait()
    g_t[:, split:] = (w_x[0].astype(F32) + w_x[1].astype(F32)).astype(BF)
    settle(g_t, g_c.at[core], local.at[3])
    near_g = push(g_c.at[core], g_c.at[core], c_send.at[0], c_recv.at[0], beside)
    near_s.wait()
    s_out[...] = s_c[0] + s_c[1]
    near_g.wait()
    for c in range(2):
        g_out[:, c * span : (c + 1) * span] = g_c[c].astype(F32)


def finish(g, w, s):
    n, rows, last = w.shape
    span = g.shape[1] + last
    vm = pl.BlockSpec(memory_space=pltpu.VMEM)
    dma = pltpu.SemaphoreType.DMA
    pair = pltpu.VMEM((2,) + s.shape[1:], F32)
    return pl.pallas_call(
        functools.partial(finish_kernel, n),
        in_specs=[vm] * 3,
        out_specs=[vm] * 2,
        out_shape=[
            jax.ShapeDtypeStruct((rows, 2 * span), F32),
            jax.ShapeDtypeStruct(s.shape[1:], F32),
        ],
        scratch_shapes=[
            pltpu.VMEM((n - 1, rows, last), BF),
            pltpu.VMEM((n - 1,) + s.shape[1:], F32),
            pltpu.VMEM(g.shape, BF),
            pltpu.VMEM((2, rows, last), BF),
            pair,
            pltpu.VMEM((2, rows, span), BF),
            pair,
            pltpu.VMEM((rows, span), BF),
            pltpu.VMEM((rows, last), BF),
            pair,
            dma((n - 1,)),
            dma((n - 1,)),
            dma((n - 1,)),
            dma((n - 1,)),
            dma((3,)),
            dma((3,)),
            dma((2,)),
            dma((2,)),
            dma((4,)),
        ],
        compiler_params=pltpu.CompilerParams(collective_id=1, has_side_effects=True),
        name="finish",
    )(g, w, s)


def on_device(
    tokens,
    block_ids,
    ln1_scale,
    ln1_bias,
    qkv_weight,
    qkv_bias,
    out_weight,
    out_bias,
    ln2_scale,
    ln2_bias,
    up_weight,
    up_bias,
    down_weight,
    down_bias,
    cotangent,
):
    tok = tokens[0]
    local_rows, width = tok.shape
    ids = block_ids[0].astype(jnp.int32)
    length = ids.shape[0]
    shard = ln1_scale.shape[0]
    heads = H // 2
    span = heads * HD
    me = lax.axis_index("seq")
    core = me % 2
    noisy = me < 2
    swap = [(0, 1), (1, 0), (2, 3), (3, 2)]
    other = lax.ppermute(tok, "seq", swap)
    clean_in = lax.ppermute(tok, "seq", [(2, 0), (3, 1)])
    clean_mine = jnp.where(noisy, clean_in, tok)
    clean_other = lax.ppermute(clean_mine, "seq", swap)

    q_cols = lax.dynamic_slice_in_dim(qkv_weight, core * 3 * span, 3 * span, 1)
    small = jnp.concatenate(
        [
            ln1_scale.reshape(1, shard),
            ln1_bias.reshape(1, shard),
            out_bias.reshape(1, shard),
            ln2_scale.reshape(1, shard),
            ln2_bias.reshape(1, shard),
            down_bias.reshape(1, shard),
            qkv_bias.reshape(-1, shard),
            up_bias.reshape(-1, shard),
        ],
        0,
    )
    n_small = small.shape[0]
    small = jnp.pad(small, ((0, 128 - n_small), (0, 0))).T
    gathered = lax.all_gather(
        jnp.concatenate([q_cols, small], 1), "fsdp", axis=0, tiled=True
    )
    n_fsdp = width // shard
    vectors = gathered[:, 3 * span :].reshape(n_fsdp, shard, 128)[:, :, :n_small]
    vectors = jnp.transpose(vectors, (2, 0, 1)).astype(F32)
    flat = vectors[:6].reshape(6, width)
    qkv_b = jnp.transpose(vectors[6:9], (1, 0, 2)).reshape(-1)
    scale_one, shift_one, out_shift, scale_two, shift_two, down_shift = [flat[i] for i in range(6)]

    inner = up_bias.shape[0] // 2
    up_b = jnp.transpose(vectors[9:], (1, 0, 2)).reshape(n_fsdp, 2, inner)
    up_b = lax.dynamic_index_in_dim(up_b, core, 1, False).reshape(-1)
    up_cols = lax.dynamic_index_in_dim(
        up_weight.reshape(shard, n_fsdp, 2, inner), core, 2, False
    ).reshape(shard, n_fsdp * inner)
    down_rows = lax.dynamic_slice_in_dim(down_weight, core * inner, inner, 0)
    out_cols = lax.dynamic_slice_in_dim(out_weight, core * span, span, 1)
    out_up = lax.all_gather(
        jnp.concatenate([out_cols, up_cols], 1), "fsdp", axis=0, tiled=True
    )
    down_own = lax.all_gather(down_rows, "fsdp", axis=0, tiled=True)
    in_order = lambda near, far, axis: jnp.where(
        core == 0, jnp.concatenate([near, far], axis), jnp.concatenate([far, near], axis)
    )
    cot_far = lax.ppermute(cotangent[0], "seq", swap)

    frequency = jnp.exp(-jnp.log(10000.0) * jnp.arange(HD // 2, dtype=F32) / (HD // 2))
    angles = frequency[:, None] * jnp.arange(length, dtype=F32)[None, :]
    cos_t, sin_t = jnp.cos(angles), jnp.sin(angles)

    first = ids[::TQ][:, None]
    last = ids[TQ - 1 :: TQ][:, None]
    before = lambda edge: jnp.sum((ids[None, :] < edge).astype(jnp.int32), 1)
    start_first, end_first = before(first), before(first + 1)
    start_last, end_last = before(last), before(last + 1)
    ceil_m = lambda value: (value + TM - 1) // TM
    lift = jnp.where(noisy, 0, 1)
    zero = jnp.zeros_like(start_first)
    bounds = jnp.stack(
        [
            jnp.where(noisy, start_first, end_first) // TK,
            ceil_m(jnp.where(noisy, start_last, end_last)),
            jnp.where(noisy, start_first // TM, zero),
            jnp.where(noisy, ceil_m(end_last), zero),
            zero + jnp.where(jnp.arange(zero.shape[0]) == 0, lift, core),
        ]
    ).astype(jnp.int32)
    id_row = jnp.broadcast_to(ids[None, :], (8, length))
    id_col = jnp.broadcast_to(ids[:, None], (length, 128))

    vec = jnp.concatenate([scale_one[None], shift_one[None], jnp.zeros((6, width), F32)], 0)
    bias_own = lax.dynamic_slice_in_dim(qkv_b, core * 3 * span, 3 * span, 0)
    bias_own = jnp.transpose(bias_own.reshape(heads, 3, HD), (1, 0, 2)).reshape(3 * span, 1)
    q, k, v, kc, vc, a_own = project(
        core.reshape(1).astype(jnp.int32), tok, other, clean_mine, clean_other, gathered, vec,
        bias_own, cos_t, sin_t, heads
    )
    o, lse = attend(bounds, q, k, v, kc, vc, id_row, id_col, heads, 2)
    o, lse, out_up, cot_far = lax.optimization_barrier((o, lse, out_up, cot_far))
    cot_both = jnp.concatenate([cotangent[0], cot_far], 0)
    out_near, up_own = out_up[:, :span], out_up[:, span:]
    out_full = in_order(out_near, lax.ppermute(out_near, "seq", swap), 1)
    cut = lambda value, which: lax.dynamic_slice_in_dim(value, which * local_rows, local_rows, 1)
    o_mine = cut(o, core)
    o_in = lax.ppermute(cut(o, 1 - core), "seq", swap)
    attended = in_order(o_mine, o_in, 0)

    rows_in = tok.astype(F32)
    hidden = rows_in + rows_contract(attended, out_full) + out_shift
    normed_two, inverse_two = normalize_parts(hidden)
    second_in = (normed_two * scale_two + shift_two).astype(BF)
    second_in, down_own = lax.optimization_barrier((second_in, down_own))
    both_in = jnp.concatenate([second_in, lax.ppermute(second_in, "seq", swap)], 0)

    def join(partial):
        return partial[:local_rows] + lax.ppermute(
            partial[local_rows:].astype(BF), "seq", swap
        ).astype(F32)

    pre_act = dot(both_in, up_own) + up_b
    root = (2 / math.pi) ** 0.5
    square = pre_act * pre_act
    bend = jnp.tanh(root * pre_act * (1 + 0.044715 * square))
    rise = 0.5 * (1 + bend)
    act_low = (pre_act * rise).astype(BF)
    curve = 0.5 * pre_act * (1 - bend * bend) * (1 + 3 * 0.044715 * square)
    slope = (rise + root * curve).astype(BF)
    grad_down_w = rows_contract(act_low, cot_both).astype(BF)
    scatter = lambda grad: lax.psum_scatter(grad, "fsdp", scatter_dimension=0, tiled=True)
    act_low, slope, grad_down_w, cot_both = lax.optimization_barrier(
        (act_low, slope, grad_down_w, cot_both)
    )
    down_part = scatter(grad_down_w)
    result = hidden + join(dot(act_low, down_own)) + down_shift

    grad_top = cotangent[0].astype(F32)
    grad_down_b = jnp.sum(grad_top, 0)
    grad_pre = (right_transposed(cot_both, down_own) * slope.astype(F32)).astype(BF)
    grad_second = join(right_transposed(grad_pre, up_own))
    grad_up_b = jnp.sum(grad_pre.astype(F32), 0)
    grad_up_w = rows_contract(both_in, grad_pre).astype(BF)
    grad_scale_two = jnp.sum(grad_second * normed_two, 0)
    grad_shift_two = jnp.sum(grad_second, 0)
    grad_hidden = grad_top + norm_backward(grad_second, normed_two, inverse_two, scale_two)

    grad_attn = grad_hidden.astype(BF)
    grad_out_w = dot(attended, grad_attn).astype(BF)
    grad_out_b = jnp.sum(grad_attn.astype(F32), 0)
    grad_o = right_transposed(out_full, grad_attn).astype(BF)
    cut_heads = lambda which: lax.dynamic_slice_in_dim(grad_o, which * span, span, 0)
    do_mine = cut_heads(core)
    do_in = lax.ppermute(cut_heads(1 - core), "seq", swap)
    cut_cols = lambda which: lax.dynamic_slice_in_dim(grad_out_w, which * span, span, 1)
    out_sum = (
        cut_cols(core).astype(F32) + lax.ppermute(cut_cols(1 - core), "seq", swap).astype(F32)
    ).astype(BF)
    do_mine, do_in, grad_up_w, out_sum = lax.optimization_barrier(
        (do_mine, do_in, grad_up_w, out_sum)
    )
    out_up_part = scatter(jnp.concatenate([out_sum, grad_up_w], 1))

    back_args = lambda mine: (
        bounds, q, k, v, kc, vc, o, lse, mine, do_in, id_row, id_col, cos_t, sin_t
    )
    hold = lax.optimization_barrier
    cross = [(0, 2), (1, 3), (2, 0), (3, 1)]
    to_clean = lambda send: lax.ppermute(send, "seq", [(0, 2), (1, 3)])
    pair_w = 2 * 3 * HD

    def joined(own, got):
        own = own.reshape(2, 3, HD, -1)
        key_value = own[:, 1:].astype(F32) + got.reshape(2, 2, HD, -1).astype(F32)
        return jnp.concatenate([own[:, :1], key_value.astype(BF)], 1).reshape(pair_w, -1)

    def weight_grad(own):
        return lax.dot_general(
            a_own, own, (((0,), (1,)), ((), ())), preferred_element_type=F32
        ).astype(BF)

    def back(own, first, count):
        cols = gathered[:, first * pair_w : (first + count) * pair_w]
        return lax.dot_general(
            own, cols, (((0,), (1,)), ((), ())), preferred_element_type=F32
        )

    own_0, send_0 = attend_back(*back_args(do_mine), 0, 2)
    send_0, do_mine = hold((send_0, do_mine))
    got_0 = to_clean(send_0)
    own_1, send_1 = attend_back(*back_args(do_mine), 1, 2)
    own_1, send_1, got_0, down_part = hold((own_1, send_1, got_0, down_part))
    got_1, down_far = to_clean(send_1), lax.ppermute(down_part, "seq", cross)
    own_0 = joined(own_0, got_0)
    grad_0, do_mine = hold((weight_grad(own_0), do_mine))
    own_2, send_2 = attend_back(*back_args(do_mine), 2, 2)
    own_2, send_2, got_1, down_far, out_up_part = hold(
        (own_2, send_2, got_1, down_far, out_up_part)
    )
    got_2 = to_clean(send_2)
    own_1 = joined(own_1, got_1)
    grad_01, own_1 = hold((jnp.concatenate([grad_0, weight_grad(own_1)], 1), own_1))
    part_01 = scatter(grad_01)
    own_01 = jnp.concatenate([own_0, own_1], 0)
    first_01 = back(own_01, 0, 2)
    got_2, out_up_part, first_01 = hold((got_2, out_up_part, first_01))
    own_2 = joined(own_2, got_2)
    far_rows = first_01[local_rows:] + back(own_2[:, local_rows:], 2, 1)
    got_rows = lax.ppermute(far_rows.astype(BF), "seq", swap).astype(F32)
    grad_first = first_01[:local_rows] + back(own_2[:, :local_rows], 2, 1) + got_rows
    grad_2 = weight_grad(own_2)

    def gather_cores(part, far):
        total = (part.astype(F32) + far.astype(F32)).astype(BF)
        return in_order(total[None], lax.ppermute(total, "seq", swap)[None], 0)

    down_g = gather_cores(down_part, down_far)
    out_up_g = gather_cores(out_up_part, lax.ppermute(out_up_part, "seq", cross))

    sum_cols = lambda own: jnp.sum(own.astype(F32), 1)
    grad_qkv_b = jnp.concatenate([sum_cols(own_01), sum_cols(own_2)])
    normed_one, inverse_one = normalize_parts(rows_in)
    grad_scale_one = jnp.sum(grad_first * normed_one, 0)
    grad_shift_one = jnp.sum(grad_first, 0)
    grad_rows = grad_hidden + norm_backward(grad_first, normed_one, inverse_one, scale_one)

    qkv_b_wide = lax.dynamic_update_slice_in_dim(
        jnp.zeros((2 * 3 * span,), F32), grad_qkv_b, core * 3 * span, 0
    )
    up_b_wide = lax.dynamic_update_slice_in_dim(
        jnp.zeros((n_fsdp, 2, inner), F32), grad_up_b.reshape(n_fsdp, 1, inner), core, 1
    )
    pieces = [
        piece.reshape(n_fsdp, -1)
        for piece in (
            grad_scale_one, grad_shift_one, qkv_b_wide, grad_out_b, grad_scale_two,
            grad_shift_two, up_b_wide, grad_down_b,
        )
    ]
    sizes = [piece.shape[1] for piece in pieces]
    packed = jnp.concatenate(pieces, 1)
    lines = -(-packed.shape[1] // 128)
    packed = jnp.pad(packed, ((0, 0), (0, lines * 128 - packed.shape[1])))
    packed = packed.reshape(n_fsdp, lines, 128)
    grad_rows, out_up_g, down_g, packed, part_01 = hold(
        (grad_rows, out_up_g, down_g, packed, part_01)
    )
    qkv_g, small_sum = finish(part_01, grad_2.reshape(n_fsdp, shard, pair_w), packed)
    small_sum = small_sum.reshape(-1)
    small_out, at = [], 0
    for size in sizes:
        small_out.append(small_sum[at : at + size])
        at += size
    side = lambda pair: jnp.concatenate([pair[0], pair[1]], 1).astype(F32)
    out_g, up_g = out_up_g[:, :, :span], out_up_g[:, :, span:]
    up_g = jnp.transpose(up_g.reshape(2, shard, n_fsdp, inner), (1, 2, 0, 3))
    return (
        result.astype(BF)[None],
        grad_rows[None],
        small_out[0],
        small_out[1],
        qkv_g,
        small_out[2],
        side(out_g),
        small_out[3],
        small_out[4],
        small_out[5],
        up_g.reshape(shard, -1).astype(F32),
        small_out[6],
        down_g.reshape(2 * inner, width).astype(F32),
        small_out[7],
    )


def solution(mesh):
    row, mat, vec = P("fsdp", "seq", None), P("fsdp", None), P("fsdp")
    in_specs = (row, mat, vec, vec, mat, vec, mat, vec, vec, vec, mat, vec, mat, vec, row)
    out_specs = (row, row, vec, vec, mat, vec, mat, vec, vec, vec, mat, vec, mat, vec)
    return jax.shard_map(
        on_device, mesh=mesh, in_specs=in_specs, out_specs=out_specs, check_vma=False
    )
```

```python
import functools
import math

import jax
import jax.numpy as jnp
from jax import lax
from jax.experimental import pallas as pl
from jax.experimental.pallas import tpu as pltpu
from jax.sharding import PartitionSpec as P

H = 12
HD = 64
EPSILON = 1e-05
LOG2E = 1.4426950408889634
NEG = -1e30
TQ = 512
TK = 256
TM = 256
BF = jnp.bfloat16
F32 = jnp.float32


def normalize_parts(values):
    mean_value = jnp.mean(values, -1, keepdims=True)
    centred = values - mean_value
    variance = jnp.mean(centred * centred, -1, keepdims=True)
    inverse = lax.rsqrt(variance + EPSILON)
    return (centred * inverse, inverse)


def norm_backward(grad_out, normed, inverse, scale):
    grad_norm = grad_out * scale
    return inverse * (
        grad_norm
        - jnp.mean(grad_norm, -1, keepdims=True)
        - normed * jnp.mean(grad_norm * normed, -1, keepdims=True)
    )


def rows_contract(left, right):
    return lax.dot_general(left, right, (((0,), (0,)), ((), ())), preferred_element_type=F32)


def right_transposed(left, right):
    return lax.dot_general(left, right, (((1,), (1,)), ((), ())), preferred_element_type=F32)


def dot(left, right):
    return jnp.dot(left, right, preferred_element_type=F32)


def qkv_kernel(heads, core_ref, mine, other, cmine, cother, w_ref, vec_ref, bias_ref, cos_ref,
               sin_ref, q_out, k_out, v_out, kc_out, vc_out, a_out, wt):
    step = pl.program_id(0)
    span = heads * HD

    @pl.when(step == 0)
    def _():
        whole = jnp.transpose(w_ref[...])
        for h in range(heads):
            for part in range(3):
                wt[part * span + h * HD : part * span + (h + 1) * HD, :] = whole[
                    (3 * h + part) * HD : (3 * h + part + 1) * HD, :
                ]

    def normed(rows):
        values = rows.astype(F32)
        n, _ = normalize_parts(values)
        return (n * vec_ref[0:1, :] + vec_ref[1:2, :]).astype(BF)

    def turn(lin, base, out):
        cos_t, sin_t = cos_ref[...], sin_ref[...]
        half = HD // 2
        for h in range(heads):
            first = lin[base + h * HD : base + h * HD + half, :]
            second = lin[base + h * HD + half : base + (h + 1) * HD, :]
            out[h * HD : h * HD + half, :] = (first * cos_t - second * sin_t).astype(BF)
            out[h * HD + half : (h + 1) * HD, :] = (first * sin_t + second * cos_t).astype(BF)

    quarter = pl.num_programs(0) // 4

    @pl.when(step < 2 * quarter)
    def _():
        a = normed(jnp.where(step < quarter, mine[...], other[...]))
        a_out[...] = a
        lin = right_transposed(wt[...], a) + bias_ref[...]
        turn(lin, 0, q_out)
        turn(lin, span, k_out)
        v_out[...] = lin[2 * span :, :].astype(BF)

    @pl.when(step >= 2 * quarter)
    def _():
        a = normed(jnp.where(step < 3 * quarter, cmine[...], cother[...]))
        lin = right_transposed(wt[span:, :], a) + bias_ref[span:, :]
        turn(lin, 0, kc_out)
        vc_out[...] = lin[span:, :].astype(BF)


def project(core, mine, other, cmine, cother, weight, vec, bias, cos_t, sin_t, heads):
    local, width = mine.shape
    span = heads * HD
    tile = 256
    n = local // tile

    def place(t, c):
        mine_first = jnp.where(t % (2 * n) < n, c[0], 1 - c[0])
        return mine_first * n + t % n

    def src(k):
        return pl.BlockSpec((tile, width), lambda t, c: (jnp.clip(t - k * n, 0, n - 1), 0))

    whole = lambda shape: pl.BlockSpec(shape, lambda t, c: (0, 0))
    own = pl.BlockSpec((span, tile), lambda t, c: (0, place(jnp.minimum(t, 2 * n - 1), c)))
    cln = pl.BlockSpec((span, tile), lambda t, c: (0, place(jnp.maximum(t, 2 * n), c)))
    own_a = pl.BlockSpec((tile, width), lambda t, c: (jnp.minimum(t, 2 * n - 1), 0))
    tab = pl.BlockSpec((HD // 2, tile), lambda t, c: (0, place(t, c)))
    head_shape = jax.ShapeDtypeStruct((span, 2 * local), BF)
    row_shape = jax.ShapeDtypeStruct((2 * local, width), BF)
    return pl.pallas_call(
        functools.partial(qkv_kernel, heads),
        grid_spec=pltpu.PrefetchScalarGridSpec(
            num_scalar_prefetch=1,
            grid=(4 * n,),
            in_specs=[src(0), src(1), src(2), src(3), whole((width, 3 * span)), whole(vec.shape),
                      whole(bias.shape), tab, tab],
            out_specs=[own, own, own, cln, cln, own_a],
            scratch_shapes=[pltpu.VMEM((3 * span, width), BF)],
        ),
        out_shape=[head_shape] * 5 + [row_shape],
        name="project",
    )(core, mine, other, cmine, cother, weight, vec, bias, cos_t, sin_t)


def attend_kernel(group, bounds, q, k, v, kc, vc, id_row, id_col, o_out, lse_out, ks, kcs, vs,
                  vcs):
    total = q.shape[1]
    scale = LOG2E * HD**-0.5
    ones = jnp.ones((16, total), BF)
    for h in range(group):
        rows = slice(h * HD, (h + 1) * HD)
        ks[h] = jnp.transpose(k[rows, :])
        kcs[h] = jnp.transpose(kc[rows, :])
        vs[h, :HD] = v[rows, :]
        vcs[h, :HD] = vc[rows, :]
        vs[h, HD:] = ones
        vcs[h, HD:] = ones
    lift = bounds[4, 0]

    lead = jnp.ones((8, HD), BF)
    top = lambda ref, rows: jnp.max(dot(lead, ref[rows, :] * ref[rows, :]))
    limit = jnp.float32(0.9 * (96.0 / scale) ** 2)
    small = None
    for h in range(group):
        rows = slice(h * HD, (h + 1) * HD)
        fits = top(q, rows) * jnp.maximum(top(k, rows), top(kc, rows)) < limit
        small = fits if small is None else jnp.logical_and(small, fits)

    def key_ids(keys):
        col = id_col[keys, :]
        return jnp.concatenate([col] * (TQ // 128), 1)

    def sweep(i, q_ids, update, state):
        def band(j, state):
            keys = pl.ds(pl.multiple_of(j * TM, TM), TM)
            return update(state, ks, vs, keys, key_ids(keys) == q_ids)

        def full(j, state):
            keys = pl.ds(pl.multiple_of(j * TK, TK), TK)
            return update(state, kcs, vcs, keys, None)

        def edge(j, state):
            keys = pl.ds(pl.multiple_of(j * TM, TM), TM)
            return update(state, kcs, vcs, keys, key_ids(keys) < q_ids + lift)

        state = lax.fori_loop(bounds[2, i], bounds[3, i], band, state)
        state = lax.fori_loop(0, bounds[0, i], full, state)
        return lax.fori_loop(bounds[0, i] * (TK // TM), bounds[1, i], edge, state)

    def store(h, at, acc, log_shift):
        total_w = acc[HD : HD + 1, :]
        o_out[h * HD : (h + 1) * HD, at] = (acc[:HD, :] / total_w).astype(BF)
        lse_out[h, :, at] = jnp.broadcast_to(log_shift + jnp.log2(total_w), (8, TQ))

    def plain_tile(i, _):
        at = pl.ds(pl.multiple_of(i * TQ, TQ), TQ)
        queries = [q[h * HD : (h + 1) * HD, at] for h in range(group)]

        def update(state, key_ref, val_ref, keys, mask):
            out = []
            for h in range(group):
                p = jnp.exp2(dot(key_ref[h, keys, :], queries[h]) * scale)
                if mask is not None:
                    p = jnp.where(mask, p, 0.0)
                out.append(state[h] + dot(val_ref[h, :, keys], p.astype(BF)))
            return tuple(out)

        state = (jnp.zeros((HD + 16, TQ), F32),) * group
        state = sweep(i, id_row[0:1, at], update, state)
        for h in range(group):
            store(h, at, state[h], 0.0)
        return 0

    def shifted_tile(i, _):
        at = pl.ds(pl.multiple_of(i * TQ, TQ), TQ)
        q_ids = id_row[0:1, at]
        for h in range(group):
            query = q[h * HD : (h + 1) * HD, at]

            def update(state, key_ref, val_ref, keys, mask):
                m, acc = state
                s = dot(key_ref[h, keys, :], query)
                if mask is not None:
                    s = jnp.where(mask, s, NEG)
                m_new = jnp.maximum(m, jnp.max(s, 0, keepdims=True))
                p = jnp.exp2((s - m_new) * scale).astype(BF)
                alpha = jnp.exp2((m - m_new) * scale)
                return m_new, acc * alpha + dot(val_ref[h, :, keys], p)

            state = (jnp.full((1, TQ), NEG, F32), jnp.zeros((HD + 16, TQ), F32))
            m, acc = sweep(i, q_ids, update, state)
            store(h, at, acc, m * scale)
        return 0

    @pl.when(small)
    def _():
        lax.fori_loop(0, total // TQ, plain_tile, 0)

    @pl.when(jnp.logical_not(small))
    def _():
        lax.fori_loop(0, total // TQ, shifted_tile, 0)


def attend(bounds, q, k, v, kc, vc, id_row, id_col, heads, group):
    total = q.shape[1]
    head = pl.BlockSpec((group * HD, total), lambda g, b: (g, 0))
    whole = lambda shape: pl.BlockSpec(shape, lambda g, b: (0, 0))
    return pl.pallas_call(
        functools.partial(attend_kernel, group),
        grid_spec=pltpu.PrefetchScalarGridSpec(
            num_scalar_prefetch=1,
            grid=(heads // group,),
            in_specs=[head] * 5 + [whole(id_row.shape), whole(id_col.shape)],
            out_specs=[head, pl.BlockSpec((group, 8, total), lambda g, b: (g, 0, 0))],
            scratch_shapes=[pltpu.VMEM((group, total, HD), BF)] * 2
            + [pltpu.VMEM((group, HD + 16, total), BF)] * 2,
        ),
        out_shape=[
            jax.ShapeDtypeStruct((heads * HD, total), BF),
            jax.ShapeDtypeStruct((heads, 8, total), F32),
        ],
        cost_estimate=pl.CostEstimate(
            flops=16 * heads * HD * total * total, bytes_accessed=2**24, transcendentals=0
        ),
        name="attend",
    )(bounds, q, k, v, kc, vc, id_row, id_col)


def attend_back_kernel(group, bounds, q, k, v, kc, vc, o, lse, do_mine, do_other, id_row, id_col,
                       cos_ref, sin_ref, own_out, cln_out, ks, vs, kcs, vcs, qs, dos, dot_s,
                       dk_acc, dv_acc, dkc_acc, dvc_acc, dq_acc):
    total = q.shape[1]
    half_rows = total // 2
    scale = LOG2E * HD**-0.5
    lift = bounds[4, 0]
    core = bounds[4, 1]
    near = pl.ds(pl.multiple_of(core * half_rows, 128), half_rows)
    far = pl.ds(pl.multiple_of((1 - core) * half_rows, 128), half_rows)
    dot_s[:, near] = do_mine[...]
    dot_s[:, far] = do_other[...]
    for h in range(group):
        rows = slice(h * HD, (h + 1) * HD)
        ks[h] = jnp.transpose(k[rows, :])
        vs[h] = jnp.transpose(v[rows, :])
        kcs[h] = jnp.transpose(kc[rows, :])
        vcs[h] = jnp.transpose(vc[rows, :])
        qs[h] = jnp.transpose(q[rows, :])
        dos[h] = jnp.transpose(dot_s[rows, :])
    for ref in (dk_acc, dv_acc, dkc_acc, dvc_acc):
        ref[...] = jnp.zeros_like(ref)

    def one_tile(i, _):
        at = pl.ds(pl.multiple_of(i * TQ, TQ), TQ)
        q_ids = id_row[0:1, at]
        queries, grads, deltas, sums, q_rows, g_rows = [], [], [], [], [], []
        for h in range(group):
            rows = slice(h * HD, (h + 1) * HD)
            queries.append(q[rows, at])
            g = dot_s[rows, at]
            grads.append(g)
            deltas.append(jnp.sum(g.astype(F32) * o[rows, at].astype(F32), 0, keepdims=True))
            sums.append(lse[h, 0:1, at])
            q_rows.append(qs[h, at, :])
            g_rows.append(dos[h, at, :])

        def update(state, key_ref, val_ref, key_cols, dk, dv, keys, mask):
            out = []
            for h in range(group):
                s = dot(key_ref[h, keys, :], queries[h])
                p = jnp.exp2(s * scale - sums[h])
                if mask is not None:
                    p = jnp.where(mask, p, 0.0)
                dp = dot(val_ref[h, keys, :], grads[h])
                ds = (p * (dp - deltas[h])).astype(BF)
                dv[h, keys, :] += dot(p.astype(BF), g_rows[h])
                dk[h, keys, :] += dot(ds, q_rows[h])
                out.append(state[h] + dot(key_cols[h * HD : (h + 1) * HD, keys], ds))
            return tuple(out)

        def key_ids(keys):
            col = id_col[keys, :]
            return jnp.concatenate([col] * (TQ // 128), 1)

        def band(j, state):
            keys = pl.ds(pl.multiple_of(j * TM, TM), TM)
            return update(state, ks, vs, k, dk_acc, dv_acc, keys, key_ids(keys) == q_ids)

        def full(j, state):
            keys = pl.ds(pl.multiple_of(j * TK, TK), TK)
            return update(state, kcs, vcs, kc, dkc_acc, dvc_acc, keys, None)

        def edge(j, state):
            keys = pl.ds(pl.multiple_of(j * TM, TM), TM)
            mask = key_ids(keys) < q_ids + lift
            return update(state, kcs, vcs, kc, dkc_acc, dvc_acc, keys, mask)

        state = (jnp.zeros((HD, TQ), F32),) * group
        state = lax.fori_loop(bounds[2, i], bounds[3, i], band, state)
        state = lax.fori_loop(0, bounds[0, i], full, state)
        state = lax.fori_loop(bounds[0, i] * (TK // TM), bounds[1, i], edge, state)
        for h in range(group):
            dq_acc[h * HD : (h + 1) * HD, at] = state[h]
        return 0

    lax.fori_loop(0, total // TQ, one_tile, 0)

    half = HD // 2
    cos_t, sin_t = cos_ref[...], sin_ref[...]
    noisy = lift == 0

    def spread(out, value, base):
        rows = slice(base, base + value.shape[0])
        out[rows, near] = value[:, :half_rows].astype(BF)
        out[rows, far] = value[:, half_rows:].astype(BF)

    def back_turn(out, w, base):
        first, second = w[:half, :], w[half:, :]
        spread(out, first * cos_t + second * sin_t, base)
        spread(out, second * cos_t - first * sin_t, base + half)

    for h in range(group):
        back_turn(own_out, dq_acc[h * HD : (h + 1) * HD, :] * HD**-0.5, 3 * h * HD)
        band_k = jnp.where(noisy, dk_acc[h], dkc_acc[h])
        band_v = jnp.where(noisy, dv_acc[h], dvc_acc[h])
        back_turn(own_out, jnp.transpose(band_k) * HD**-0.5, (3 * h + 1) * HD)
        spread(own_out, jnp.transpose(band_v), (3 * h + 2) * HD)
        back_turn(cln_out, jnp.transpose(dkc_acc[h]) * HD**-0.5, 2 * h * HD)
        spread(cln_out, jnp.transpose(dvc_acc[h]), (2 * h + 1) * HD)


def attend_back(bounds, q, k, v, kc, vc, o, lse, do_mine, do_other, id_row, id_col, cos_t, sin_t,
                pair, group):
    total = q.shape[1]
    head = pl.BlockSpec((group * HD, total), lambda g, b: (pair, 0))
    halfhead = pl.BlockSpec((group * HD, total // 2), lambda g, b: (pair, 0))
    whole = lambda shape: pl.BlockSpec(shape, lambda g, b: (0, 0))
    rows16 = pltpu.VMEM((group, total, HD), BF)
    rows32 = pltpu.VMEM((group, total, HD), F32)
    outs = [(group * 3 * HD, total), (group * 2 * HD, total)]
    return pl.pallas_call(
        functools.partial(attend_back_kernel, group),
        grid_spec=pltpu.PrefetchScalarGridSpec(
            num_scalar_prefetch=1,
            grid=(1,),
            in_specs=[head] * 6
            + [pl.BlockSpec((group, 8, total), lambda g, b: (pair, 0, 0)), halfhead, halfhead]
            + [whole(id_row.shape), whole(id_col.shape), whole(cos_t.shape), whole(sin_t.shape)],
            out_specs=[whole(shape) for shape in outs],
            scratch_shapes=[rows16] * 6
            + [pltpu.VMEM((group * HD, total), BF)]
            + [rows32] * 4
            + [pltpu.VMEM((group * HD, total), F32)],
        ),
        out_shape=[jax.ShapeDtypeStruct(shape, BF) for shape in outs],
        cost_estimate=pl.CostEstimate(
            flops=20 * group * HD * total * total, bytes_accessed=8 * 2**20, transcendentals=0
        ),
        name="attend_back",
    )(bounds, q, k, v, kc, vc, o, lse, do_mine, do_other, id_row, id_col, cos_t, sin_t)


def finish_kernel(n, g, w, s, g_out, s_out, w_in, s_in, g_x, w_x, s_x, g_c, s_c, g_t, w_t, s_t,
                  w_send, w_recv, s_send, s_recv, x_send, x_recv, c_send, c_recv, local):
    me = lax.axis_index("fsdp")
    seat = lax.axis_index("seq")
    core = lax.rem(seat, 2)
    across = {"seq": lax.rem(seat + 2, 4)}
    beside = {"seq": seat + 1 - 2 * core}
    mesh_id = pl.DeviceIdType.MESH
    barrier = pltpu.get_barrier_semaphore()
    peers = [{"fsdp": lax.rem(me + d, n)} for d in range(1, n)]
    for where in peers + [across, beside]:
        pl.semaphore_signal(barrier, inc=1, device_id=where, device_id_type=mesh_id)
    pl.semaphore_wait(barrier, n + 1)

    def push(src, dst, one, two, where):
        copy = pltpu.make_async_remote_copy(
            src_ref=src, dst_ref=dst, send_sem=one, recv_sem=two, device_id=where,
            device_id_type=mesh_id,
        )
        copy.start()
        return copy

    def settle(tmp, out, sem):
        copy = pltpu.make_async_copy(tmp, out, sem)
        copy.start()
        copy.wait()

    first_s, first_w = [], []
    for d in range(1, n):
        to = lax.rem(me + d, n)
        first_s.append(
            push(s.at[to], s_in.at[d - 1], s_send.at[d - 1], s_recv.at[d - 1], peers[d - 1])
        )
        first_w.append(
            push(w.at[to], w_in.at[d - 1], w_send.at[d - 1], w_recv.at[d - 1], peers[d - 1])
        )
    far_g = push(g, g_x, x_send.at[0], x_recv.at[0], across)
    for copy in first_s:
        copy.wait()
    total = s[me]
    for d in range(n - 1):
        total = total + s_in[d]
    s_t[0] = total
    settle(s_t.at[0], s_x.at[0], local.at[0])
    far_s = push(s_x.at[0], s_x.at[1], x_send.at[1], x_recv.at[1], across)
    split = g.shape[1]
    span = split + w.shape[2]
    far_g.wait()
    g_t[:, :split] = (g[...].astype(F32) + g_x[...].astype(F32)).astype(BF)
    far_s.wait()
    s_t[1] = s_x[0] + s_x[1]
    settle(s_t.at[1], s_c.at[0], local.at[1])
    near_s = push(s_c.at[0], s_c.at[1], c_send.at[1], c_recv.at[1], beside)
    for copy in first_w:
        copy.wait()
    rows = w.shape[1]
    block = 16 if rows % 16 == 0 else rows

    def add_rows(i, _):
        at = pl.ds(pl.multiple_of(i * block, block), block)
        total = w[me, at, :].astype(F32)
        for d in range(n - 1):
            total = total + w_in[d, at, :].astype(F32)
        w_t[at, :] = total.astype(BF)
        return 0

    lax.fori_loop(0, rows // block, add_rows, 0)
    settle(w_t, w_x.at[0], local.at[2])
    far_w = push(w_x.at[0], w_x.at[1], x_send.at[2], x_recv.at[2], across)
    far_w.wait()
    g_t[:, split:] = (w_x[0].astype(F32) + w_x[1].astype(F32)).astype(BF)
    settle(g_t, g_c.at[core], local.at[3])
    near_g = push(g_c.at[core], g_c.at[core], c_send.at[0], c_recv.at[0], beside)
    near_s.wait()
    s_out[...] = s_c[0] + s_c[1]
    near_g.wait()
    for c in range(2):
        g_out[:, c * span : (c + 1) * span] = g_c[c].astype(F32)


def finish(g, w, s):
    n, rows, last = w.shape
    span = g.shape[1] + last
    vm = pl.BlockSpec(memory_space=pltpu.VMEM)
    dma = pltpu.SemaphoreType.DMA
    pair = pltpu.VMEM((2,) + s.shape[1:], F32)
    return pl.pallas_call(
        functools.partial(finish_kernel, n),
        in_specs=[vm] * 3,
        out_specs=[vm] * 2,
        out_shape=[
            jax.ShapeDtypeStruct((rows, 2 * span), F32),
            jax.ShapeDtypeStruct(s.shape[1:], F32),
        ],
        scratch_shapes=[
            pltpu.VMEM((n - 1, rows, last), BF),
            pltpu.VMEM((n - 1,) + s.shape[1:], F32),
            pltpu.VMEM(g.shape, BF),
            pltpu.VMEM((2, rows, last), BF),
            pair,
            pltpu.VMEM((2, rows, span), BF),
            pair,
            pltpu.VMEM((rows, span), BF),
            pltpu.VMEM((rows, last), BF),
            pair,
            dma((n - 1,)),
            dma((n - 1,)),
            dma((n - 1,)),
            dma((n - 1,)),
            dma((3,)),
            dma((3,)),
            dma((2,)),
            dma((2,)),
            dma((4,)),
        ],
        compiler_params=pltpu.CompilerParams(collective_id=1, has_side_effects=True),
        name="finish",
    )(g, w, s)


def assemble_kernel(span, inner, core_ref, mine, other, d_mine, d_other, out_ref, up_ref, down_ref):
    first_core = core_ref[0] == 0
    pick = lambda one, two: (
        jnp.where(first_core, one, two).astype(F32), jnp.where(first_core, two, one).astype(F32)
    )
    first, second = pick(mine[...].astype(F32), other[...].astype(F32))
    out_ref[:, :span] = first[:, :span]
    out_ref[:, span:] = second[:, :span]
    for i in range((first.shape[1] - span) // inner):
        cols = slice(span + i * inner, span + (i + 1) * inner)
        up_ref[:, 2 * i * inner : 2 * (i + 1) * inner] = jnp.concatenate(
            [first[:, cols], second[:, cols]], 1
        )
    first, second = pick(d_mine[...].astype(F32), d_other[...].astype(F32))
    down_ref[: first.shape[0], :] = first
    down_ref[first.shape[0] :, :] = second


def assemble(core, mine, other, d_mine, d_other, span, inner):
    rows, width = mine.shape
    vm = pl.BlockSpec(memory_space=pltpu.VMEM)
    return pl.pallas_call(
        functools.partial(assemble_kernel, span, inner),
        in_specs=[pl.BlockSpec(memory_space=pltpu.SMEM)] + [vm] * 4,
        out_specs=[vm] * 3,
        out_shape=[
            jax.ShapeDtypeStruct((rows, 2 * span), F32),
            jax.ShapeDtypeStruct((rows, 2 * (width - span)), F32),
            jax.ShapeDtypeStruct((2 * d_mine.shape[0], d_mine.shape[1]), F32),
        ],
        name="assemble",
    )(core, mine, other, d_mine, d_other)


def on_device(
    tokens,
    block_ids,
    ln1_scale,
    ln1_bias,
    qkv_weight,
    qkv_bias,
    out_weight,
    out_bias,
    ln2_scale,
    ln2_bias,
    up_weight,
    up_bias,
    down_weight,
    down_bias,
    cotangent,
):
    tok = tokens[0]
    local_rows, width = tok.shape
    ids = block_ids[0].astype(jnp.int32)
    length = ids.shape[0]
    shard = ln1_scale.shape[0]
    heads = H // 2
    span = heads * HD
    me = lax.axis_index("seq")
    core = me % 2
    noisy = me < 2
    swap = [(0, 1), (1, 0), (2, 3), (3, 2)]
    other = lax.ppermute(tok, "seq", swap)
    clean_in = lax.ppermute(tok, "seq", [(2, 0), (3, 1)])
    cot_far = lax.ppermute(cotangent[0], "seq", swap)

    q_cols = lax.dynamic_slice_in_dim(qkv_weight, core * 3 * span, 3 * span, 1)
    small = jnp.concatenate(
        [
            ln1_scale.reshape(1, shard),
            ln1_bias.reshape(1, shard),
            out_bias.reshape(1, shard),
            ln2_scale.reshape(1, shard),
            ln2_bias.reshape(1, shard),
            down_bias.reshape(1, shard),
            qkv_bias.reshape(-1, shard),
            up_bias.reshape(-1, shard),
        ],
        0,
    )
    n_small = small.shape[0]
    small = jnp.pad(small, ((0, 128 - n_small), (0, 0))).T
    gathered = lax.all_gather(
        jnp.concatenate([q_cols, small], 1), "fsdp", axis=0, tiled=True
    )
    n_fsdp = width // shard
    vectors = gathered[:, 3 * span :].reshape(n_fsdp, shard, 128)[:, :, :n_small]
    vectors = jnp.transpose(vectors, (2, 0, 1)).astype(F32)
    flat = vectors[:6].reshape(6, width)
    qkv_b = jnp.transpose(vectors[6:9], (1, 0, 2)).reshape(-1)
    scale_one, shift_one, out_shift, scale_two, shift_two, down_shift = [flat[i] for i in range(6)]

    inner = up_bias.shape[0] // 2
    up_b = jnp.transpose(vectors[9:], (1, 0, 2)).reshape(n_fsdp, 2, inner)
    up_b = lax.dynamic_index_in_dim(up_b, core, 1, False).reshape(-1)
    up_cols = lax.dynamic_index_in_dim(
        up_weight.reshape(shard, n_fsdp, 2, inner), core, 2, False
    ).reshape(shard, n_fsdp * inner)
    down_rows = lax.dynamic_slice_in_dim(down_weight, core * inner, inner, 0)
    out_cols = lax.dynamic_slice_in_dim(out_weight, core * span, span, 1)
    out_up = lax.all_gather(
        jnp.concatenate([out_cols, up_cols], 1), "fsdp", axis=0, tiled=True
    )
    down_own = lax.all_gather(down_rows, "fsdp", axis=0, tiled=True)
    in_order = lambda near, far, axis: jnp.where(
        core == 0, jnp.concatenate([near, far], axis), jnp.concatenate([far, near], axis)
    )

    frequency = jnp.exp(-jnp.log(10000.0) * jnp.arange(HD // 2, dtype=F32) / (HD // 2))
    angles = frequency[:, None] * jnp.arange(length, dtype=F32)[None, :]
    cos_t, sin_t = jnp.cos(angles), jnp.sin(angles)

    first = ids[::TQ][:, None]
    last = ids[TQ - 1 :: TQ][:, None]
    before = lambda edge: jnp.sum((ids[None, :] < edge).astype(jnp.int32), 1)
    start_first, end_first = before(first), before(first + 1)
    start_last, end_last = before(last), before(last + 1)
    ceil_m = lambda value: (value + TM - 1) // TM
    lift = jnp.where(noisy, 0, 1)
    zero = jnp.zeros_like(start_first)
    bounds = jnp.stack(
        [
            jnp.where(noisy, start_first, end_first) // TK,
            ceil_m(jnp.where(noisy, start_last, end_last)),
            jnp.where(noisy, start_first // TM, zero),
            jnp.where(noisy, ceil_m(end_last), zero),
            zero + jnp.where(jnp.arange(zero.shape[0]) == 0, lift, core),
        ]
    ).astype(jnp.int32)
    id_row = jnp.broadcast_to(ids[None, :], (8, length))
    id_col = jnp.broadcast_to(ids[:, None], (length, 128))

    cot_both = jnp.concatenate([cotangent[0], cot_far], 0)
    clean_in, cot_both, cos_t, sin_t, bounds, id_row, id_col = lax.optimization_barrier(
        (clean_in, cot_both, cos_t, sin_t, bounds, id_row, id_col)
    )
    clean_mine = jnp.where(noisy, clean_in, tok)
    clean_other = lax.ppermute(clean_mine, "seq", swap)

    vec = jnp.concatenate([scale_one[None], shift_one[None], jnp.zeros((6, width), F32)], 0)
    bias_own = lax.dynamic_slice_in_dim(qkv_b, core * 3 * span, 3 * span, 0)
    bias_own = jnp.transpose(bias_own.reshape(heads, 3, HD), (1, 0, 2)).reshape(3 * span, 1)
    q, k, v, kc, vc, a_own = project(
        core.reshape(1).astype(jnp.int32), tok, other, clean_mine, clean_other, gathered, vec,
        bias_own, cos_t, sin_t, heads
    )
    o, lse = attend(bounds, q, k, v, kc, vc, id_row, id_col, heads, 2)
    o, lse, out_up = lax.optimization_barrier((o, lse, out_up))
    out_near, up_own = out_up[:, :span], out_up[:, span:]
    out_full = in_order(out_near, lax.ppermute(out_near, "seq", swap), 1)
    cut = lambda value, which: lax.dynamic_slice_in_dim(value, which * local_rows, local_rows, 1)
    o_mine = cut(o, core)
    o_in = lax.ppermute(cut(o, 1 - core), "seq", swap)
    attended = in_order(o_mine, o_in, 0)

    rows_in = tok.astype(F32)
    hidden = rows_in + rows_contract(attended, out_full) + out_shift
    normed_two, inverse_two = normalize_parts(hidden)
    second_in = (normed_two * scale_two + shift_two).astype(BF)
    second_in, down_own = lax.optimization_barrier((second_in, down_own))
    both_in = jnp.concatenate([second_in, lax.ppermute(second_in, "seq", swap)], 0)

    def join(partial):
        return partial[:local_rows] + lax.ppermute(
            partial[local_rows:].astype(BF), "seq", swap
        ).astype(F32)

    pre_act = dot(both_in, up_own) + up_b
    root = (2 / math.pi) ** 0.5
    square = pre_act * pre_act
    bend = jnp.tanh(root * pre_act * (1 + 0.044715 * square))
    rise = 0.5 * (1 + bend)
    act_low = (pre_act * rise).astype(BF)
    curve = 0.5 * pre_act * (1 - bend * bend) * (1 + 3 * 0.044715 * square)
    slope = (rise + root * curve).astype(BF)
    grad_down_w = rows_contract(act_low, cot_both).astype(BF)
    scatter = lambda grad: lax.psum_scatter(grad, "fsdp", scatter_dimension=0, tiled=True)
    act_low, slope, grad_down_w, cot_both = lax.optimization_barrier(
        (act_low, slope, grad_down_w, cot_both)
    )
    down_part = scatter(grad_down_w)
    result = hidden + join(dot(act_low, down_own)) + down_shift

    grad_top = cotangent[0].astype(F32)
    grad_down_b = jnp.sum(grad_top, 0)
    grad_pre = (right_transposed(cot_both, down_own) * slope.astype(F32)).astype(BF)
    grad_second = join(right_transposed(grad_pre, up_own))
    grad_up_b = jnp.sum(grad_pre.astype(F32), 0)
    grad_up_w = rows_contract(both_in, grad_pre).astype(BF)
    grad_scale_two = jnp.sum(grad_second * normed_two, 0)
    grad_shift_two = jnp.sum(grad_second, 0)
    grad_hidden = grad_top + norm_backward(grad_second, normed_two, inverse_two, scale_two)

    grad_attn = grad_hidden.astype(BF)
    grad_out_w = dot(attended, grad_attn).astype(BF)
    grad_out_b = jnp.sum(grad_attn.astype(F32), 0)
    grad_o = right_transposed(out_full, grad_attn).astype(BF)
    cut_heads = lambda which: lax.dynamic_slice_in_dim(grad_o, which * span, span, 0)
    do_mine = cut_heads(core)
    do_in = lax.ppermute(cut_heads(1 - core), "seq", swap)
    cut_cols = lambda which: lax.dynamic_slice_in_dim(grad_out_w, which * span, span, 1)
    out_sum = (
        cut_cols(core).astype(F32) + lax.ppermute(cut_cols(1 - core), "seq", swap).astype(F32)
    ).astype(BF)
    do_mine, do_in, grad_up_w, out_sum = lax.optimization_barrier(
        (do_mine, do_in, grad_up_w, out_sum)
    )
    out_up_part = scatter(jnp.concatenate([out_sum, grad_up_w], 1))

    back_args = lambda mine: (
        bounds, q, k, v, kc, vc, o, lse, mine, do_in, id_row, id_col, cos_t, sin_t
    )
    hold = lax.optimization_barrier
    cross = [(0, 2), (1, 3), (2, 0), (3, 1)]
    to_clean = lambda send: lax.ppermute(send, "seq", [(0, 2), (1, 3)])
    pair_w = 2 * 3 * HD

    def joined(own, got):
        own = own.reshape(2, 3, HD, -1)
        key_value = own[:, 1:].astype(F32) + got.reshape(2, 2, HD, -1).astype(F32)
        return jnp.concatenate([own[:, :1], key_value.astype(BF)], 1).reshape(pair_w, -1)

    def weight_grad(own):
        return lax.dot_general(
            a_own, own, (((0,), (1,)), ((), ())), preferred_element_type=F32
        ).astype(BF)

    def back(own, first, count):
        cols = gathered[:, first * pair_w : (first + count) * pair_w]
        return lax.dot_general(
            own, cols, (((0,), (1,)), ((), ())), preferred_element_type=F32
        )

    own_0, send_0 = attend_back(*back_args(do_mine), 0, 2)
    send_0, do_mine = hold((send_0, do_mine))
    got_0 = to_clean(send_0)
    own_1, send_1 = attend_back(*back_args(do_mine), 1, 2)
    own_1, send_1, got_0, down_part = hold((own_1, send_1, got_0, down_part))
    got_1, down_far = to_clean(send_1), lax.ppermute(down_part, "seq", cross)
    own_0 = joined(own_0, got_0)
    grad_0, do_mine = hold((weight_grad(own_0), do_mine))
    own_2, send_2 = attend_back(*back_args(do_mine), 2, 2)
    own_2, send_2, got_1, down_far, out_up_part = hold(
        (own_2, send_2, got_1, down_far, out_up_part)
    )
    got_2 = to_clean(send_2)
    own_1 = joined(own_1, got_1)
    grad_01, own_1 = hold((jnp.concatenate([grad_0, weight_grad(own_1)], 1), own_1))
    exchange = lambda grad: lax.all_to_all(
        grad.reshape(n_fsdp, shard, grad.shape[1]), "fsdp", 0, 0
    )
    piece_sum = lambda pieces: functools.reduce(
        jnp.add, [pieces[d].astype(F32) for d in range(n_fsdp)]
    ).astype(BF)
    pieces_01 = exchange(grad_01)
    own_01 = jnp.concatenate([own_0, own_1], 0)
    first_01 = back(own_01, 0, 2)
    got_2, out_up_part, first_01 = hold((got_2, out_up_part, first_01))
    own_2 = joined(own_2, got_2)
    far_rows = (first_01[local_rows:] + back(own_2[:, local_rows:], 2, 1)).astype(BF)
    got_rows = lax.ppermute(far_rows, "seq", swap).astype(F32)
    grad_2 = weight_grad(own_2)
    grad_first = first_01[:local_rows] + back(own_2[:, :local_rows], 2, 1) + got_rows

    def chip_sum(part, far):
        total = (part.astype(F32) + far.astype(F32)).astype(BF)
        return total, lax.ppermute(total, "seq", swap)

    out_up_both = chip_sum(out_up_part, lax.ppermute(out_up_part, "seq", cross))
    out_g, up_g, down_g = assemble(
        core.reshape(1).astype(jnp.int32), *out_up_both, *chip_sum(down_part, down_far), span, inner
    )

    sum_cols = lambda own: jnp.sum(own.astype(F32), 1)
    grad_qkv_b = jnp.concatenate([sum_cols(own_01), sum_cols(own_2)])
    normed_one, inverse_one = normalize_parts(rows_in)
    grad_scale_one = jnp.sum(grad_first * normed_one, 0)
    grad_shift_one = jnp.sum(grad_first, 0)
    grad_rows = grad_hidden + norm_backward(grad_first, normed_one, inverse_one, scale_one)

    qkv_b_wide = lax.dynamic_update_slice_in_dim(
        jnp.zeros((2 * 3 * span,), F32), grad_qkv_b, core * 3 * span, 0
    )
    up_b_wide = lax.dynamic_update_slice_in_dim(
        jnp.zeros((n_fsdp, 2, inner), F32), grad_up_b.reshape(n_fsdp, 1, inner), core, 1
    )
    pieces = [
        piece.reshape(n_fsdp, -1)
        for piece in (
            grad_scale_one, grad_shift_one, qkv_b_wide, grad_out_b, grad_scale_two,
            grad_shift_two, up_b_wide, grad_down_b,
        )
    ]
    sizes = [piece.shape[1] for piece in pieces]
    packed = jnp.concatenate(pieces, 1)
    lines = -(-packed.shape[1] // 128)
    packed = jnp.pad(packed, ((0, 0), (0, lines * 128 - packed.shape[1])))
    packed = packed.reshape(n_fsdp, lines, 128)
    part_01 = piece_sum(pieces_01)
    grad_rows, out_g, up_g, down_g, packed, part_01 = hold(
        (grad_rows, out_g, up_g, down_g, packed, part_01)
    )
    qkv_g, small_sum = finish(part_01, grad_2.reshape(n_fsdp, shard, pair_w), packed)
    small_sum = small_sum.reshape(-1)
    small_out, at = [], 0
    for size in sizes:
        small_out.append(small_sum[at : at + size])
        at += size
    return (
        result.astype(BF)[None],
        grad_rows[None],
        small_out[0],
        small_out[1],
        qkv_g,
        small_out[2],
        out_g,
        small_out[3],
        small_out[4],
        small_out[5],
        up_g,
        small_out[6],
        down_g,
        small_out[7],
    )


def solution(mesh):
    row, mat, vec = P("fsdp", "seq", None), P("fsdp", None), P("fsdp")
    in_specs = (row, mat, vec, vec, mat, vec, mat, vec, vec, vec, mat, vec, mat, vec, row)
    out_specs = (row, row, vec, vec, mat, vec, mat, vec, vec, vec, mat, vec, mat, vec)
    return jax.shard_map(
        on_device, mesh=mesh, in_specs=in_specs, out_specs=out_specs, check_vma=False
    )
```

```python
import functools
import math

import jax
import jax.numpy as jnp
from jax import lax
from jax.experimental import pallas as pl
from jax.experimental.pallas import tpu as pltpu
from jax.sharding import PartitionSpec as P

H = 12
HD = 64
EPSILON = 1e-05
LOG2E = 1.4426950408889634
NEG = -1e30
TQ = 512
TK = 256
TM = 256
FK = 1024
BF = jnp.bfloat16
F32 = jnp.float32


def normalize_parts(values):
    mean_value = jnp.mean(values, -1, keepdims=True)
    centred = values - mean_value
    variance = jnp.mean(centred * centred, -1, keepdims=True)
    inverse = lax.rsqrt(variance + EPSILON)
    return (centred * inverse, inverse)


def norm_backward(grad_out, normed, inverse, scale):
    grad_norm = grad_out * scale
    return inverse * (
        grad_norm
        - jnp.mean(grad_norm, -1, keepdims=True)
        - normed * jnp.mean(grad_norm * normed, -1, keepdims=True)
    )


def rows_contract(left, right):
    return lax.dot_general(left, right, (((0,), (0,)), ((), ())), preferred_element_type=F32)


def right_transposed(left, right):
    return lax.dot_general(left, right, (((1,), (1,)), ((), ())), preferred_element_type=F32)


def dot(left, right):
    return jnp.dot(left, right, preferred_element_type=F32)


def qkv_kernel(heads, core_ref, mine, other, mine_c, other_c, sent, sent_other, w_ref, vec_ref, bias_ref, cos_ref,
               sin_ref, q_out, k_out, v_out, kc_out, vc_out, a_out, wt):
    step = pl.program_id(0)
    span = heads * HD

    @pl.when(step == 0)
    def _():
        whole = jnp.transpose(w_ref[...])
        for h in range(heads):
            for part in range(3):
                wt[part * span + h * HD : part * span + (h + 1) * HD, :] = whole[
                    (3 * h + part) * HD : (3 * h + part + 1) * HD, :
                ]

    def normed(rows):
        values = rows.astype(F32)
        n, _ = normalize_parts(values)
        return (n * vec_ref[0:1, :] + vec_ref[1:2, :]).astype(BF)

    def turn(lin, base, out):
        cos_t, sin_t = cos_ref[...], sin_ref[...]
        half = HD // 2
        for h in range(heads):
            first = lin[base + h * HD : base + h * HD + half, :]
            second = lin[base + h * HD + half : base + (h + 1) * HD, :]
            out[h * HD : h * HD + half, :] = (first * cos_t - second * sin_t).astype(BF)
            out[h * HD + half : (h + 1) * HD, :] = (first * sin_t + second * cos_t).astype(BF)

    quarter = pl.num_programs(0) // 4

    @pl.when(step < 2 * quarter)
    def _():
        a = normed(jnp.where(step < quarter, mine[...], other[...]))
        a_out[...] = a
        lin = right_transposed(wt[...], a) + bias_ref[...]
        turn(lin, 0, q_out)
        turn(lin, span, k_out)
        v_out[...] = lin[2 * span :, :].astype(BF)

    @pl.when(step >= 2 * quarter)
    def _():
        here = jnp.where(step < 3 * quarter, mine_c[...], other_c[...])
        there = jnp.where(step < 3 * quarter, sent[...], sent_other[...])
        a = normed(jnp.where(core_ref[1] == 1, there, here))
        lin = right_transposed(wt[span:, :], a) + bias_ref[span:, :]
        turn(lin, 0, kc_out)
        vc_out[...] = lin[span:, :].astype(BF)


def project(core, mine, other, sent, sent_other, weight, vec, bias, cos_t, sin_t, heads):
    local, width = mine.shape
    span = heads * HD
    tile = 256
    n = local // tile

    def place(t, c):
        mine_first = jnp.where(t % (2 * n) < n, c[0], 1 - c[0])
        return mine_first * n + t % n

    def src(k):
        return pl.BlockSpec((tile, width), lambda t, c: (jnp.clip(t - k * n, 0, n - 1), 0))

    whole = lambda shape: pl.BlockSpec(shape, lambda t, c: (0, 0))
    own = pl.BlockSpec((span, tile), lambda t, c: (0, place(jnp.minimum(t, 2 * n - 1), c)))
    cln = pl.BlockSpec((span, tile), lambda t, c: (0, place(jnp.maximum(t, 2 * n), c)))
    own_a = pl.BlockSpec((tile, width), lambda t, c: (jnp.minimum(t, 2 * n - 1), 0))
    tab = pl.BlockSpec((HD // 2, tile), lambda t, c: (0, place(t, c)))
    head_shape = jax.ShapeDtypeStruct((span, 2 * local), BF)
    row_shape = jax.ShapeDtypeStruct((2 * local, width), BF)
    return pl.pallas_call(
        functools.partial(qkv_kernel, heads),
        grid_spec=pltpu.PrefetchScalarGridSpec(
            num_scalar_prefetch=1,
            grid=(4 * n,),
            in_specs=[src(0), src(1)] + [src(2), src(3)] * 2 + [whole((width, 3 * span)), whole(vec.shape),
                      whole(bias.shape), tab, tab],
            out_specs=[own, own, own, cln, cln, own_a],
            scratch_shapes=[pltpu.VMEM((3 * span, width), BF)],
        ),
        out_shape=[head_shape] * 5 + [row_shape],
        name="project",
    )(core, mine, other, mine, other, sent, sent_other, weight, vec, bias, cos_t, sin_t)


def attend_kernel(group, bounds, q, k, v, kc, vc, id_row, id_col, o_out, lse_out, ks, kcs, vs,
                  vcs):
    total = q.shape[1]
    scale = LOG2E * HD**-0.5
    ones = jnp.ones((16, total), BF)
    for h in range(group):
        rows = slice(h * HD, (h + 1) * HD)
        ks[h] = jnp.transpose(k[rows, :])
        kcs[h] = jnp.transpose(kc[rows, :])
        vs[h, :HD] = v[rows, :]
        vcs[h, :HD] = vc[rows, :]
        vs[h, HD:] = ones
        vcs[h, HD:] = ones
    lift = bounds[4, 0]

    lead = jnp.ones((8, HD), BF)
    top = lambda ref, rows: jnp.max(dot(lead, ref[rows, :] * ref[rows, :]))
    limit = jnp.float32(0.9 * (96.0 / scale) ** 2)
    small = None
    for h in range(group):
        rows = slice(h * HD, (h + 1) * HD)
        fits = top(q, rows) * jnp.maximum(top(k, rows), top(kc, rows)) < limit
        small = fits if small is None else jnp.logical_and(small, fits)

    def key_ids(keys):
        col = id_col[keys, :]
        return jnp.concatenate([col] * (TQ // 128), 1)

    def sweep(i, q_ids, update, state):
        def band(j, state):
            keys = pl.ds(pl.multiple_of(j * FK, FK), FK)
            return update(state, ks, vs, keys, key_ids(keys) == q_ids)

        def full(j, state):
            keys = pl.ds(pl.multiple_of(j * FK, FK), FK)
            return update(state, kcs, vcs, keys, None)

        def edge(j, state):
            keys = pl.ds(pl.multiple_of(j * FK, FK), FK)
            return update(state, kcs, vcs, keys, key_ids(keys) < q_ids + lift)

        state = lax.fori_loop(bounds[2, i], bounds[3, i], band, state)
        state = lax.fori_loop(0, bounds[0, i], full, state)
        return lax.fori_loop(bounds[0, i], bounds[1, i], edge, state)

    def store(h, at, acc, log_shift):
        total_w = acc[HD : HD + 1, :]
        o_out[h * HD : (h + 1) * HD, at] = (acc[:HD, :] / total_w).astype(BF)
        lse_out[h, :, at] = jnp.broadcast_to(log_shift + jnp.log2(total_w), (8, TQ))

    def plain_tile(i, _):
        at = pl.ds(pl.multiple_of(i * TQ, TQ), TQ)
        queries = [q[h * HD : (h + 1) * HD, at] for h in range(group)]

        def update(state, key_ref, val_ref, keys, mask):
            out = []
            for h in range(group):
                p = jnp.exp2(dot(key_ref[h, keys, :], queries[h]) * scale)
                if mask is not None:
                    p = jnp.where(mask, p, 0.0)
                out.append(state[h] + dot(val_ref[h, :, keys], p.astype(BF)))
            return tuple(out)

        state = (jnp.zeros((HD + 16, TQ), F32),) * group
        state = sweep(i, id_row[0:1, at], update, state)
        for h in range(group):
            store(h, at, state[h], 0.0)
        return 0

    def shifted_tile(i, _):
        at = pl.ds(pl.multiple_of(i * TQ, TQ), TQ)
        q_ids = id_row[0:1, at]
        for h in range(group):
            query = q[h * HD : (h + 1) * HD, at]

            def update(state, key_ref, val_ref, keys, mask):
                m, acc = state
                s = dot(key_ref[h, keys, :], query)
                if mask is not None:
                    s = jnp.where(mask, s, NEG)
                m_new = jnp.maximum(m, jnp.max(s, 0, keepdims=True))
                p = jnp.exp2((s - m_new) * scale).astype(BF)
                alpha = jnp.exp2((m - m_new) * scale)
                return m_new, acc * alpha + dot(val_ref[h, :, keys], p)

            state = (jnp.full((1, TQ), NEG, F32), jnp.zeros((HD + 16, TQ), F32))
            m, acc = sweep(i, q_ids, update, state)
            store(h, at, acc, m * scale)
        return 0

    @pl.when(small)
    def _():
        lax.fori_loop(0, total // TQ, plain_tile, 0)

    @pl.when(jnp.logical_not(small))
    def _():
        lax.fori_loop(0, total // TQ, shifted_tile, 0)


def attend(bounds, q, k, v, kc, vc, id_row, id_col, heads, group):
    total = q.shape[1]
    head = pl.BlockSpec((group * HD, total), lambda g, b: (g, 0))
    whole = lambda shape: pl.BlockSpec(shape, lambda g, b: (0, 0))
    return pl.pallas_call(
        functools.partial(attend_kernel, group),
        grid_spec=pltpu.PrefetchScalarGridSpec(
            num_scalar_prefetch=1,
            grid=(heads // group,),
            in_specs=[head] * 5 + [whole(id_row.shape), whole(id_col.shape)],
            out_specs=[head, pl.BlockSpec((group, 8, total), lambda g, b: (g, 0, 0))],
            scratch_shapes=[pltpu.VMEM((group, total, HD), BF)] * 2
            + [pltpu.VMEM((group, HD + 16, total), BF)] * 2,
        ),
        out_shape=[
            jax.ShapeDtypeStruct((heads * HD, total), BF),
            jax.ShapeDtypeStruct((heads, 8, total), F32),
        ],
        cost_estimate=pl.CostEstimate(
            flops=16 * heads * HD * total * total, bytes_accessed=2**24, transcendentals=0
        ),
        name="attend",
    )(bounds, q, k, v, kc, vc, id_row, id_col)


def attend_back_kernel(group, bounds, q, k, v, kc, vc, o, lse, do_mine, do_other, id_row, id_col,
                       cos_ref, sin_ref, own_out, cln_out, ks, vs, kcs, vcs, qs, dos, dot_s,
                       dk_acc, dv_acc, dkc_acc, dvc_acc, dq_acc):
    total = q.shape[1]
    half_rows = total // 2
    scale = LOG2E * HD**-0.5
    lift = bounds[4, 0]
    core = bounds[4, 1]
    near = pl.ds(pl.multiple_of(core * half_rows, 128), half_rows)
    far = pl.ds(pl.multiple_of((1 - core) * half_rows, 128), half_rows)
    dot_s[:, near] = do_mine[...]
    dot_s[:, far] = do_other[...]
    for h in range(group):
        rows = slice(h * HD, (h + 1) * HD)
        ks[h] = jnp.transpose(k[rows, :])
        vs[h] = jnp.transpose(v[rows, :])
        kcs[h] = jnp.transpose(kc[rows, :])
        vcs[h] = jnp.transpose(vc[rows, :])
        qs[h] = jnp.transpose(q[rows, :])
        dos[h] = jnp.transpose(dot_s[rows, :])
    for ref in (dk_acc, dv_acc, dkc_acc, dvc_acc):
        ref[...] = jnp.zeros_like(ref)

    def one_tile(i, _):
        at = pl.ds(pl.multiple_of(i * TQ, TQ), TQ)
        q_ids = id_row[0:1, at]
        queries, grads, deltas, sums, q_rows, g_rows = [], [], [], [], [], []
        for h in range(group):
            rows = slice(h * HD, (h + 1) * HD)
            queries.append(q[rows, at])
            g = dot_s[rows, at]
            grads.append(g)
            deltas.append(jnp.sum(g.astype(F32) * o[rows, at].astype(F32), 0, keepdims=True))
            sums.append(lse[h, 0:1, at])
            q_rows.append(qs[h, at, :])
            g_rows.append(dos[h, at, :])

        def update(state, key_ref, val_ref, key_cols, dk, dv, keys, mask):
            out = []
            for h in range(group):
                s = dot(key_ref[h, keys, :], queries[h])
                p = jnp.exp2(s * scale - sums[h])
                if mask is not None:
                    p = jnp.where(mask, p, 0.0)
                dp = dot(val_ref[h, keys, :], grads[h])
                ds = (p * (dp - deltas[h])).astype(BF)
                dv[h, keys, :] += dot(p.astype(BF), g_rows[h])
                dk[h, keys, :] += dot(ds, q_rows[h])
                out.append(state[h] + dot(key_cols[h * HD : (h + 1) * HD, keys], ds))
            return tuple(out)

        def key_ids(keys):
            col = id_col[keys, :]
            return jnp.concatenate([col] * (TQ // 128), 1)

        def band(j, state):
            keys = pl.ds(pl.multiple_of(j * TM, TM), TM)
            return update(state, ks, vs, k, dk_acc, dv_acc, keys, key_ids(keys) == q_ids)

        def full(j, state):
            keys = pl.ds(pl.multiple_of(j * TK, TK), TK)
            return update(state, kcs, vcs, kc, dkc_acc, dvc_acc, keys, None)

        def edge(j, state):
            keys = pl.ds(pl.multiple_of(j * TM, TM), TM)
            mask = key_ids(keys) < q_ids + lift
            return update(state, kcs, vcs, kc, dkc_acc, dvc_acc, keys, mask)

        state = (jnp.zeros((HD, TQ), F32),) * group
        state = lax.fori_loop(bounds[2, i], bounds[3, i], band, state)
        state = lax.fori_loop(0, bounds[0, i], full, state)
        state = lax.fori_loop(bounds[0, i] * (TK // TM), bounds[1, i], edge, state)
        for h in range(group):
            dq_acc[h * HD : (h + 1) * HD, at] = state[h]
        return 0

    lax.fori_loop(0, total // TQ, one_tile, 0)

    half = HD // 2
    cos_t, sin_t = cos_ref[...], sin_ref[...]
    noisy = lift == 0

    def spread(out, value, base):
        rows = slice(base, base + value.shape[0])
        out[rows, near] = value[:, :half_rows].astype(BF)
        out[rows, far] = value[:, half_rows:].astype(BF)

    def back_turn(out, w, base):
        first, second = w[:half, :], w[half:, :]
        spread(out, first * cos_t + second * sin_t, base)
        spread(out, second * cos_t - first * sin_t, base + half)

    for h in range(group):
        back_turn(own_out, dq_acc[h * HD : (h + 1) * HD, :] * HD**-0.5, 3 * h * HD)
        band_k = jnp.where(noisy, dk_acc[h], dkc_acc[h])
        band_v = jnp.where(noisy, dv_acc[h], dvc_acc[h])
        back_turn(own_out, jnp.transpose(band_k) * HD**-0.5, (3 * h + 1) * HD)
        spread(own_out, jnp.transpose(band_v), (3 * h + 2) * HD)
        back_turn(cln_out, jnp.transpose(dkc_acc[h]) * HD**-0.5, 2 * h * HD)
        spread(cln_out, jnp.transpose(dvc_acc[h]), (2 * h + 1) * HD)


def attend_back(bounds, q, k, v, kc, vc, o, lse, do_mine, do_other, id_row, id_col, cos_t, sin_t,
                pair, group):
    total = q.shape[1]
    head = pl.BlockSpec((group * HD, total), lambda g, b: (pair, 0))
    halfhead = pl.BlockSpec((group * HD, total // 2), lambda g, b: (pair, 0))
    whole = lambda shape: pl.BlockSpec(shape, lambda g, b: (0, 0))
    rows16 = pltpu.VMEM((group, total, HD), BF)
    rows32 = pltpu.VMEM((group, total, HD), F32)
    outs = [(group * 3 * HD, total), (group * 2 * HD, total)]
    return pl.pallas_call(
        functools.partial(attend_back_kernel, group),
        grid_spec=pltpu.PrefetchScalarGridSpec(
            num_scalar_prefetch=1,
            grid=(1,),
            in_specs=[head] * 6
            + [pl.BlockSpec((group, 8, total), lambda g, b: (pair, 0, 0)), halfhead, halfhead]
            + [whole(id_row.shape), whole(id_col.shape), whole(cos_t.shape), whole(sin_t.shape)],
            out_specs=[whole(shape) for shape in outs],
            scratch_shapes=[rows16] * 6
            + [pltpu.VMEM((group * HD, total), BF)]
            + [rows32] * 4
            + [pltpu.VMEM((group * HD, total), F32)],
        ),
        out_shape=[jax.ShapeDtypeStruct(shape, BF) for shape in outs],
        cost_estimate=pl.CostEstimate(
            flops=20 * group * HD * total * total, bytes_accessed=8 * 2**20, transcendentals=0
        ),
        name="attend_back",
    )(bounds, q, k, v, kc, vc, o, lse, do_mine, do_other, id_row, id_col, cos_t, sin_t)


def finish_kernel(n, g, s, g_out, s_out, s_in, g_x, s_x, g_c, s_c, g_t, s_t, s_send, s_recv,
                  x_send, x_recv, c_send, c_recv, local):
    me = lax.axis_index("fsdp")
    seat = lax.axis_index("seq")
    core = lax.rem(seat, 2)
    across = {"seq": lax.rem(seat + 2, 4)}
    beside = {"seq": seat + 1 - 2 * core}
    mesh_id = pl.DeviceIdType.MESH
    barrier = pltpu.get_barrier_semaphore()
    peers = [{"fsdp": lax.rem(me + d, n)} for d in range(1, n)]
    for where in peers + [across, beside]:
        pl.semaphore_signal(barrier, inc=1, device_id=where, device_id_type=mesh_id)
    pl.semaphore_wait(barrier, n + 1)

    def push(src, dst, one, two, where):
        copy = pltpu.make_async_remote_copy(
            src_ref=src, dst_ref=dst, send_sem=one, recv_sem=two, device_id=where,
            device_id_type=mesh_id,
        )
        copy.start()
        return copy

    def settle(tmp, out, sem):
        copy = pltpu.make_async_copy(tmp, out, sem)
        copy.start()
        copy.wait()

    first = [
        push(s.at[lax.rem(me + d, n)], s_in.at[d - 1], s_send.at[d - 1], s_recv.at[d - 1],
             peers[d - 1])
        for d in range(1, n)
    ]
    far_g = push(g, g_x, x_send.at[0], x_recv.at[0], across)
    for copy in first:
        copy.wait()
    total = s[me]
    for d in range(n - 1):
        total = total + s_in[d]
    s_t[0] = total
    settle(s_t.at[0], s_x.at[0], local.at[0])
    far_s = push(s_x.at[0], s_x.at[1], x_send.at[1], x_recv.at[1], across)
    far_g.wait()
    g_t[...] = (g[...].astype(F32) + g_x[...].astype(F32)).astype(BF)
    settle(g_t, g_c.at[core], local.at[1])
    near_g = push(g_c.at[core], g_c.at[core], c_send.at[0], c_recv.at[0], beside)
    far_s.wait()
    s_t[1] = s_x[0] + s_x[1]
    settle(s_t.at[1], s_c.at[0], local.at[2])
    near_s = push(s_c.at[0], s_c.at[1], c_send.at[1], c_recv.at[1], beside)
    near_g.wait()
    span = g.shape[1]
    for c in range(2):
        g_out[:, c * span : (c + 1) * span] = g_c[c].astype(F32)
    near_s.wait()
    s_out[...] = s_c[0] + s_c[1]


def finish(g, s):
    n = s.shape[0]
    vm = pl.BlockSpec(memory_space=pltpu.VMEM)
    dma = pltpu.SemaphoreType.DMA
    return pl.pallas_call(
        functools.partial(finish_kernel, n),
        in_specs=[vm] * 2,
        out_specs=[vm] * 2,
        out_shape=[
            jax.ShapeDtypeStruct((g.shape[0], 2 * g.shape[1]), F32),
            jax.ShapeDtypeStruct(s.shape[1:], F32),
        ],
        scratch_shapes=[
            pltpu.VMEM((n - 1,) + s.shape[1:], F32),
            pltpu.VMEM(g.shape, BF),
            pltpu.VMEM((2,) + s.shape[1:], F32),
            pltpu.VMEM((2,) + g.shape, BF),
            pltpu.VMEM((2,) + s.shape[1:], F32),
            pltpu.VMEM(g.shape, BF),
            pltpu.VMEM((2,) + s.shape[1:], F32),
            dma((n - 1,)),
            dma((n - 1,)),
            dma((2,)),
            dma((2,)),
            dma((2,)),
            dma((2,)),
            dma((3,)),
        ],
        compiler_params=pltpu.CompilerParams(collective_id=1, has_side_effects=True),
        name="finish",
    )(g, s)


def assemble_kernel(span, inner, core_ref, mine, other, d_mine, d_other, out_ref, up_ref, down_ref):
    first_core = core_ref[0] == 0
    pick = lambda one, two: (
        jnp.where(first_core, one, two).astype(F32), jnp.where(first_core, two, one).astype(F32)
    )
    first, second = pick(mine[...].astype(F32), other[...].astype(F32))
    out_ref[:, :span] = first[:, :span]
    out_ref[:, span:] = second[:, :span]
    for i in range((first.shape[1] - span) // inner):
        cols = slice(span + i * inner, span + (i + 1) * inner)
        up_ref[:, 2 * i * inner : 2 * (i + 1) * inner] = jnp.concatenate(
            [first[:, cols], second[:, cols]], 1
        )
    first, second = pick(d_mine[...].astype(F32), d_other[...].astype(F32))
    down_ref[: first.shape[0], :] = first
    down_ref[first.shape[0] :, :] = second


def assemble(core, mine, other, d_mine, d_other, span, inner):
    rows, width = mine.shape
    vm = pl.BlockSpec(memory_space=pltpu.VMEM)
    return pl.pallas_call(
        functools.partial(assemble_kernel, span, inner),
        in_specs=[pl.BlockSpec(memory_space=pltpu.SMEM)] + [vm] * 4,
        out_specs=[vm] * 3,
        out_shape=[
            jax.ShapeDtypeStruct((rows, 2 * span), F32),
            jax.ShapeDtypeStruct((rows, 2 * (width - span)), F32),
            jax.ShapeDtypeStruct((2 * d_mine.shape[0], d_mine.shape[1]), F32),
        ],
        name="assemble",
    )(core, mine, other, d_mine, d_other)


def on_device(
    tokens,
    block_ids,
    ln1_scale,
    ln1_bias,
    qkv_weight,
    qkv_bias,
    out_weight,
    out_bias,
    ln2_scale,
    ln2_bias,
    up_weight,
    up_bias,
    down_weight,
    down_bias,
    cotangent,
):
    tok = tokens[0]
    local_rows, width = tok.shape
    ids = block_ids[0].astype(jnp.int32)
    length = ids.shape[0]
    shard = ln1_scale.shape[0]
    heads = H // 2
    span = heads * HD
    me = lax.axis_index("seq")
    core = me % 2
    noisy = me < 2
    swap = [(0, 1), (1, 0), (2, 3), (3, 2)]
    other = lax.ppermute(tok, "seq", swap)
    clean_in = lax.ppermute(tok, "seq", [(2, 0), (3, 1)])
    cot_far = lax.ppermute(cotangent[0], "seq", swap)

    q_cols = lax.dynamic_slice_in_dim(qkv_weight, core * 3 * span, 3 * span, 1)
    small = jnp.concatenate(
        [
            ln1_scale.reshape(1, shard),
            ln1_bias.reshape(1, shard),
            out_bias.reshape(1, shard),
            ln2_scale.reshape(1, shard),
            ln2_bias.reshape(1, shard),
            down_bias.reshape(1, shard),
            qkv_bias.reshape(-1, shard),
            up_bias.reshape(-1, shard),
        ],
        0,
    )
    n_small = small.shape[0]
    small = jnp.pad(small, ((0, 128 - n_small), (0, 0))).T
    gathered = lax.all_gather(
        jnp.concatenate([q_cols, small], 1), "fsdp", axis=0, tiled=True
    )
    n_fsdp = width // shard
    vectors = gathered[:, 3 * span :].reshape(n_fsdp, shard, 128)[:, :, :n_small]
    vectors = jnp.transpose(vectors, (2, 0, 1)).astype(F32)
    flat = vectors[:6].reshape(6, width)
    qkv_b = jnp.transpose(vectors[6:9], (1, 0, 2)).reshape(-1)
    scale_one, shift_one, out_shift, scale_two, shift_two, down_shift = [flat[i] for i in range(6)]

    inner = up_bias.shape[0] // 2
    up_b = jnp.transpose(vectors[9:], (1, 0, 2)).reshape(n_fsdp, 2, inner)
    up_b = lax.dynamic_index_in_dim(up_b, core, 1, False).reshape(-1)
    up_cols = lax.dynamic_index_in_dim(
        up_weight.reshape(shard, n_fsdp, 2, inner), core, 2, False
    ).reshape(shard, n_fsdp * inner)
    down_rows = lax.dynamic_slice_in_dim(down_weight, core * inner, inner, 0)
    out_cols = lax.dynamic_slice_in_dim(out_weight, core * span, span, 1)
    out_up = lax.all_gather(
        jnp.concatenate([out_cols, up_cols], 1), "fsdp", axis=0, tiled=True
    )
    down_own = lax.all_gather(down_rows, "fsdp", axis=0, tiled=True)
    in_order = lambda near, far, axis: jnp.where(
        core == 0, jnp.concatenate([near, far], axis), jnp.concatenate([far, near], axis)
    )

    frequency = jnp.exp(-jnp.log(10000.0) * jnp.arange(HD // 2, dtype=F32) / (HD // 2))
    angles = frequency[:, None] * jnp.arange(length, dtype=F32)[None, :]
    cos_t, sin_t = jnp.cos(angles), jnp.sin(angles)

    first = ids[::TQ][:, None]
    last = ids[TQ - 1 :: TQ][:, None]
    before = lambda edge: jnp.sum((ids[None, :] < edge).astype(jnp.int32), 1)
    start_first, end_first = before(first), before(first + 1)
    start_last, end_last = before(last), before(last + 1)
    lift = jnp.where(noisy, 0, 1)
    zero = jnp.zeros_like(start_first)

    def key_bounds(full, masked):
        ceil_m = lambda value: (value + masked - 1) // masked
        return jnp.stack(
            [
                jnp.where(noisy, start_first, end_first) // full,
                ceil_m(jnp.where(noisy, start_last, end_last)),
                jnp.where(noisy, start_first // masked, zero),
                jnp.where(noisy, ceil_m(end_last), zero),
                zero + jnp.where(jnp.arange(zero.shape[0]) == 0, lift, core),
            ]
        ).astype(jnp.int32)

    bounds, wide_bounds = key_bounds(TK, TM), key_bounds(FK, FK)
    id_row = jnp.broadcast_to(ids[None, :], (8, length))
    id_col = jnp.broadcast_to(ids[:, None], (length, 128))

    cot_both = jnp.concatenate([cotangent[0], cot_far], 0)
    clean_in, cot_both, cos_t, sin_t, bounds, wide_bounds, id_row, id_col = (
        lax.optimization_barrier(
            (clean_in, cot_both, cos_t, sin_t, bounds, wide_bounds, id_row, id_col)
        )
    )
    clean_far = lax.ppermute(clean_in, "seq", swap)

    vec = jnp.concatenate([scale_one[None], shift_one[None], jnp.zeros((6, width), F32)], 0)
    bias_own = lax.dynamic_slice_in_dim(qkv_b, core * 3 * span, 3 * span, 0)
    bias_own = jnp.transpose(bias_own.reshape(heads, 3, HD), (1, 0, 2)).reshape(3 * span, 1)
    q, k, v, kc, vc, a_own = project(
        jnp.stack([core, noisy.astype(core.dtype)]), tok, other, clean_in, clean_far, gathered, vec,
        bias_own, cos_t, sin_t, heads
    )
    o, lse = attend(wide_bounds, q, k, v, kc, vc, id_row, id_col, heads, 1)
    o, lse, out_up = lax.optimization_barrier((o, lse, out_up))
    out_near, up_own = out_up[:, :span], out_up[:, span:]
    out_full = in_order(out_near, lax.ppermute(out_near, "seq", swap), 1)
    cut = lambda value, which: lax.dynamic_slice_in_dim(value, which * local_rows, local_rows, 1)
    o_mine = cut(o, core)
    o_in = lax.ppermute(cut(o, 1 - core), "seq", swap)
    attended = in_order(o_mine, o_in, 0)

    rows_in = tok.astype(F32)
    hidden = rows_in + rows_contract(attended, out_full) + out_shift
    normed_two, inverse_two = normalize_parts(hidden)
    second_in = (normed_two * scale_two + shift_two).astype(BF)
    second_in, down_own = lax.optimization_barrier((second_in, down_own))
    both_in = jnp.concatenate([second_in, lax.ppermute(second_in, "seq", swap)], 0)

    def join(product, rows):
        far = product(rows[local_rows:]).astype(BF)
        return product(rows[:local_rows]) + lax.ppermute(far, "seq", swap).astype(F32)

    pre_act = dot(both_in, up_own) + up_b
    root = (2 / math.pi) ** 0.5
    square = pre_act * pre_act
    bend = jnp.tanh(pre_act * (root + 0.044715 * root * square))
    rise = 0.5 + 0.5 * bend
    act_low = (pre_act * rise).astype(BF)
    curve = pre_act * (1 - bend * bend) * (0.5 * root + 1.5 * 0.044715 * root * square)
    slope = (rise + curve).astype(BF)
    grad_down_w = rows_contract(act_low, cot_both).astype(BF)
    scatter = lambda grad: lax.psum_scatter(grad, "fsdp", scatter_dimension=0, tiled=True)
    act_low, slope, grad_down_w, cot_both = lax.optimization_barrier(
        (act_low, slope, grad_down_w, cot_both)
    )
    down_part = scatter(grad_down_w)
    result = hidden + join(lambda rows: dot(rows, down_own), act_low) + down_shift

    grad_top = cotangent[0].astype(F32)
    grad_down_b = jnp.sum(grad_top, 0)
    grad_pre = (right_transposed(cot_both, down_own) * slope.astype(F32)).astype(BF)
    grad_second = join(lambda rows: right_transposed(rows, up_own), grad_pre)
    grad_up_b = jnp.sum(grad_pre.astype(F32), 0)
    grad_up_w = rows_contract(both_in, grad_pre).astype(BF)
    grad_scale_two = jnp.sum(grad_second * normed_two, 0)
    grad_shift_two = jnp.sum(grad_second, 0)
    grad_hidden = grad_top + norm_backward(grad_second, normed_two, inverse_two, scale_two)

    grad_attn = grad_hidden.astype(BF)
    grad_out_w = dot(attended, grad_attn).astype(BF)
    grad_out_b = jnp.sum(grad_attn.astype(F32), 0)
    grad_o = right_transposed(out_full, grad_attn).astype(BF)
    cut_heads = lambda which: lax.dynamic_slice_in_dim(grad_o, which * span, span, 0)
    do_mine = cut_heads(core)
    do_in = lax.ppermute(cut_heads(1 - core), "seq", swap)
    cut_cols = lambda which: lax.dynamic_slice_in_dim(grad_out_w, which * span, span, 1)
    out_sum = (
        cut_cols(core).astype(F32) + lax.ppermute(cut_cols(1 - core), "seq", swap).astype(F32)
    ).astype(BF)
    do_mine, do_in, grad_up_w, out_sum = lax.optimization_barrier(
        (do_mine, do_in, grad_up_w, out_sum)
    )
    out_up_part = scatter(jnp.concatenate([out_sum, grad_up_w], 1))

    back_args = lambda mine: (
        bounds, q, k, v, kc, vc, o, lse, mine, do_in, id_row, id_col, cos_t, sin_t
    )
    hold = lax.optimization_barrier
    cross = [(0, 2), (1, 3), (2, 0), (3, 1)]
    to_clean = lambda send: lax.ppermute(send, "seq", [(0, 2), (1, 3)])
    pair_w = 2 * 3 * HD

    def joined(own, got):
        own = own.reshape(2, 3, HD, -1)
        key_value = own[:, 1:].astype(F32) + got.reshape(2, 2, HD, -1).astype(F32)
        return jnp.concatenate([own[:, :1], key_value.astype(BF)], 1).reshape(pair_w, -1)

    def weight_grad(own):
        return lax.dot_general(
            a_own, own, (((0,), (1,)), ((), ())), preferred_element_type=F32
        ).astype(BF)

    def back(own, first, count):
        cols = gathered[:, first * pair_w : (first + count) * pair_w]
        return lax.dot_general(
            own, cols, (((0,), (1,)), ((), ())), preferred_element_type=F32
        )

    own_0, send_0 = attend_back(*back_args(do_mine), 0, 2)
    send_0, do_mine = hold((send_0, do_mine))
    got_0 = to_clean(send_0)
    own_1, send_1 = attend_back(*back_args(do_mine), 1, 2)
    own_1, send_1, got_0, down_part = hold((own_1, send_1, got_0, down_part))
    got_1, down_far = to_clean(send_1), lax.ppermute(down_part, "seq", cross)
    own_0 = joined(own_0, got_0)
    grad_0, do_mine = hold((weight_grad(own_0), do_mine))
    own_2, send_2 = attend_back(*back_args(do_mine), 2, 2)
    own_2, send_2, got_1, down_far, out_up_part = hold(
        (own_2, send_2, got_1, down_far, out_up_part)
    )
    got_2 = to_clean(send_2)
    own_1 = joined(own_1, got_1)
    grad_01, own_1 = hold((jnp.concatenate([grad_0, weight_grad(own_1)], 1), own_1))
    exchange = lambda grad: lax.all_to_all(
        grad.reshape(n_fsdp, shard, grad.shape[1]), "fsdp", 0, 0
    )
    piece_sum = lambda pieces: functools.reduce(
        jnp.add, [pieces[d].astype(F32) for d in range(n_fsdp)]
    ).astype(BF)
    pieces_01 = exchange(grad_01)
    own_01 = jnp.concatenate([own_0, own_1], 0)
    first_01 = back(own_01, 0, 2)
    got_2, out_up_part, first_01 = hold((got_2, out_up_part, first_01))
    own_2 = joined(own_2, got_2)
    far_rows = (first_01[local_rows:] + back(own_2[:, local_rows:], 2, 1)).astype(BF)
    grad_2, far_rows, pieces_01 = hold((weight_grad(own_2), far_rows, pieces_01))
    pieces_2 = exchange(grad_2)
    got_rows = lax.ppermute(far_rows, "seq", swap).astype(F32)
    grad_first = first_01[:local_rows] + back(own_2[:, :local_rows], 2, 1) + got_rows

    def chip_sum(part, far):
        total = (part.astype(F32) + far.astype(F32)).astype(BF)
        return total, lax.ppermute(total, "seq", swap)

    out_up_both = chip_sum(out_up_part, lax.ppermute(out_up_part, "seq", cross))
    out_g, up_g, down_g = assemble(
        core.reshape(1).astype(jnp.int32), *out_up_both, *chip_sum(down_part, down_far), span, inner
    )

    sum_cols = lambda own: jnp.sum(own.astype(F32), 1)
    grad_qkv_b = jnp.concatenate([sum_cols(own_01), sum_cols(own_2)])
    normed_one, inverse_one = normalize_parts(rows_in)
    grad_scale_one = jnp.sum(grad_first * normed_one, 0)
    grad_shift_one = jnp.sum(grad_first, 0)
    grad_rows = grad_hidden + norm_backward(grad_first, normed_one, inverse_one, scale_one)

    qkv_b_wide = lax.dynamic_update_slice_in_dim(
        jnp.zeros((2 * 3 * span,), F32), grad_qkv_b, core * 3 * span, 0
    )
    up_b_wide = lax.dynamic_update_slice_in_dim(
        jnp.zeros((n_fsdp, 2, inner), F32), grad_up_b.reshape(n_fsdp, 1, inner), core, 1
    )
    pieces = [
        piece.reshape(n_fsdp, -1)
        for piece in (
            grad_scale_one, grad_shift_one, qkv_b_wide, grad_out_b, grad_scale_two,
            grad_shift_two, up_b_wide, grad_down_b,
        )
    ]
    sizes = [piece.shape[1] for piece in pieces]
    packed = jnp.concatenate(pieces, 1)
    lines = -(-packed.shape[1] // 128)
    packed = jnp.pad(packed, ((0, 0), (0, lines * 128 - packed.shape[1])))
    packed = packed.reshape(n_fsdp, lines, 128)
    part_01 = piece_sum(pieces_01)
    grad_rows, out_g, up_g, down_g, packed, part_01, pieces_2 = hold(
        (grad_rows, out_g, up_g, down_g, packed, part_01, pieces_2)
    )
    qkv_part = jnp.concatenate([part_01, piece_sum(pieces_2)], 1)
    qkv_g, small_sum = finish(qkv_part, packed)
    small_sum = small_sum.reshape(-1)
    small_out, at = [], 0
    for size in sizes:
        small_out.append(small_sum[at : at + size])
        at += size
    return (
        result.astype(BF)[None],
        grad_rows[None],
        small_out[0],
        small_out[1],
        qkv_g,
        small_out[2],
        out_g,
        small_out[3],
        small_out[4],
        small_out[5],
        up_g,
        small_out[6],
        down_g,
        small_out[7],
    )


def solution(mesh):
    row, mat, vec = P("fsdp", "seq", None), P("fsdp", None), P("fsdp")
    in_specs = (row, mat, vec, vec, mat, vec, mat, vec, vec, vec, mat, vec, mat, vec, row)
    out_specs = (row, row, vec, vec, mat, vec, mat, vec, vec, vec, mat, vec, mat, vec)
    return jax.shard_map(
        on_device, mesh=mesh, in_specs=in_specs, out_specs=out_specs, check_vma=False
    )
```

```python
import functools
import math

import jax
import jax.numpy as jnp
from jax import lax
from jax.experimental import pallas as pl
from jax.experimental.pallas import tpu as pltpu
from jax.sharding import PartitionSpec as P

H = 12
HD = 64
EPSILON = 1e-05
LOG2E = 1.4426950408889634
NEG = -1e30
TQ = 512
TK = 256
TM = 256
FK = 1024
BF = jnp.bfloat16
F32 = jnp.float32


def normalize_parts(values):
    mean_value = jnp.mean(values, -1, keepdims=True)
    centred = values - mean_value
    variance = jnp.mean(centred * centred, -1, keepdims=True)
    inverse = lax.rsqrt(variance + EPSILON)
    return (centred * inverse, inverse)


def norm_backward(grad_out, normed, inverse, scale):
    grad_norm = grad_out * scale
    return inverse * (
        grad_norm
        - jnp.mean(grad_norm, -1, keepdims=True)
        - normed * jnp.mean(grad_norm * normed, -1, keepdims=True)
    )


def rows_contract(left, right):
    return lax.dot_general(left, right, (((0,), (0,)), ((), ())), preferred_element_type=F32)


def right_transposed(left, right):
    return lax.dot_general(left, right, (((1,), (1,)), ((), ())), preferred_element_type=F32)


def dot(left, right):
    return jnp.dot(left, right, preferred_element_type=F32)


def qkv_kernel(heads, core_ref, mine, other, mine_c, other_c, sent, sent_other, w_ref, vec_ref, bias_ref, cos_ref,
               sin_ref, q_out, k_out, v_out, kc_out, vc_out, a_out, wt):
    step = pl.program_id(0)
    span = heads * HD

    @pl.when(step == 0)
    def _():
        whole = jnp.transpose(w_ref[...])
        for h in range(heads):
            for part in range(3):
                wt[part * span + h * HD : part * span + (h + 1) * HD, :] = whole[
                    (3 * h + part) * HD : (3 * h + part + 1) * HD, :
                ]

    def normed(rows):
        values = rows.astype(F32)
        n, _ = normalize_parts(values)
        return (n * vec_ref[0:1, :] + vec_ref[1:2, :]).astype(BF)

    def turn(lin, base, out):
        cos_t, sin_t = cos_ref[...], sin_ref[...]
        half = HD // 2
        for h in range(heads):
            first = lin[base + h * HD : base + h * HD + half, :]
            second = lin[base + h * HD + half : base + (h + 1) * HD, :]
            out[h * HD : h * HD + half, :] = (first * cos_t - second * sin_t).astype(BF)
            out[h * HD + half : (h + 1) * HD, :] = (first * sin_t + second * cos_t).astype(BF)

    quarter = pl.num_programs(0) // 4

    @pl.when(step < 2 * quarter)
    def _():
        a = normed(jnp.where(step < quarter, mine[...], other[...]))
        a_out[...] = a
        lin = right_transposed(wt[...], a) + bias_ref[...]
        turn(lin, 0, q_out)
        turn(lin, span, k_out)
        v_out[...] = lin[2 * span :, :].astype(BF)

    @pl.when(step >= 2 * quarter)
    def _():
        here = jnp.where(step < 3 * quarter, mine_c[...], other_c[...])
        there = jnp.where(step < 3 * quarter, sent[...], sent_other[...])
        a = normed(jnp.where(core_ref[1] == 1, there, here))
        lin = right_transposed(wt[span:, :], a) + bias_ref[span:, :]
        turn(lin, 0, kc_out)
        vc_out[...] = lin[span:, :].astype(BF)


def project(core, mine, other, sent, sent_other, weight, vec, bias, cos_t, sin_t, heads):
    local, width = mine.shape
    span = heads * HD
    tile = 256
    n = local // tile

    def place(t, c):
        mine_first = jnp.where(t % (2 * n) < n, c[0], 1 - c[0])
        return mine_first * n + t % n

    def src(k):
        return pl.BlockSpec((tile, width), lambda t, c: (jnp.clip(t - k * n, 0, n - 1), 0))

    whole = lambda shape: pl.BlockSpec(shape, lambda t, c: (0, 0))
    own = pl.BlockSpec((span, tile), lambda t, c: (0, place(jnp.minimum(t, 2 * n - 1), c)))
    cln = pl.BlockSpec((span, tile), lambda t, c: (0, place(jnp.maximum(t, 2 * n), c)))
    own_a = pl.BlockSpec((tile, width), lambda t, c: (jnp.minimum(t, 2 * n - 1), 0))
    tab = pl.BlockSpec((HD // 2, tile), lambda t, c: (0, place(t, c)))
    head_shape = jax.ShapeDtypeStruct((span, 2 * local), BF)
    row_shape = jax.ShapeDtypeStruct((2 * local, width), BF)
    return pl.pallas_call(
        functools.partial(qkv_kernel, heads),
        grid_spec=pltpu.PrefetchScalarGridSpec(
            num_scalar_prefetch=1,
            grid=(4 * n,),
            in_specs=[src(0), src(1)] + [src(2), src(3)] * 2 + [whole((width, 3 * span)), whole(vec.shape),
                      whole(bias.shape), tab, tab],
            out_specs=[own, own, own, cln, cln, own_a],
            scratch_shapes=[pltpu.VMEM((3 * span, width), BF)],
        ),
        out_shape=[head_shape] * 5 + [row_shape],
        name="project",
    )(core, mine, other, mine, other, sent, sent_other, weight, vec, bias, cos_t, sin_t)


def attend_kernel(group, bounds, q, k, v, kc, vc, id_row, id_col, o_out, lse_out, ks, kcs, vs,
                  vcs):
    total = q.shape[1]
    scale = LOG2E * HD**-0.5
    ones = jnp.ones((16, total), BF)
    for h in range(group):
        rows = slice(h * HD, (h + 1) * HD)
        ks[h] = jnp.transpose(k[rows, :])
        kcs[h] = jnp.transpose(kc[rows, :])
        vs[h, :HD] = v[rows, :]
        vcs[h, :HD] = vc[rows, :]
        vs[h, HD:] = ones
        vcs[h, HD:] = ones
    lift = bounds[4, 0]

    lead = jnp.ones((8, HD), BF)
    top = lambda ref, rows: jnp.max(dot(lead, ref[rows, :] * ref[rows, :]))
    limit = jnp.float32(0.9 * (96.0 / scale) ** 2)
    small = None
    for h in range(group):
        rows = slice(h * HD, (h + 1) * HD)
        fits = top(q, rows) * jnp.maximum(top(k, rows), top(kc, rows)) < limit
        small = fits if small is None else jnp.logical_and(small, fits)

    def key_ids(keys):
        col = id_col[keys, :]
        return jnp.concatenate([col] * (TQ // 128), 1)

    def sweep(i, q_ids, update, state):
        def band(j, state):
            keys = pl.ds(pl.multiple_of(j * FK, FK), FK)
            return update(state, ks, vs, keys, key_ids(keys) == q_ids)

        def full(j, state):
            keys = pl.ds(pl.multiple_of(j * FK, FK), FK)
            return update(state, kcs, vcs, keys, None)

        def edge(j, state):
            keys = pl.ds(pl.multiple_of(j * FK, FK), FK)
            return update(state, kcs, vcs, keys, key_ids(keys) < q_ids + lift)

        state = lax.fori_loop(bounds[2, i], bounds[3, i], band, state)
        state = lax.fori_loop(0, bounds[0, i], full, state)
        return lax.fori_loop(bounds[0, i], bounds[1, i], edge, state)

    def store(h, at, acc, log_shift):
        total_w = acc[HD : HD + 1, :]
        o_out[h * HD : (h + 1) * HD, at] = (acc[:HD, :] / total_w).astype(BF)
        lse_out[h, :, at] = jnp.broadcast_to(log_shift + jnp.log2(total_w), (8, TQ))

    def plain_tile(i, _):
        at = pl.ds(pl.multiple_of(i * TQ, TQ), TQ)
        queries = [q[h * HD : (h + 1) * HD, at] for h in range(group)]

        def update(state, key_ref, val_ref, keys, mask):
            out = []
            for h in range(group):
                p = jnp.exp2(dot(key_ref[h, keys, :], queries[h]) * scale)
                if mask is not None:
                    p = jnp.where(mask, p, 0.0)
                out.append(state[h] + dot(val_ref[h, :, keys], p.astype(BF)))
            return tuple(out)

        state = (jnp.zeros((HD + 16, TQ), F32),) * group
        state = sweep(i, id_row[0:1, at], update, state)
        for h in range(group):
            store(h, at, state[h], 0.0)
        return 0

    def shifted_tile(i, _):
        at = pl.ds(pl.multiple_of(i * TQ, TQ), TQ)
        q_ids = id_row[0:1, at]
        for h in range(group):
            query = q[h * HD : (h + 1) * HD, at]

            def update(state, key_ref, val_ref, keys, mask):
                m, acc = state
                s = dot(key_ref[h, keys, :], query)
                if mask is not None:
                    s = jnp.where(mask, s, NEG)
                m_new = jnp.maximum(m, jnp.max(s, 0, keepdims=True))
                p = jnp.exp2((s - m_new) * scale).astype(BF)
                alpha = jnp.exp2((m - m_new) * scale)
                return m_new, acc * alpha + dot(val_ref[h, :, keys], p)

            state = (jnp.full((1, TQ), NEG, F32), jnp.zeros((HD + 16, TQ), F32))
            m, acc = sweep(i, q_ids, update, state)
            store(h, at, acc, m * scale)
        return 0

    @pl.when(small)
    def _():
        lax.fori_loop(0, total // TQ, plain_tile, 0)

    @pl.when(jnp.logical_not(small))
    def _():
        lax.fori_loop(0, total // TQ, shifted_tile, 0)


def attend(bounds, q, k, v, kc, vc, id_row, id_col, heads, group):
    total = q.shape[1]
    head = pl.BlockSpec((group * HD, total), lambda g, b: (g, 0))
    whole = lambda shape: pl.BlockSpec(shape, lambda g, b: (0, 0))
    return pl.pallas_call(
        functools.partial(attend_kernel, group),
        grid_spec=pltpu.PrefetchScalarGridSpec(
            num_scalar_prefetch=1,
            grid=(heads // group,),
            in_specs=[head] * 5 + [whole(id_row.shape), whole(id_col.shape)],
            out_specs=[head, pl.BlockSpec((group, 8, total), lambda g, b: (g, 0, 0))],
            scratch_shapes=[pltpu.VMEM((group, total, HD), BF)] * 2
            + [pltpu.VMEM((group, HD + 16, total), BF)] * 2,
        ),
        out_shape=[
            jax.ShapeDtypeStruct((heads * HD, total), BF),
            jax.ShapeDtypeStruct((heads, 8, total), F32),
        ],
        cost_estimate=pl.CostEstimate(
            flops=16 * heads * HD * total * total, bytes_accessed=2**24, transcendentals=0
        ),
        name="attend",
    )(bounds, q, k, v, kc, vc, id_row, id_col)


def attend_back_kernel(group, bounds, q, k, v, kc, vc, o, lse, do_mine, do_other, id_row, id_col,
                       cos_ref, sin_ref, own_out, cln_out, ks, vs, kcs, vcs, qs, dos, dot_s,
                       dk_acc, dv_acc, dkc_acc, dvc_acc, dq_acc):
    total = q.shape[1]
    half_rows = total // 2
    scale = LOG2E * HD**-0.5
    lift = bounds[4, 0]
    core = bounds[4, 1]
    near = pl.ds(pl.multiple_of(core * half_rows, 128), half_rows)
    far = pl.ds(pl.multiple_of((1 - core) * half_rows, 128), half_rows)
    dot_s[:, near] = do_mine[...]
    dot_s[:, far] = do_other[...]
    for h in range(group):
        rows = slice(h * HD, (h + 1) * HD)
        ks[h] = jnp.transpose(k[rows, :])
        vs[h] = jnp.transpose(v[rows, :])
        kcs[h] = jnp.transpose(kc[rows, :])
        vcs[h] = jnp.transpose(vc[rows, :])
        qs[h] = jnp.transpose(q[rows, :])
        dos[h] = jnp.transpose(dot_s[rows, :])
    for ref in (dk_acc, dv_acc, dkc_acc, dvc_acc):
        ref[...] = jnp.zeros_like(ref)

    def one_tile(i, _):
        at = pl.ds(pl.multiple_of(i * TQ, TQ), TQ)
        q_ids = id_row[0:1, at]
        queries, grads, deltas, sums, q_rows, g_rows = [], [], [], [], [], []
        for h in range(group):
            rows = slice(h * HD, (h + 1) * HD)
            queries.append(q[rows, at])
            g = dot_s[rows, at]
            grads.append(g)
            deltas.append(jnp.sum(g.astype(F32) * o[rows, at].astype(F32), 0, keepdims=True))
            sums.append(lse[h, 0:1, at])
            q_rows.append(qs[h, at, :])
            g_rows.append(dos[h, at, :])

        def update(state, key_ref, val_ref, key_cols, dk, dv, keys, mask):
            out = []
            for h in range(group):
                s = dot(key_ref[h, keys, :], queries[h])
                p = jnp.exp2(s * scale - sums[h])
                if mask is not None:
                    p = jnp.where(mask, p, 0.0)
                dp = dot(val_ref[h, keys, :], grads[h])
                ds = (p * (dp - deltas[h])).astype(BF)
                dv[h, keys, :] += dot(p.astype(BF), g_rows[h])
                dk[h, keys, :] += dot(ds, q_rows[h])
                out.append(state[h] + dot(key_cols[h * HD : (h + 1) * HD, keys], ds))
            return tuple(out)

        def key_ids(keys):
            col = id_col[keys, :]
            return jnp.concatenate([col] * (TQ // 128), 1)

        def band(j, state):
            keys = pl.ds(pl.multiple_of(j * TM, TM), TM)
            return update(state, ks, vs, k, dk_acc, dv_acc, keys, key_ids(keys) == q_ids)

        def full(j, state):
            keys = pl.ds(pl.multiple_of(j * TK, TK), TK)
            return update(state, kcs, vcs, kc, dkc_acc, dvc_acc, keys, None)

        def edge(j, state):
            keys = pl.ds(pl.multiple_of(j * TM, TM), TM)
            mask = key_ids(keys) < q_ids + lift
            return update(state, kcs, vcs, kc, dkc_acc, dvc_acc, keys, mask)

        state = (jnp.zeros((HD, TQ), F32),) * group
        state = lax.fori_loop(bounds[2, i], bounds[3, i], band, state)
        state = lax.fori_loop(0, bounds[0, i], full, state)
        state = lax.fori_loop(bounds[0, i] * (TK // TM), bounds[1, i], edge, state)
        for h in range(group):
            dq_acc[h * HD : (h + 1) * HD, at] = state[h]
        return 0

    lax.fori_loop(0, total // TQ, one_tile, 0)

    half = HD // 2
    cos_t, sin_t = cos_ref[...], sin_ref[...]
    noisy = lift == 0

    def spread(out, value, base):
        rows = slice(base, base + value.shape[0])
        out[rows, near] = value[:, :half_rows].astype(BF)
        out[rows, far] = value[:, half_rows:].astype(BF)

    def back_turn(out, w, base):
        first, second = w[:half, :], w[half:, :]
        spread(out, first * cos_t + second * sin_t, base)
        spread(out, second * cos_t - first * sin_t, base + half)

    for h in range(group):
        back_turn(own_out, dq_acc[h * HD : (h + 1) * HD, :] * HD**-0.5, 3 * h * HD)
        band_k = jnp.where(noisy, dk_acc[h], dkc_acc[h])
        band_v = jnp.where(noisy, dv_acc[h], dvc_acc[h])
        back_turn(own_out, jnp.transpose(band_k) * HD**-0.5, (3 * h + 1) * HD)
        spread(own_out, jnp.transpose(band_v), (3 * h + 2) * HD)
        back_turn(cln_out, jnp.transpose(dkc_acc[h]) * HD**-0.5, 2 * h * HD)
        spread(cln_out, jnp.transpose(dvc_acc[h]), (2 * h + 1) * HD)


def attend_back(bounds, q, k, v, kc, vc, o, lse, do_mine, do_other, id_row, id_col, cos_t, sin_t,
                pair, group):
    total = q.shape[1]
    head = pl.BlockSpec((group * HD, total), lambda g, b: (pair, 0))
    halfhead = pl.BlockSpec((group * HD, total // 2), lambda g, b: (pair, 0))
    whole = lambda shape: pl.BlockSpec(shape, lambda g, b: (0, 0))
    rows16 = pltpu.VMEM((group, total, HD), BF)
    rows32 = pltpu.VMEM((group, total, HD), F32)
    outs = [(group * 3 * HD, total), (group * 2 * HD, total)]
    return pl.pallas_call(
        functools.partial(attend_back_kernel, group),
        grid_spec=pltpu.PrefetchScalarGridSpec(
            num_scalar_prefetch=1,
            grid=(1,),
            in_specs=[head] * 6
            + [pl.BlockSpec((group, 8, total), lambda g, b: (pair, 0, 0)), halfhead, halfhead]
            + [whole(id_row.shape), whole(id_col.shape), whole(cos_t.shape), whole(sin_t.shape)],
            out_specs=[whole(shape) for shape in outs],
            scratch_shapes=[rows16] * 6
            + [pltpu.VMEM((group * HD, total), BF)]
            + [rows32] * 4
            + [pltpu.VMEM((group * HD, total), F32)],
        ),
        out_shape=[jax.ShapeDtypeStruct(shape, BF) for shape in outs],
        cost_estimate=pl.CostEstimate(
            flops=20 * group * HD * total * total, bytes_accessed=8 * 2**20, transcendentals=0
        ),
        name="attend_back",
    )(bounds, q, k, v, kc, vc, o, lse, do_mine, do_other, id_row, id_col, cos_t, sin_t)


def finish_kernel(n, g, s, g_out, s_out, s_in, g_x, s_x, g_c, s_c, g_t, s_t, s_send, s_recv,
                  x_send, x_recv, c_send, c_recv, local):
    me = lax.axis_index("fsdp")
    seat = lax.axis_index("seq")
    core = lax.rem(seat, 2)
    across = {"seq": lax.rem(seat + 2, 4)}
    beside = {"seq": seat + 1 - 2 * core}
    mesh_id = pl.DeviceIdType.MESH
    barrier = pltpu.get_barrier_semaphore()
    peers = [{"fsdp": lax.rem(me + d, n)} for d in range(1, n)]
    for where in peers + [across, beside]:
        pl.semaphore_signal(barrier, inc=1, device_id=where, device_id_type=mesh_id)
    pl.semaphore_wait(barrier, n + 1)

    def push(src, dst, one, two, where):
        copy = pltpu.make_async_remote_copy(
            src_ref=src, dst_ref=dst, send_sem=one, recv_sem=two, device_id=where,
            device_id_type=mesh_id,
        )
        copy.start()
        return copy

    def settle(tmp, out, sem):
        copy = pltpu.make_async_copy(tmp, out, sem)
        copy.start()
        copy.wait()

    first = [
        push(s.at[lax.rem(me + d, n)], s_in.at[d - 1], s_send.at[d - 1], s_recv.at[d - 1],
             peers[d - 1])
        for d in range(1, n)
    ]
    far_g = push(g, g_x, x_send.at[0], x_recv.at[0], across)
    for copy in first:
        copy.wait()
    total = s[me]
    for d in range(n - 1):
        total = total + s_in[d]
    s_t[0] = total
    settle(s_t.at[0], s_x.at[0], local.at[0])
    far_s = push(s_x.at[0], s_x.at[1], x_send.at[1], x_recv.at[1], across)
    far_g.wait()
    g_t[...] = (g[...].astype(F32) + g_x[...].astype(F32)).astype(BF)
    settle(g_t, g_c.at[core], local.at[1])
    near_g = push(g_c.at[core], g_c.at[core], c_send.at[0], c_recv.at[0], beside)
    far_s.wait()
    s_t[1] = s_x[0] + s_x[1]
    settle(s_t.at[1], s_c.at[0], local.at[2])
    near_s = push(s_c.at[0], s_c.at[1], c_send.at[1], c_recv.at[1], beside)
    near_g.wait()
    span = g.shape[1]
    for c in range(2):
        g_out[:, c * span : (c + 1) * span] = g_c[c].astype(F32)
    near_s.wait()
    s_out[...] = s_c[0] + s_c[1]


def finish(g, s):
    n = s.shape[0]
    vm = pl.BlockSpec(memory_space=pltpu.VMEM)
    dma = pltpu.SemaphoreType.DMA
    return pl.pallas_call(
        functools.partial(finish_kernel, n),
        in_specs=[vm] * 2,
        out_specs=[vm] * 2,
        out_shape=[
            jax.ShapeDtypeStruct((g.shape[0], 2 * g.shape[1]), F32),
            jax.ShapeDtypeStruct(s.shape[1:], F32),
        ],
        scratch_shapes=[
            pltpu.VMEM((n - 1,) + s.shape[1:], F32),
            pltpu.VMEM(g.shape, BF),
            pltpu.VMEM((2,) + s.shape[1:], F32),
            pltpu.VMEM((2,) + g.shape, BF),
            pltpu.VMEM((2,) + s.shape[1:], F32),
            pltpu.VMEM(g.shape, BF),
            pltpu.VMEM((2,) + s.shape[1:], F32),
            dma((n - 1,)),
            dma((n - 1,)),
            dma((2,)),
            dma((2,)),
            dma((2,)),
            dma((2,)),
            dma((3,)),
        ],
        compiler_params=pltpu.CompilerParams(collective_id=1, has_side_effects=True),
        name="finish",
    )(g, s)


def assemble_kernel(span, n, core_ref, mine, other, d_mine, d_other, out_ref, up_ref, down_ref):
    first_core = core_ref[0] == 0
    pick = lambda one, two: (
        jnp.where(first_core, one, two).astype(F32), jnp.where(first_core, two, one).astype(F32)
    )
    pair = pick(mine[...].astype(F32), other[...].astype(F32))
    rows = pair[0].shape[0]
    half = (pair[0].shape[1] - span) // (2 * n)
    for c in range(2):
        out_ref[:, c * span : (c + 1) * span] = pair[c][:, :span]
    for i in range(n):
        up_ref[:, 4 * i * half : 4 * (i + 1) * half] = jnp.concatenate(
            [
                part[:, span + (j * n + i) * half : span + (j * n + i + 1) * half]
                for part in pair
                for j in range(2)
            ],
            1,
        )
    pair = pick(d_mine[...].astype(F32), d_other[...].astype(F32))
    width = down_ref.shape[1]
    for c in range(2):
        for j in range(2):
            at = (2 * c + j) * rows
            down_ref[at : at + rows, :] = pair[c][:, j * width : (j + 1) * width]


def assemble(core, mine, other, d_mine, d_other, span, n):
    rows, width = mine.shape
    vm = pl.BlockSpec(memory_space=pltpu.VMEM)
    return pl.pallas_call(
        functools.partial(assemble_kernel, span, n),
        in_specs=[pl.BlockSpec(memory_space=pltpu.SMEM)] + [vm] * 4,
        out_specs=[vm] * 3,
        out_shape=[
            jax.ShapeDtypeStruct((rows, 2 * span), F32),
            jax.ShapeDtypeStruct((rows, 2 * (width - span)), F32),
            jax.ShapeDtypeStruct((4 * rows, d_mine.shape[1] // 2), F32),
        ],
        name="assemble",
    )(core, mine, other, d_mine, d_other)


def on_device(
    tokens,
    block_ids,
    ln1_scale,
    ln1_bias,
    qkv_weight,
    qkv_bias,
    out_weight,
    out_bias,
    ln2_scale,
    ln2_bias,
    up_weight,
    up_bias,
    down_weight,
    down_bias,
    cotangent,
):
    tok = tokens[0]
    local_rows, width = tok.shape
    ids = block_ids[0].astype(jnp.int32)
    length = ids.shape[0]
    shard = ln1_scale.shape[0]
    heads = H // 2
    span = heads * HD
    me = lax.axis_index("seq")
    core = me % 2
    noisy = me < 2
    swap = [(0, 1), (1, 0), (2, 3), (3, 2)]
    other = lax.ppermute(tok, "seq", swap)
    clean_in = lax.ppermute(tok, "seq", [(2, 0), (3, 1)])
    cot_far = lax.ppermute(cotangent[0], "seq", swap)

    q_cols = lax.dynamic_slice_in_dim(qkv_weight, core * 3 * span, 3 * span, 1)
    small = jnp.concatenate(
        [
            ln1_scale.reshape(1, shard),
            ln1_bias.reshape(1, shard),
            out_bias.reshape(1, shard),
            ln2_scale.reshape(1, shard),
            ln2_bias.reshape(1, shard),
            down_bias.reshape(1, shard),
            qkv_bias.reshape(-1, shard),
            up_bias.reshape(-1, shard),
        ],
        0,
    )
    n_small = small.shape[0]
    small = jnp.pad(small, ((0, 128 - n_small), (0, 0))).T
    gathered = lax.all_gather(
        jnp.concatenate([q_cols, small], 1), "fsdp", axis=0, tiled=True
    )
    n_fsdp = width // shard
    vectors = gathered[:, 3 * span :].reshape(n_fsdp, shard, 128)[:, :, :n_small]
    vectors = jnp.transpose(vectors, (2, 0, 1)).astype(F32)
    flat = vectors[:6].reshape(6, width)
    qkv_b = jnp.transpose(vectors[6:9], (1, 0, 2)).reshape(-1)
    scale_one, shift_one, out_shift, scale_two, shift_two, down_shift = [flat[i] for i in range(6)]

    inner = up_bias.shape[0] // 2
    up_b = jnp.transpose(vectors[9:], (1, 0, 2)).reshape(n_fsdp, 2, inner)
    by_half = lambda a: jnp.swapaxes(a.reshape(-1, n_fsdp, 2, inner // 2), 1, 2)
    up_b = by_half(lax.dynamic_index_in_dim(up_b, core, 1, False)).reshape(-1)
    up_cols = by_half(
        lax.dynamic_index_in_dim(up_weight.reshape(shard, n_fsdp, 2, inner), core, 2, False)
    ).reshape(shard, n_fsdp * inner)
    down_rows = lax.dynamic_slice_in_dim(down_weight, core * inner, inner, 0)
    beside = lambda a: jnp.concatenate([a[: a.shape[0] // 2], a[a.shape[0] // 2 :]], 1)
    out_cols = lax.dynamic_slice_in_dim(out_weight, core * span, span, 1)
    ffn = lax.all_gather(
        jnp.concatenate([out_cols, up_cols, beside(down_rows)], 1), "fsdp", axis=0, tiled=True
    )
    in_order = lambda near, far, axis: jnp.where(
        core == 0, jnp.concatenate([near, far], axis), jnp.concatenate([far, near], axis)
    )

    frequency = jnp.exp(-jnp.log(10000.0) * jnp.arange(HD // 2, dtype=F32) / (HD // 2))
    angles = frequency[:, None] * jnp.arange(length, dtype=F32)[None, :]
    cos_t, sin_t = jnp.cos(angles), jnp.sin(angles)

    first = ids[::TQ][:, None]
    last = ids[TQ - 1 :: TQ][:, None]
    before = lambda edge: jnp.sum((ids[None, :] < edge).astype(jnp.int32), 1)
    start_first, end_first = before(first), before(first + 1)
    start_last, end_last = before(last), before(last + 1)
    lift = jnp.where(noisy, 0, 1)
    zero = jnp.zeros_like(start_first)

    def key_bounds(full, masked):
        ceil_m = lambda value: (value + masked - 1) // masked
        return jnp.stack(
            [
                jnp.where(noisy, start_first, end_first) // full,
                ceil_m(jnp.where(noisy, start_last, end_last)),
                jnp.where(noisy, start_first // masked, zero),
                jnp.where(noisy, ceil_m(end_last), zero),
                zero + jnp.where(jnp.arange(zero.shape[0]) == 0, lift, core),
            ]
        ).astype(jnp.int32)

    bounds, wide_bounds = key_bounds(TK, TM), key_bounds(FK, FK)
    id_row = jnp.broadcast_to(ids[None, :], (8, length))
    id_col = jnp.broadcast_to(ids[:, None], (length, 128))

    cot_both = jnp.concatenate([cotangent[0], cot_far], 0)
    clean_in, cot_both, cos_t, sin_t, bounds, wide_bounds, id_row, id_col = (
        lax.optimization_barrier(
            (clean_in, cot_both, cos_t, sin_t, bounds, wide_bounds, id_row, id_col)
        )
    )
    clean_far = lax.ppermute(clean_in, "seq", swap)

    vec = jnp.concatenate([scale_one[None], shift_one[None], jnp.zeros((6, width), F32)], 0)
    bias_own = lax.dynamic_slice_in_dim(qkv_b, core * 3 * span, 3 * span, 0)
    bias_own = jnp.transpose(bias_own.reshape(heads, 3, HD), (1, 0, 2)).reshape(3 * span, 1)
    q, k, v, kc, vc, a_own = project(
        jnp.stack([core, noisy.astype(core.dtype)]), tok, other, clean_in, clean_far, gathered, vec,
        bias_own, cos_t, sin_t, heads
    )
    o, lse = attend(wide_bounds, q, k, v, kc, vc, id_row, id_col, heads, 1)
    o, lse, ffn = lax.optimization_barrier((o, lse, ffn))
    at = span + n_fsdp * inner
    out_near, up_own = ffn[:, :span], ffn[:, span:at]
    down_own = jnp.concatenate([ffn[:, at : at + width], ffn[:, at + width :]], 0)
    out_full = in_order(out_near, lax.ppermute(out_near, "seq", swap), 1)
    cut = lambda value, which: lax.dynamic_slice_in_dim(value, which * local_rows, local_rows, 1)
    o_mine = cut(o, core)
    o_in = lax.ppermute(cut(o, 1 - core), "seq", swap)
    attended = in_order(o_mine, o_in, 0)

    rows_in = tok.astype(F32)
    hidden = rows_in + rows_contract(attended, out_full) + out_shift
    normed_two, inverse_two = normalize_parts(hidden)
    second_in = (normed_two * scale_two + shift_two).astype(BF)
    both_in = jnp.concatenate([second_in, lax.ppermute(second_in, "seq", swap)], 0)

    def join(product, rows):
        far = product(rows[local_rows:]).astype(BF)
        return product(rows[:local_rows]) + lax.ppermute(far, "seq", swap).astype(F32)

    pre_act = dot(both_in, up_own) + up_b
    root = (2 / math.pi) ** 0.5
    square = pre_act * pre_act
    bend = jnp.tanh(pre_act * (root + 0.044715 * root * square))
    rise = 0.5 + 0.5 * bend
    act_low = (pre_act * rise).astype(BF)
    curve = pre_act * (1 - bend * bend) * (0.5 * root + 1.5 * 0.044715 * root * square)
    slope = (rise + curve).astype(BF)
    grad_down_w = beside(rows_contract(act_low, cot_both).astype(BF))
    scatter = lambda grad: lax.psum_scatter(grad, "fsdp", scatter_dimension=0, tiled=True)
    act_low, slope, grad_down_w, cot_both = lax.optimization_barrier(
        (act_low, slope, grad_down_w, cot_both)
    )
    down_part = scatter(grad_down_w)
    result = hidden + join(lambda rows: dot(rows, down_own), act_low) + down_shift

    grad_top = cotangent[0].astype(F32)
    grad_down_b = jnp.sum(grad_top, 0)
    grad_pre = (right_transposed(cot_both, down_own) * slope.astype(F32)).astype(BF)
    grad_second = join(lambda rows: right_transposed(rows, up_own), grad_pre)
    grad_up_b = jnp.sum(grad_pre.astype(F32), 0)
    grad_up_w = rows_contract(both_in, grad_pre).astype(BF)
    grad_scale_two = jnp.sum(grad_second * normed_two, 0)
    grad_shift_two = jnp.sum(grad_second, 0)
    grad_hidden = grad_top + norm_backward(grad_second, normed_two, inverse_two, scale_two)

    grad_attn = grad_hidden.astype(BF)
    grad_out_w = dot(attended, grad_attn).astype(BF)
    grad_out_b = jnp.sum(grad_attn.astype(F32), 0)
    grad_o = right_transposed(out_full, grad_attn).astype(BF)
    cut_heads = lambda which: lax.dynamic_slice_in_dim(grad_o, which * span, span, 0)
    do_mine = cut_heads(core)
    do_in = lax.ppermute(cut_heads(1 - core), "seq", swap)
    cut_cols = lambda which: lax.dynamic_slice_in_dim(grad_out_w, which * span, span, 1)
    out_sum = (
        cut_cols(core).astype(F32) + lax.ppermute(cut_cols(1 - core), "seq", swap).astype(F32)
    ).astype(BF)
    do_mine, do_in, grad_up_w, out_sum = lax.optimization_barrier(
        (do_mine, do_in, grad_up_w, out_sum)
    )
    out_up_part = scatter(jnp.concatenate([out_sum, grad_up_w], 1))

    back_args = lambda mine: (
        bounds, q, k, v, kc, vc, o, lse, mine, do_in, id_row, id_col, cos_t, sin_t
    )
    hold = lax.optimization_barrier
    cross = [(0, 2), (1, 3), (2, 0), (3, 1)]
    to_clean = lambda send: lax.ppermute(send, "seq", [(0, 2), (1, 3)])
    pair_w = 2 * 3 * HD

    def joined(own, got):
        own = own.reshape(2, 3, HD, -1)
        key_value = own[:, 1:].astype(F32) + got.reshape(2, 2, HD, -1).astype(F32)
        return jnp.concatenate([own[:, :1], key_value.astype(BF)], 1).reshape(pair_w, -1)

    def weight_grad(own):
        return lax.dot_general(
            a_own, own, (((0,), (1,)), ((), ())), preferred_element_type=F32
        ).astype(BF)

    def back(own, first, count):
        cols = gathered[:, first * pair_w : (first + count) * pair_w]
        return lax.dot_general(
            own, cols, (((0,), (1,)), ((), ())), preferred_element_type=F32
        )

    own_0, send_0 = attend_back(*back_args(do_mine), 0, 2)
    send_0, do_mine = hold((send_0, do_mine))
    got_0 = to_clean(send_0)
    own_1, send_1 = attend_back(*back_args(do_mine), 1, 2)
    own_1, send_1, got_0, down_part = hold((own_1, send_1, got_0, down_part))
    got_1, down_far = to_clean(send_1), lax.ppermute(down_part, "seq", cross)
    own_0 = joined(own_0, got_0)
    grad_0, do_mine = hold((weight_grad(own_0), do_mine))
    own_2, send_2 = attend_back(*back_args(do_mine), 2, 2)
    own_2, send_2, got_1, down_far, out_up_part = hold(
        (own_2, send_2, got_1, down_far, out_up_part)
    )
    got_2 = to_clean(send_2)
    own_1 = joined(own_1, got_1)
    grad_01, own_1 = hold((jnp.concatenate([grad_0, weight_grad(own_1)], 1), own_1))
    exchange = lambda grad: lax.all_to_all(
        grad.reshape(n_fsdp, shard, grad.shape[1]), "fsdp", 0, 0
    )
    piece_sum = lambda pieces: functools.reduce(
        jnp.add, [pieces[d].astype(F32) for d in range(n_fsdp)]
    ).astype(BF)
    pieces_01 = exchange(grad_01)
    own_01 = jnp.concatenate([own_0, own_1], 0)
    first_01 = back(own_01, 0, 2)
    got_2, out_up_part, first_01 = hold((got_2, out_up_part, first_01))
    own_2 = joined(own_2, got_2)
    far_rows = (first_01[local_rows:] + back(own_2[:, local_rows:], 2, 1)).astype(BF)
    grad_2, far_rows, pieces_01 = hold((weight_grad(own_2), far_rows, pieces_01))
    pieces_2 = exchange(grad_2)
    got_rows = lax.ppermute(far_rows, "seq", swap).astype(F32)
    grad_first = first_01[:local_rows] + back(own_2[:, :local_rows], 2, 1) + got_rows

    def chip_sum(part, far):
        total = (part.astype(F32) + far.astype(F32)).astype(BF)
        return total, lax.ppermute(total, "seq", swap)

    out_up_both = chip_sum(out_up_part, lax.ppermute(out_up_part, "seq", cross))
    out_g, up_g, down_g = assemble(
        core.reshape(1).astype(jnp.int32), *out_up_both, *chip_sum(down_part, down_far), span, n_fsdp
    )

    sum_cols = lambda own: jnp.sum(own.astype(F32), 1)
    grad_qkv_b = jnp.concatenate([sum_cols(own_01), sum_cols(own_2)])
    normed_one, inverse_one = normalize_parts(rows_in)
    grad_scale_one = jnp.sum(grad_first * normed_one, 0)
    grad_shift_one = jnp.sum(grad_first, 0)
    grad_rows = grad_hidden + norm_backward(grad_first, normed_one, inverse_one, scale_one)

    qkv_b_wide = lax.dynamic_update_slice_in_dim(
        jnp.zeros((2 * 3 * span,), F32), grad_qkv_b, core * 3 * span, 0
    )
    up_b_wide = lax.dynamic_update_slice_in_dim(
        jnp.zeros((n_fsdp, 2, inner), F32),
        jnp.swapaxes(grad_up_b.reshape(2, n_fsdp, inner // 2), 0, 1).reshape(n_fsdp, 1, inner),
        core,
        1,
    )
    pieces = [
        piece.reshape(n_fsdp, -1)
        for piece in (
            grad_scale_one, grad_shift_one, qkv_b_wide, grad_out_b, grad_scale_two,
            grad_shift_two, up_b_wide, grad_down_b,
        )
    ]
    sizes = [piece.shape[1] for piece in pieces]
    packed = jnp.concatenate(pieces, 1)
    lines = -(-packed.shape[1] // 128)
    packed = jnp.pad(packed, ((0, 0), (0, lines * 128 - packed.shape[1])))
    packed = packed.reshape(n_fsdp, lines, 128)
    part_01 = piece_sum(pieces_01)
    grad_rows, out_g, up_g, down_g, packed, part_01, pieces_2 = hold(
        (grad_rows, out_g, up_g, down_g, packed, part_01, pieces_2)
    )
    qkv_part = jnp.concatenate([part_01, piece_sum(pieces_2)], 1)
    qkv_g, small_sum = finish(qkv_part, packed)
    small_sum = small_sum.reshape(-1)
    small_out, at = [], 0
    for size in sizes:
        small_out.append(small_sum[at : at + size])
        at += size
    return (
        result.astype(BF)[None],
        grad_rows[None],
        small_out[0],
        small_out[1],
        qkv_g,
        small_out[2],
        out_g,
        small_out[3],
        small_out[4],
        small_out[5],
        up_g,
        small_out[6],
        down_g,
        small_out[7],
    )


def solution(mesh):
    row, mat, vec = P("fsdp", "seq", None), P("fsdp", None), P("fsdp")
    in_specs = (row, mat, vec, vec, mat, vec, mat, vec, vec, vec, mat, vec, mat, vec, row)
    out_specs = (row, row, vec, vec, mat, vec, mat, vec, vec, vec, mat, vec, mat, vec)
    return jax.shard_map(
        on_device, mesh=mesh, in_specs=in_specs, out_specs=out_specs, check_vma=False
    )
```

```python
import functools
import math

import jax
import jax.numpy as jnp
from jax import lax
from jax.experimental import pallas as pl
from jax.experimental.pallas import tpu as pltpu
from jax.sharding import PartitionSpec as P

H = 12
HD = 64
EPSILON = 1e-05
LOG2E = 1.4426950408889634
NEG = -1e30
TQ = 512
TK = 256
TM = 256
FK = 1024
BF = jnp.bfloat16
F32 = jnp.float32


def normalize_parts(values):
    mean_value = jnp.mean(values, -1, keepdims=True)
    centred = values - mean_value
    variance = jnp.mean(centred * centred, -1, keepdims=True)
    inverse = lax.rsqrt(variance + EPSILON)
    return (centred * inverse, inverse)


def norm_backward(grad_out, normed, inverse, scale):
    grad_norm = grad_out * scale
    return inverse * (
        grad_norm
        - jnp.mean(grad_norm, -1, keepdims=True)
        - normed * jnp.mean(grad_norm * normed, -1, keepdims=True)
    )


def rows_contract(left, right):
    return lax.dot_general(left, right, (((0,), (0,)), ((), ())), preferred_element_type=F32)


def right_transposed(left, right):
    return lax.dot_general(left, right, (((1,), (1,)), ((), ())), preferred_element_type=F32)


def dot(left, right):
    return jnp.dot(left, right, preferred_element_type=F32)


def qkv_kernel(heads, core_ref, mine, other, mine_c, other_c, sent, sent_other, w_ref, vec_ref, bias_ref, cos_ref,
               sin_ref, q_out, k_out, v_out, kc_out, vc_out, a_out, wt):
    step = pl.program_id(0)
    span = heads * HD

    @pl.when(step == 0)
    def _():
        whole = jnp.transpose(w_ref[...])
        for h in range(heads):
            for part in range(3):
                wt[part * span + h * HD : part * span + (h + 1) * HD, :] = whole[
                    (3 * h + part) * HD : (3 * h + part + 1) * HD, :
                ]

    def normed(rows):
        values = rows.astype(F32)
        n, _ = normalize_parts(values)
        return (n * vec_ref[0:1, :] + vec_ref[1:2, :]).astype(BF)

    def turn(lin, base, out):
        cos_t, sin_t = cos_ref[...], sin_ref[...]
        half = HD // 2
        for h in range(heads):
            first = lin[base + h * HD : base + h * HD + half, :]
            second = lin[base + h * HD + half : base + (h + 1) * HD, :]
            out[h * HD : h * HD + half, :] = (first * cos_t - second * sin_t).astype(BF)
            out[h * HD + half : (h + 1) * HD, :] = (first * sin_t + second * cos_t).astype(BF)

    quarter = pl.num_programs(0) // 4

    @pl.when(step < 2 * quarter)
    def _():
        a = normed(jnp.where(step < quarter, mine[...], other[...]))
        a_out[...] = a
        lin = right_transposed(wt[...], a) + bias_ref[...]
        turn(lin, 0, q_out)
        turn(lin, span, k_out)
        v_out[...] = lin[2 * span :, :].astype(BF)

    @pl.when(step >= 2 * quarter)
    def _():
        here = jnp.where(step < 3 * quarter, mine_c[...], other_c[...])
        there = jnp.where(step < 3 * quarter, sent[...], sent_other[...])
        a = normed(jnp.where(core_ref[1] == 1, there, here))
        lin = right_transposed(wt[span:, :], a) + bias_ref[span:, :]
        turn(lin, 0, kc_out)
        vc_out[...] = lin[span:, :].astype(BF)


def project(core, mine, other, sent, sent_other, weight, vec, bias, cos_t, sin_t, heads):
    local, width = mine.shape
    span = heads * HD
    tile = 256
    n = local // tile

    def place(t, c):
        mine_first = jnp.where(t % (2 * n) < n, c[0], 1 - c[0])
        return mine_first * n + t % n

    def src(k):
        return pl.BlockSpec((tile, width), lambda t, c: (jnp.clip(t - k * n, 0, n - 1), 0))

    whole = lambda shape: pl.BlockSpec(shape, lambda t, c: (0, 0))
    own = pl.BlockSpec((span, tile), lambda t, c: (0, place(jnp.minimum(t, 2 * n - 1), c)))
    cln = pl.BlockSpec((span, tile), lambda t, c: (0, place(jnp.maximum(t, 2 * n), c)))
    own_a = pl.BlockSpec((tile, width), lambda t, c: (jnp.minimum(t, 2 * n - 1), 0))
    tab = pl.BlockSpec((HD // 2, tile), lambda t, c: (0, place(t, c)))
    head_shape = jax.ShapeDtypeStruct((span, 2 * local), BF)
    row_shape = jax.ShapeDtypeStruct((2 * local, width), BF)
    return pl.pallas_call(
        functools.partial(qkv_kernel, heads),
        grid_spec=pltpu.PrefetchScalarGridSpec(
            num_scalar_prefetch=1,
            grid=(4 * n,),
            in_specs=[src(0), src(1)] + [src(2), src(3)] * 2 + [whole((width, 3 * span)), whole(vec.shape),
                      whole(bias.shape), tab, tab],
            out_specs=[own, own, own, cln, cln, own_a],
            scratch_shapes=[pltpu.VMEM((3 * span, width), BF)],
        ),
        out_shape=[head_shape] * 5 + [row_shape],
        name="project",
    )(core, mine, other, mine, other, sent, sent_other, weight, vec, bias, cos_t, sin_t)


def attend_kernel(group, bounds, q, k, v, kc, vc, id_row, id_col, o_out, lse_out, ks, kcs, vs,
                  vcs):
    total = q.shape[1]
    scale = LOG2E * HD**-0.5
    ones = jnp.ones((16, total), BF)
    for h in range(group):
        rows = slice(h * HD, (h + 1) * HD)
        ks[h] = jnp.transpose(k[rows, :])
        kcs[h] = jnp.transpose(kc[rows, :])
        vs[h, :HD] = v[rows, :]
        vcs[h, :HD] = vc[rows, :]
        vs[h, HD:] = ones
        vcs[h, HD:] = ones
    lift = bounds[4, 0]

    lead = jnp.ones((8, HD), BF)
    top = lambda ref, rows: jnp.max(dot(lead, ref[rows, :] * ref[rows, :]))
    limit = jnp.float32(0.9 * (96.0 / scale) ** 2)
    small = None
    for h in range(group):
        rows = slice(h * HD, (h + 1) * HD)
        fits = top(q, rows) * jnp.maximum(top(k, rows), top(kc, rows)) < limit
        small = fits if small is None else jnp.logical_and(small, fits)

    def key_ids(keys):
        col = id_col[keys, :]
        return jnp.concatenate([col] * (TQ // 128), 1)

    def sweep(i, q_ids, update, state):
        def band(j, state):
            keys = pl.ds(pl.multiple_of(j * FK, FK), FK)
            return update(state, ks, vs, keys, key_ids(keys) == q_ids)

        def full(j, state):
            keys = pl.ds(pl.multiple_of(j * FK, FK), FK)
            return update(state, kcs, vcs, keys, None)

        def edge(j, state):
            keys = pl.ds(pl.multiple_of(j * FK, FK), FK)
            return update(state, kcs, vcs, keys, key_ids(keys) < q_ids + lift)

        state = lax.fori_loop(bounds[2, i], bounds[3, i], band, state)
        state = lax.fori_loop(0, bounds[0, i], full, state)
        return lax.fori_loop(bounds[0, i], bounds[1, i], edge, state)

    def store(h, at, acc, log_shift):
        total_w = acc[HD : HD + 1, :]
        o_out[h * HD : (h + 1) * HD, at] = (acc[:HD, :] / total_w).astype(BF)
        lse_out[h, :, at] = jnp.broadcast_to(log_shift + jnp.log2(total_w), (8, TQ))

    def plain_tile(i, _):
        at = pl.ds(pl.multiple_of(i * TQ, TQ), TQ)
        queries = [q[h * HD : (h + 1) * HD, at] for h in range(group)]

        def update(state, key_ref, val_ref, keys, mask):
            out = []
            for h in range(group):
                p = jnp.exp2(dot(key_ref[h, keys, :], queries[h]) * scale)
                if mask is not None:
                    p = jnp.where(mask, p, 0.0)
                out.append(state[h] + dot(val_ref[h, :, keys], p.astype(BF)))
            return tuple(out)

        state = (jnp.zeros((HD + 16, TQ), F32),) * group
        state = sweep(i, id_row[0:1, at], update, state)
        for h in range(group):
            store(h, at, state[h], 0.0)
        return 0

    def shifted_tile(i, _):
        at = pl.ds(pl.multiple_of(i * TQ, TQ), TQ)
        q_ids = id_row[0:1, at]
        for h in range(group):
            query = q[h * HD : (h + 1) * HD, at]

            def update(state, key_ref, val_ref, keys, mask):
                m, acc = state
                s = dot(key_ref[h, keys, :], query)
                if mask is not None:
                    s = jnp.where(mask, s, NEG)
                m_new = jnp.maximum(m, jnp.max(s, 0, keepdims=True))
                p = jnp.exp2((s - m_new) * scale).astype(BF)
                alpha = jnp.exp2((m - m_new) * scale)
                return m_new, acc * alpha + dot(val_ref[h, :, keys], p)

            state = (jnp.full((1, TQ), NEG, F32), jnp.zeros((HD + 16, TQ), F32))
            m, acc = sweep(i, q_ids, update, state)
            store(h, at, acc, m * scale)
        return 0

    @pl.when(small)
    def _():
        lax.fori_loop(0, total // TQ, plain_tile, 0)

    @pl.when(jnp.logical_not(small))
    def _():
        lax.fori_loop(0, total // TQ, shifted_tile, 0)


def attend(bounds, q, k, v, kc, vc, id_row, id_col, heads, group):
    total = q.shape[1]
    head = pl.BlockSpec((group * HD, total), lambda g, b: (g, 0))
    whole = lambda shape: pl.BlockSpec(shape, lambda g, b: (0, 0))
    return pl.pallas_call(
        functools.partial(attend_kernel, group),
        grid_spec=pltpu.PrefetchScalarGridSpec(
            num_scalar_prefetch=1,
            grid=(heads // group,),
            in_specs=[head] * 5 + [whole(id_row.shape), whole(id_col.shape)],
            out_specs=[head, pl.BlockSpec((group, 8, total), lambda g, b: (g, 0, 0))],
            scratch_shapes=[pltpu.VMEM((group, total, HD), BF)] * 2
            + [pltpu.VMEM((group, HD + 16, total), BF)] * 2,
        ),
        out_shape=[
            jax.ShapeDtypeStruct((heads * HD, total), BF),
            jax.ShapeDtypeStruct((heads, 8, total), F32),
        ],
        cost_estimate=pl.CostEstimate(
            flops=16 * heads * HD * total * total, bytes_accessed=2**24, transcendentals=0
        ),
        name="attend",
    )(bounds, q, k, v, kc, vc, id_row, id_col)


def attend_back_kernel(group, bounds, q, k, v, kc, vc, o, lse, do_mine, do_other, id_row, id_col,
                       cos_ref, sin_ref, own_out, cln_out, ks, vs, kcs, vcs, qs, dos, dot_s,
                       dk_acc, dv_acc, dkc_acc, dvc_acc, dq_acc):
    total = q.shape[1]
    half_rows = total // 2
    scale = LOG2E * HD**-0.5
    lift = bounds[4, 0]
    core = bounds[4, 1]
    near = pl.ds(pl.multiple_of(core * half_rows, 128), half_rows)
    far = pl.ds(pl.multiple_of((1 - core) * half_rows, 128), half_rows)
    dot_s[:, near] = do_mine[...]
    dot_s[:, far] = do_other[...]
    for h in range(group):
        rows = slice(h * HD, (h + 1) * HD)
        ks[h] = jnp.transpose(k[rows, :])
        vs[h] = jnp.transpose(v[rows, :])
        kcs[h] = jnp.transpose(kc[rows, :])
        vcs[h] = jnp.transpose(vc[rows, :])
        qs[h] = jnp.transpose(q[rows, :])
        dos[h] = jnp.transpose(dot_s[rows, :])
    for ref in (dk_acc, dv_acc, dkc_acc, dvc_acc):
        ref[...] = jnp.zeros_like(ref)

    def one_tile(i, _):
        at = pl.ds(pl.multiple_of(i * TQ, TQ), TQ)
        q_ids = id_row[0:1, at]
        queries, grads, deltas, sums, q_rows, g_rows = [], [], [], [], [], []
        for h in range(group):
            rows = slice(h * HD, (h + 1) * HD)
            queries.append(q[rows, at])
            g = dot_s[rows, at]
            grads.append(g)
            deltas.append(jnp.sum(g.astype(F32) * o[rows, at].astype(F32), 0, keepdims=True))
            sums.append(lse[h, 0:1, at])
            q_rows.append(qs[h, at, :])
            g_rows.append(dos[h, at, :])

        def update(state, key_ref, val_ref, key_cols, dk, dv, keys, mask):
            out = []
            for h in range(group):
                s = dot(key_ref[h, keys, :], queries[h])
                p = jnp.exp2(s * scale - sums[h])
                if mask is not None:
                    p = jnp.where(mask, p, 0.0)
                dp = dot(val_ref[h, keys, :], grads[h])
                ds = (p * (dp - deltas[h])).astype(BF)
                dv[h, keys, :] += dot(p.astype(BF), g_rows[h])
                dk[h, keys, :] += dot(ds, q_rows[h])
                out.append(state[h] + dot(key_cols[h * HD : (h + 1) * HD, keys], ds))
            return tuple(out)

        def key_ids(keys):
            col = id_col[keys, :]
            return jnp.concatenate([col] * (TQ // 128), 1)

        def band(j, state):
            keys = pl.ds(pl.multiple_of(j * TM, TM), TM)
            return update(state, ks, vs, k, dk_acc, dv_acc, keys, key_ids(keys) == q_ids)

        def full(j, state):
            keys = pl.ds(pl.multiple_of(j * TK, TK), TK)
            return update(state, kcs, vcs, kc, dkc_acc, dvc_acc, keys, None)

        def edge(j, state):
            keys = pl.ds(pl.multiple_of(j * TM, TM), TM)
            mask = key_ids(keys) < q_ids + lift
            return update(state, kcs, vcs, kc, dkc_acc, dvc_acc, keys, mask)

        state = (jnp.zeros((HD, TQ), F32),) * group
        state = lax.fori_loop(bounds[2, i], bounds[3, i], band, state)
        state = lax.fori_loop(0, bounds[0, i], full, state)
        state = lax.fori_loop(bounds[0, i] * (TK // TM), bounds[1, i], edge, state)
        for h in range(group):
            dq_acc[h * HD : (h + 1) * HD, at] = state[h]
        return 0

    lax.fori_loop(0, total // TQ, one_tile, 0)

    half = HD // 2
    cos_t, sin_t = cos_ref[...], sin_ref[...]
    noisy = lift == 0

    def spread(out, value, base):
        rows = slice(base, base + value.shape[0])
        out[rows, near] = value[:, :half_rows].astype(BF)
        out[rows, far] = value[:, half_rows:].astype(BF)

    def back_turn(out, w, base):
        first, second = w[:half, :], w[half:, :]
        spread(out, first * cos_t + second * sin_t, base)
        spread(out, second * cos_t - first * sin_t, base + half)

    for h in range(group):
        back_turn(own_out, dq_acc[h * HD : (h + 1) * HD, :] * HD**-0.5, 3 * h * HD)
        band_k = jnp.where(noisy, dk_acc[h], dkc_acc[h])
        band_v = jnp.where(noisy, dv_acc[h], dvc_acc[h])
        back_turn(own_out, jnp.transpose(band_k) * HD**-0.5, (3 * h + 1) * HD)
        spread(own_out, jnp.transpose(band_v), (3 * h + 2) * HD)
        back_turn(cln_out, jnp.transpose(dkc_acc[h]) * HD**-0.5, 2 * h * HD)
        spread(cln_out, jnp.transpose(dvc_acc[h]), (2 * h + 1) * HD)


def attend_back(bounds, q, k, v, kc, vc, o, lse, do_mine, do_other, id_row, id_col, cos_t, sin_t,
                pair, group):
    total = q.shape[1]
    head = pl.BlockSpec((group * HD, total), lambda g, b: (pair, 0))
    halfhead = pl.BlockSpec((group * HD, total // 2), lambda g, b: (pair, 0))
    whole = lambda shape: pl.BlockSpec(shape, lambda g, b: (0, 0))
    rows16 = pltpu.VMEM((group, total, HD), BF)
    rows32 = pltpu.VMEM((group, total, HD), F32)
    outs = [(group * 3 * HD, total), (group * 2 * HD, total)]
    return pl.pallas_call(
        functools.partial(attend_back_kernel, group),
        grid_spec=pltpu.PrefetchScalarGridSpec(
            num_scalar_prefetch=1,
            grid=(1,),
            in_specs=[head] * 6
            + [pl.BlockSpec((group, 8, total), lambda g, b: (pair, 0, 0)), halfhead, halfhead]
            + [whole(id_row.shape), whole(id_col.shape), whole(cos_t.shape), whole(sin_t.shape)],
            out_specs=[whole(shape) for shape in outs],
            scratch_shapes=[rows16] * 6
            + [pltpu.VMEM((group * HD, total), BF)]
            + [rows32] * 4
            + [pltpu.VMEM((group * HD, total), F32)],
        ),
        out_shape=[jax.ShapeDtypeStruct(shape, BF) for shape in outs],
        cost_estimate=pl.CostEstimate(
            flops=20 * group * HD * total * total, bytes_accessed=8 * 2**20, transcendentals=0
        ),
        name="attend_back",
    )(bounds, q, k, v, kc, vc, o, lse, do_mine, do_other, id_row, id_col, cos_t, sin_t)


def finish_kernel(n, g, s, g_out, s_out, s_in, g_x, s_x, g_c, s_c, g_t, s_t, s_send, s_recv,
                  x_send, x_recv, c_send, c_recv, local):
    me = lax.axis_index("fsdp")
    seat = lax.axis_index("seq")
    core = lax.rem(seat, 2)
    across = {"seq": lax.rem(seat + 2, 4)}
    beside = {"seq": seat + 1 - 2 * core}
    mesh_id = pl.DeviceIdType.MESH
    barrier = pltpu.get_barrier_semaphore()
    peers = [{"fsdp": lax.rem(me + d, n)} for d in range(1, n)]
    for where in peers + [across, beside]:
        pl.semaphore_signal(barrier, inc=1, device_id=where, device_id_type=mesh_id)
    pl.semaphore_wait(barrier, n + 1)

    def push(src, dst, one, two, where):
        copy = pltpu.make_async_remote_copy(
            src_ref=src, dst_ref=dst, send_sem=one, recv_sem=two, device_id=where,
            device_id_type=mesh_id,
        )
        copy.start()
        return copy

    def settle(tmp, out, sem):
        copy = pltpu.make_async_copy(tmp, out, sem)
        copy.start()
        copy.wait()

    first = [
        push(s.at[lax.rem(me + d, n)], s_in.at[d - 1], s_send.at[d - 1], s_recv.at[d - 1],
             peers[d - 1])
        for d in range(1, n)
    ]
    far_g = push(g, g_x, x_send.at[0], x_recv.at[0], across)
    for copy in first:
        copy.wait()
    total = s[me]
    for d in range(n - 1):
        total = total + s_in[d]
    s_t[0] = total
    settle(s_t.at[0], s_x.at[0], local.at[0])
    far_s = push(s_x.at[0], s_x.at[1], x_send.at[1], x_recv.at[1], across)
    far_g.wait()
    g_t[...] = (g[...].astype(F32) + g_x[...].astype(F32)).astype(BF)
    settle(g_t, g_c.at[core], local.at[1])
    near_g = push(g_c.at[core], g_c.at[core], c_send.at[0], c_recv.at[0], beside)
    far_s.wait()
    s_t[1] = s_x[0] + s_x[1]
    settle(s_t.at[1], s_c.at[0], local.at[2])
    near_s = push(s_c.at[0], s_c.at[1], c_send.at[1], c_recv.at[1], beside)
    near_g.wait()
    span = g.shape[1]
    for c in range(2):
        g_out[:, c * span : (c + 1) * span] = g_c[c].astype(F32)
    near_s.wait()
    s_out[...] = s_c[0] + s_c[1]


def finish(g, s):
    n = s.shape[0]
    vm = pl.BlockSpec(memory_space=pltpu.VMEM)
    dma = pltpu.SemaphoreType.DMA
    return pl.pallas_call(
        functools.partial(finish_kernel, n),
        in_specs=[vm] * 2,
        out_specs=[vm] * 2,
        out_shape=[
            jax.ShapeDtypeStruct((g.shape[0], 2 * g.shape[1]), F32),
            jax.ShapeDtypeStruct(s.shape[1:], F32),
        ],
        scratch_shapes=[
            pltpu.VMEM((n - 1,) + s.shape[1:], F32),
            pltpu.VMEM(g.shape, BF),
            pltpu.VMEM((2,) + s.shape[1:], F32),
            pltpu.VMEM((2,) + g.shape, BF),
            pltpu.VMEM((2,) + s.shape[1:], F32),
            pltpu.VMEM(g.shape, BF),
            pltpu.VMEM((2,) + s.shape[1:], F32),
            dma((n - 1,)),
            dma((n - 1,)),
            dma((2,)),
            dma((2,)),
            dma((2,)),
            dma((2,)),
            dma((3,)),
        ],
        compiler_params=pltpu.CompilerParams(collective_id=1, has_side_effects=True),
        name="finish",
    )(g, s)


def assemble_kernel(span, n, core_ref, mine, other, d_mine, d_other, out_ref, up_ref, down_ref):
    first_core = core_ref[0] == 0
    pick = lambda one, two: (
        jnp.where(first_core, one, two).astype(F32), jnp.where(first_core, two, one).astype(F32)
    )
    pair = pick(mine[...].astype(F32), other[...].astype(F32))
    rows = pair[0].shape[0]
    half = (pair[0].shape[1] - span) // (2 * n)
    for c in range(2):
        out_ref[:, c * span : (c + 1) * span] = pair[c][:, :span]
    for i in range(n):
        up_ref[:, 4 * i * half : 4 * (i + 1) * half] = jnp.concatenate(
            [
                part[:, span + (j * n + i) * half : span + (j * n + i + 1) * half]
                for part in pair
                for j in range(2)
            ],
            1,
        )
    pair = pick(d_mine[...].astype(F32), d_other[...].astype(F32))
    width = down_ref.shape[1]
    for c in range(2):
        for j in range(2):
            at = (2 * c + j) * rows
            down_ref[at : at + rows, :] = pair[c][:, j * width : (j + 1) * width]


def assemble(core, mine, other, d_mine, d_other, span, n):
    rows, width = mine.shape
    vm = pl.BlockSpec(memory_space=pltpu.VMEM)
    return pl.pallas_call(
        functools.partial(assemble_kernel, span, n),
        in_specs=[pl.BlockSpec(memory_space=pltpu.SMEM)] + [vm] * 4,
        out_specs=[vm] * 3,
        out_shape=[
            jax.ShapeDtypeStruct((rows, 2 * span), F32),
            jax.ShapeDtypeStruct((rows, 2 * (width - span)), F32),
            jax.ShapeDtypeStruct((4 * rows, d_mine.shape[1] // 2), F32),
        ],
        name="assemble",
    )(core, mine, other, d_mine, d_other)


def on_device(
    tokens,
    block_ids,
    ln1_scale,
    ln1_bias,
    qkv_weight,
    qkv_bias,
    out_weight,
    out_bias,
    ln2_scale,
    ln2_bias,
    up_weight,
    up_bias,
    down_weight,
    down_bias,
    cotangent,
):
    tok = tokens[0]
    local_rows, width = tok.shape
    ids = block_ids[0].astype(jnp.int32)
    length = ids.shape[0]
    shard = ln1_scale.shape[0]
    heads = H // 2
    span = heads * HD
    me = lax.axis_index("seq")
    core = me % 2
    noisy = me < 2
    swap = [(0, 1), (1, 0), (2, 3), (3, 2)]
    other = lax.ppermute(tok, "seq", swap)
    clean_in = lax.ppermute(tok, "seq", [(2, 0), (3, 1)])
    cot_far = lax.ppermute(cotangent[0], "seq", swap)

    q_cols = lax.dynamic_slice_in_dim(qkv_weight, core * 3 * span, 3 * span, 1)
    small = jnp.concatenate(
        [
            ln1_scale.reshape(1, shard),
            ln1_bias.reshape(1, shard),
            out_bias.reshape(1, shard),
            ln2_scale.reshape(1, shard),
            ln2_bias.reshape(1, shard),
            down_bias.reshape(1, shard),
            qkv_bias.reshape(-1, shard),
            up_bias.reshape(-1, shard),
        ],
        0,
    )
    n_small = small.shape[0]
    small = jnp.pad(small, ((0, 128 - n_small), (0, 0))).T
    gathered = lax.all_gather(
        jnp.concatenate([q_cols, small], 1), "fsdp", axis=0, tiled=True
    )
    n_fsdp = width // shard
    vectors = gathered[:, 3 * span :].reshape(n_fsdp, shard, 128)[:, :, :n_small]
    vectors = jnp.transpose(vectors, (2, 0, 1)).astype(F32)
    flat = vectors[:6].reshape(6, width)
    qkv_b = jnp.transpose(vectors[6:9], (1, 0, 2)).reshape(-1)
    scale_one, shift_one, out_shift, scale_two, shift_two, down_shift = [flat[i] for i in range(6)]

    inner = up_bias.shape[0] // 2
    up_b = jnp.transpose(vectors[9:], (1, 0, 2)).reshape(n_fsdp, 2, inner)
    by_half = lambda a: jnp.swapaxes(a.reshape(-1, n_fsdp, 2, inner // 2), 1, 2)
    up_b = by_half(lax.dynamic_index_in_dim(up_b, core, 1, False)).reshape(-1)
    up_cols = by_half(
        lax.dynamic_index_in_dim(up_weight.reshape(shard, n_fsdp, 2, inner), core, 2, False)
    ).reshape(shard, n_fsdp * inner)
    down_rows = lax.dynamic_slice_in_dim(down_weight, core * inner, inner, 0)
    beside = lambda a: jnp.concatenate([a[: a.shape[0] // 2], a[a.shape[0] // 2 :]], 1)
    out_cols = lax.dynamic_slice_in_dim(out_weight, core * span, span, 1)
    ffn = lax.all_gather(
        jnp.concatenate([out_cols, up_cols, beside(down_rows)], 1), "fsdp", axis=0, tiled=True
    )
    in_order = lambda near, far, axis: jnp.where(
        core == 0, jnp.concatenate([near, far], axis), jnp.concatenate([far, near], axis)
    )

    frequency = jnp.exp(-jnp.log(10000.0) * jnp.arange(HD // 2, dtype=F32) / (HD // 2))
    angles = frequency[:, None] * jnp.arange(length, dtype=F32)[None, :]
    cos_t, sin_t = jnp.cos(angles), jnp.sin(angles)

    first = ids[::TQ][:, None]
    last = ids[TQ - 1 :: TQ][:, None]
    before = lambda edge: jnp.sum((ids[None, :] < edge).astype(jnp.int32), 1)
    start_first, end_first = before(first), before(first + 1)
    start_last, end_last = before(last), before(last + 1)
    lift = jnp.where(noisy, 0, 1)
    zero = jnp.zeros_like(start_first)

    def key_bounds(full, masked):
        ceil_m = lambda value: (value + masked - 1) // masked
        return jnp.stack(
            [
                jnp.where(noisy, start_first, end_first) // full,
                ceil_m(jnp.where(noisy, start_last, end_last)),
                jnp.where(noisy, start_first // masked, zero),
                jnp.where(noisy, ceil_m(end_last), zero),
                zero + jnp.where(jnp.arange(zero.shape[0]) == 0, lift, core),
            ]
        ).astype(jnp.int32)

    bounds, wide_bounds = key_bounds(TK, TM), key_bounds(FK, FK)
    id_row = jnp.broadcast_to(ids[None, :], (8, length))
    id_col = jnp.broadcast_to(ids[:, None], (length, 128))

    cot_both = jnp.concatenate([cotangent[0], cot_far], 0)
    clean_in, cot_both, cos_t, sin_t, bounds, wide_bounds, id_row, id_col = (
        lax.optimization_barrier(
            (clean_in, cot_both, cos_t, sin_t, bounds, wide_bounds, id_row, id_col)
        )
    )
    clean_far = lax.ppermute(clean_in, "seq", swap)

    vec = jnp.concatenate([scale_one[None], shift_one[None], jnp.zeros((6, width), F32)], 0)
    bias_own = lax.dynamic_slice_in_dim(qkv_b, core * 3 * span, 3 * span, 0)
    bias_own = jnp.transpose(bias_own.reshape(heads, 3, HD), (1, 0, 2)).reshape(3 * span, 1)
    q, k, v, kc, vc, a_own = project(
        jnp.stack([core, noisy.astype(core.dtype)]), tok, other, clean_in, clean_far, gathered, vec,
        bias_own, cos_t, sin_t, heads
    )
    o, lse = attend(wide_bounds, q, k, v, kc, vc, id_row, id_col, heads, 1)
    cut = lambda value, which: lax.dynamic_slice_in_dim(value, which * local_rows, local_rows, 1)
    o_mine = cut(o, core)
    o_in = lax.ppermute(cut(o, 1 - core), "seq", swap)
    o_mine, o_in, ffn = lax.optimization_barrier((o_mine, o_in, ffn))
    at = span + n_fsdp * inner
    out_near, up_own = ffn[:, :span], ffn[:, span:at]
    down_own = jnp.concatenate([ffn[:, at : at + width], ffn[:, at + width :]], 0)
    out_full = in_order(out_near, lax.ppermute(out_near, "seq", swap), 1)
    attended = in_order(o_mine, o_in, 0)

    rows_in = tok.astype(F32)
    hidden = rows_in + rows_contract(attended, out_full) + out_shift
    normed_two, inverse_two = normalize_parts(hidden)
    second_in = (normed_two * scale_two + shift_two).astype(BF)
    both_in = jnp.concatenate([second_in, lax.ppermute(second_in, "seq", swap)], 0)

    def join(product, rows):
        far = product(rows[local_rows:]).astype(BF)
        return product(rows[:local_rows]) + lax.ppermute(far, "seq", swap).astype(F32)

    pre_act = dot(both_in, up_own) + up_b
    root = (2 / math.pi) ** 0.5
    square = pre_act * pre_act
    bend = jnp.tanh(pre_act * (root + 0.044715 * root * square))
    rise = 0.5 + 0.5 * bend
    act_low = (pre_act * rise).astype(BF)
    curve = pre_act * (1 - bend * bend) * (0.5 * root + 1.5 * 0.044715 * root * square)
    slope = (rise + curve).astype(BF)
    grad_down_w = beside(rows_contract(act_low, cot_both).astype(BF))
    scatter = lambda grad: lax.psum_scatter(grad, "fsdp", scatter_dimension=0, tiled=True)
    act_low, slope, grad_down_w, cot_both = lax.optimization_barrier(
        (act_low, slope, grad_down_w, cot_both)
    )
    down_part = scatter(grad_down_w)
    result = hidden + join(lambda rows: dot(rows, down_own), act_low) + down_shift

    grad_top = cotangent[0].astype(F32)
    grad_down_b = jnp.sum(grad_top, 0)
    grad_pre = (right_transposed(cot_both, down_own) * slope.astype(F32)).astype(BF)
    grad_second = join(lambda rows: right_transposed(rows, up_own), grad_pre)
    grad_up_b = jnp.sum(grad_pre.astype(F32), 0)
    grad_up_w = rows_contract(both_in, grad_pre).astype(BF)
    grad_scale_two = jnp.sum(grad_second * normed_two, 0)
    grad_shift_two = jnp.sum(grad_second, 0)
    grad_hidden = grad_top + norm_backward(grad_second, normed_two, inverse_two, scale_two)

    grad_attn = grad_hidden.astype(BF)
    grad_out_w = dot(attended, grad_attn).astype(BF)
    grad_out_b = jnp.sum(grad_attn.astype(F32), 0)
    grad_o = right_transposed(out_full, grad_attn).astype(BF)
    cut_heads = lambda which: lax.dynamic_slice_in_dim(grad_o, which * span, span, 0)
    do_mine = cut_heads(core)
    do_in = lax.ppermute(cut_heads(1 - core), "seq", swap)
    cut_cols = lambda which: lax.dynamic_slice_in_dim(grad_out_w, which * span, span, 1)
    out_sum = (
        cut_cols(core).astype(F32) + lax.ppermute(cut_cols(1 - core), "seq", swap).astype(F32)
    ).astype(BF)
    do_mine, do_in, grad_up_w, out_sum = lax.optimization_barrier(
        (do_mine, do_in, grad_up_w, out_sum)
    )
    out_up_part = scatter(jnp.concatenate([out_sum, grad_up_w], 1))

    back_args = lambda mine: (
        bounds, q, k, v, kc, vc, o, lse, mine, do_in, id_row, id_col, cos_t, sin_t
    )
    hold = lax.optimization_barrier
    cross = [(0, 2), (1, 3), (2, 0), (3, 1)]
    to_clean = lambda send: lax.ppermute(send, "seq", [(0, 2), (1, 3)])
    pair_w = 2 * 3 * HD

    def joined(own, got):
        own = own.reshape(2, 3, HD, -1)
        key_value = own[:, 1:].astype(F32) + got.reshape(2, 2, HD, -1).astype(F32)
        return jnp.concatenate([own[:, :1], key_value.astype(BF)], 1).reshape(pair_w, -1)

    def weight_grad(own):
        return lax.dot_general(
            a_own, own, (((0,), (1,)), ((), ())), preferred_element_type=F32
        ).astype(BF)

    def back(own, first, count):
        cols = gathered[:, first * pair_w : (first + count) * pair_w]
        return lax.dot_general(
            own, cols, (((0,), (1,)), ((), ())), preferred_element_type=F32
        )

    own_0, send_0 = attend_back(*back_args(do_mine), 0, 2)
    send_0, do_mine = hold((send_0, do_mine))
    got_0 = to_clean(send_0)
    own_1, send_1 = attend_back(*back_args(do_mine), 1, 2)
    own_1, send_1, got_0, down_part = hold((own_1, send_1, got_0, down_part))
    got_1, down_far = to_clean(send_1), lax.ppermute(down_part, "seq", cross)
    own_0 = joined(own_0, got_0)
    grad_0, do_mine = hold((weight_grad(own_0), do_mine))
    own_2, send_2 = attend_back(*back_args(do_mine), 2, 2)
    own_2, send_2, got_1, down_far, out_up_part = hold(
        (own_2, send_2, got_1, down_far, out_up_part)
    )
    got_2 = to_clean(send_2)
    own_1 = joined(own_1, got_1)
    grad_01, own_1 = hold((jnp.concatenate([grad_0, weight_grad(own_1)], 1), own_1))
    exchange = lambda grad: lax.all_to_all(
        grad.reshape(n_fsdp, shard, grad.shape[1]), "fsdp", 0, 0
    )
    piece_sum = lambda pieces: functools.reduce(
        jnp.add, [pieces[d].astype(F32) for d in range(n_fsdp)]
    ).astype(BF)
    pieces_01 = exchange(grad_01)
    own_01 = jnp.concatenate([own_0, own_1], 0)
    first_01 = back(own_01, 0, 2)
    got_2, out_up_part, first_01 = hold((got_2, out_up_part, first_01))
    own_2 = joined(own_2, got_2)
    far_rows = (first_01[local_rows:] + back(own_2[:, local_rows:], 2, 1)).astype(BF)
    grad_2, far_rows = hold((weight_grad(own_2), far_rows))
    got_rows = lax.ppermute(far_rows, "seq", swap).astype(F32)
    grad_first = first_01[:local_rows] + back(own_2[:, :local_rows], 2, 1) + got_rows

    def chip_sum(part, far):
        total = (part.astype(F32) + far.astype(F32)).astype(BF)
        return total, lax.ppermute(total, "seq", swap)

    out_up_both = chip_sum(out_up_part, lax.ppermute(out_up_part, "seq", cross))
    out_g, up_g, down_g = assemble(
        core.reshape(1).astype(jnp.int32), *out_up_both, *chip_sum(down_part, down_far), span, n_fsdp
    )

    grad_2, pieces_01, out_g, up_g, down_g = hold((grad_2, pieces_01, out_g, up_g, down_g))
    pieces_2 = exchange(grad_2)
    sum_cols = lambda own: jnp.sum(own.astype(F32), 1)
    grad_qkv_b = jnp.concatenate([sum_cols(own_01), sum_cols(own_2)])
    normed_one, inverse_one = normalize_parts(rows_in)
    grad_scale_one = jnp.sum(grad_first * normed_one, 0)
    grad_shift_one = jnp.sum(grad_first, 0)
    grad_rows = grad_hidden + norm_backward(grad_first, normed_one, inverse_one, scale_one)

    qkv_b_wide = lax.dynamic_update_slice_in_dim(
        jnp.zeros((2 * 3 * span,), F32), grad_qkv_b, core * 3 * span, 0
    )
    up_b_wide = lax.dynamic_update_slice_in_dim(
        jnp.zeros((n_fsdp, 2, inner), F32),
        jnp.swapaxes(grad_up_b.reshape(2, n_fsdp, inner // 2), 0, 1).reshape(n_fsdp, 1, inner),
        core,
        1,
    )
    pieces = [
        piece.reshape(n_fsdp, -1)
        for piece in (
            grad_scale_one, grad_shift_one, qkv_b_wide, grad_out_b, grad_scale_two,
            grad_shift_two, up_b_wide, grad_down_b,
        )
    ]
    sizes = [piece.shape[1] for piece in pieces]
    packed = jnp.concatenate(pieces, 1)
    lines = -(-packed.shape[1] // 128)
    packed = jnp.pad(packed, ((0, 0), (0, lines * 128 - packed.shape[1])))
    packed = packed.reshape(n_fsdp, lines, 128)
    part_01 = piece_sum(pieces_01)
    grad_rows, out_g, up_g, down_g, packed, part_01, pieces_2 = hold(
        (grad_rows, out_g, up_g, down_g, packed, part_01, pieces_2)
    )
    qkv_part = jnp.concatenate([part_01, piece_sum(pieces_2)], 1)
    qkv_g, small_sum = finish(qkv_part, packed)
    small_sum = small_sum.reshape(-1)
    small_out, at = [], 0
    for size in sizes:
        small_out.append(small_sum[at : at + size])
        at += size
    return (
        result.astype(BF)[None],
        grad_rows[None],
        small_out[0],
        small_out[1],
        qkv_g,
        small_out[2],
        out_g,
        small_out[3],
        small_out[4],
        small_out[5],
        up_g,
        small_out[6],
        down_g,
        small_out[7],
    )


def solution(mesh):
    row, mat, vec = P("fsdp", "seq", None), P("fsdp", None), P("fsdp")
    in_specs = (row, mat, vec, vec, mat, vec, mat, vec, vec, vec, mat, vec, mat, vec, row)
    out_specs = (row, row, vec, vec, mat, vec, mat, vec, vec, vec, mat, vec, mat, vec)
    return jax.shard_map(
        on_device, mesh=mesh, in_specs=in_specs, out_specs=out_specs, check_vma=False
    )
```

```python
import functools
import math

import jax
import jax.numpy as jnp
from jax import lax
from jax.experimental import pallas as pl
from jax.experimental.pallas import tpu as pltpu
from jax.sharding import PartitionSpec as P

H = 12
HD = 64
EPSILON = 1e-05
LOG2E = 1.4426950408889634
NEG = -1e30
TQ = 512
TK = 256
TM = 256
FK = 1024
BF = jnp.bfloat16
F32 = jnp.float32


def normalize_parts(values):
    mean_value = jnp.mean(values, -1, keepdims=True)
    centred = values - mean_value
    variance = jnp.mean(centred * centred, -1, keepdims=True)
    inverse = lax.rsqrt(variance + EPSILON)
    return (centred * inverse, inverse)


def norm_backward(grad_out, normed, inverse, scale):
    grad_norm = grad_out * scale
    return inverse * (
        grad_norm
        - jnp.mean(grad_norm, -1, keepdims=True)
        - normed * jnp.mean(grad_norm * normed, -1, keepdims=True)
    )


def rows_contract(left, right):
    return lax.dot_general(left, right, (((0,), (0,)), ((), ())), preferred_element_type=F32)


def right_transposed(left, right):
    return lax.dot_general(left, right, (((1,), (1,)), ((), ())), preferred_element_type=F32)


def dot(left, right):
    return jnp.dot(left, right, preferred_element_type=F32)


def qkv_kernel(heads, core_ref, mine, other, mine_c, other_c, sent, sent_other, w_ref, vec_ref, bias_ref, cos_ref,
               sin_ref, q_out, k_out, v_out, kc_out, vc_out, a_out, wt):
    step = pl.program_id(0)
    span = heads * HD

    @pl.when(step == 0)
    def _():
        whole = jnp.transpose(w_ref[...])
        for h in range(heads):
            for part in range(3):
                wt[part * span + h * HD : part * span + (h + 1) * HD, :] = whole[
                    (3 * h + part) * HD : (3 * h + part + 1) * HD, :
                ]

    def normed(rows):
        values = rows.astype(F32)
        n, _ = normalize_parts(values)
        return (n * vec_ref[0:1, :] + vec_ref[1:2, :]).astype(BF)

    def turn(lin, base, out):
        cos_t, sin_t = cos_ref[...], sin_ref[...]
        half = HD // 2
        for h in range(heads):
            first = lin[base + h * HD : base + h * HD + half, :]
            second = lin[base + h * HD + half : base + (h + 1) * HD, :]
            out[h * HD : h * HD + half, :] = (first * cos_t - second * sin_t).astype(BF)
            out[h * HD + half : (h + 1) * HD, :] = (first * sin_t + second * cos_t).astype(BF)

    quarter = pl.num_programs(0) // 4

    @pl.when(step < 2 * quarter)
    def _():
        a = normed(jnp.where(step < quarter, mine[...], other[...]))
        a_out[...] = a
        lin = right_transposed(wt[...], a) + bias_ref[...]
        turn(lin, 0, q_out)
        turn(lin, span, k_out)
        v_out[...] = lin[2 * span :, :].astype(BF)

    @pl.when(step >= 2 * quarter)
    def _():
        here = jnp.where(step < 3 * quarter, mine_c[...], other_c[...])
        there = jnp.where(step < 3 * quarter, sent[...], sent_other[...])
        a = normed(jnp.where(core_ref[1] == 1, there, here))
        lin = right_transposed(wt[span:, :], a) + bias_ref[span:, :]
        turn(lin, 0, kc_out)
        vc_out[...] = lin[span:, :].astype(BF)


def project(core, mine, other, sent, sent_other, weight, vec, bias, cos_t, sin_t, heads):
    local, width = mine.shape
    span = heads * HD
    tile = 512
    n = local // tile

    def place(t, c):
        mine_first = jnp.where(t % (2 * n) < n, c[0], 1 - c[0])
        return mine_first * n + t % n

    def src(k):
        return pl.BlockSpec((tile, width), lambda t, c: (jnp.clip(t - k * n, 0, n - 1), 0))

    whole = lambda shape: pl.BlockSpec(shape, lambda t, c: (0, 0))
    own = pl.BlockSpec((span, tile), lambda t, c: (0, place(jnp.minimum(t, 2 * n - 1), c)))
    cln = pl.BlockSpec((span, tile), lambda t, c: (0, place(jnp.maximum(t, 2 * n), c)))
    own_a = pl.BlockSpec((tile, width), lambda t, c: (jnp.minimum(t, 2 * n - 1), 0))
    tab = pl.BlockSpec((HD // 2, tile), lambda t, c: (0, place(t, c)))
    head_shape = jax.ShapeDtypeStruct((span, 2 * local), BF)
    row_shape = jax.ShapeDtypeStruct((2 * local, width), BF)
    return pl.pallas_call(
        functools.partial(qkv_kernel, heads),
        grid_spec=pltpu.PrefetchScalarGridSpec(
            num_scalar_prefetch=1,
            grid=(4 * n,),
            in_specs=[src(0), src(1)] + [src(2), src(3)] * 2 + [whole((width, 3 * span)), whole(vec.shape),
                      whole(bias.shape), tab, tab],
            out_specs=[own, own, own, cln, cln, own_a],
            scratch_shapes=[pltpu.VMEM((3 * span, width), BF)],
        ),
        out_shape=[head_shape] * 5 + [row_shape],
        name="project",
    )(core, mine, other, mine, other, sent, sent_other, weight, vec, bias, cos_t, sin_t)


def attend_kernel(group, bounds, q, k, v, kc, vc, id_row, id_col, o_out, lse_out, ks, kcs, vs,
                  vcs):
    total = q.shape[1]
    scale = LOG2E * HD**-0.5
    ones = jnp.ones((16, total), BF)
    for h in range(group):
        rows = slice(h * HD, (h + 1) * HD)
        ks[h] = jnp.transpose(k[rows, :])
        kcs[h] = jnp.transpose(kc[rows, :])
        vs[h, :HD] = v[rows, :]
        vcs[h, :HD] = vc[rows, :]
        vs[h, HD:] = ones
        vcs[h, HD:] = ones
    lift = bounds[4, 0]

    lead = jnp.ones((8, HD), BF)
    top = lambda ref, rows: jnp.max(dot(lead, ref[rows, :] * ref[rows, :]))
    limit = jnp.float32(0.9 * (96.0 / scale) ** 2)
    small = None
    for h in range(group):
        rows = slice(h * HD, (h + 1) * HD)
        fits = top(q, rows) * jnp.maximum(top(k, rows), top(kc, rows)) < limit
        small = fits if small is None else jnp.logical_and(small, fits)

    def key_ids(keys):
        col = id_col[keys, :]
        return jnp.concatenate([col] * (TQ // 128), 1)

    def sweep(i, q_ids, update, state):
        def band(j, state):
            keys = pl.ds(pl.multiple_of(j * FK, FK), FK)
            return update(state, ks, vs, keys, key_ids(keys) == q_ids)

        def full(j, state):
            keys = pl.ds(pl.multiple_of(j * FK, FK), FK)
            return update(state, kcs, vcs, keys, None)

        def edge(j, state):
            keys = pl.ds(pl.multiple_of(j * FK, FK), FK)
            return update(state, kcs, vcs, keys, key_ids(keys) < q_ids + lift)

        state = lax.fori_loop(bounds[2, i], bounds[3, i], band, state)
        state = lax.fori_loop(0, bounds[0, i], full, state)
        return lax.fori_loop(bounds[0, i], bounds[1, i], edge, state)

    def store(h, at, acc, log_shift):
        total_w = acc[HD : HD + 1, :]
        o_out[h * HD : (h + 1) * HD, at] = (acc[:HD, :] / total_w).astype(BF)
        lse_out[h, :, at] = jnp.broadcast_to(log_shift + jnp.log2(total_w), (8, TQ))

    def plain_tile(i, _):
        at = pl.ds(pl.multiple_of(i * TQ, TQ), TQ)
        queries = [q[h * HD : (h + 1) * HD, at] for h in range(group)]

        def update(state, key_ref, val_ref, keys, mask):
            out = []
            for h in range(group):
                p = jnp.exp2(dot(key_ref[h, keys, :], queries[h]) * scale)
                if mask is not None:
                    p = jnp.where(mask, p, 0.0)
                out.append(state[h] + dot(val_ref[h, :, keys], p.astype(BF)))
            return tuple(out)

        state = (jnp.zeros((HD + 16, TQ), F32),) * group
        state = sweep(i, id_row[0:1, at], update, state)
        for h in range(group):
            store(h, at, state[h], 0.0)
        return 0

    def shifted_tile(i, _):
        at = pl.ds(pl.multiple_of(i * TQ, TQ), TQ)
        q_ids = id_row[0:1, at]
        for h in range(group):
            query = q[h * HD : (h + 1) * HD, at]

            def update(state, key_ref, val_ref, keys, mask):
                m, acc = state
                s = dot(key_ref[h, keys, :], query)
                if mask is not None:
                    s = jnp.where(mask, s, NEG)
                m_new = jnp.maximum(m, jnp.max(s, 0, keepdims=True))
                p = jnp.exp2((s - m_new) * scale).astype(BF)
                alpha = jnp.exp2((m - m_new) * scale)
                return m_new, acc * alpha + dot(val_ref[h, :, keys], p)

            state = (jnp.full((1, TQ), NEG, F32), jnp.zeros((HD + 16, TQ), F32))
            m, acc = sweep(i, q_ids, update, state)
            store(h, at, acc, m * scale)
        return 0

    @pl.when(small)
    def _():
        lax.fori_loop(0, total // TQ, plain_tile, 0)

    @pl.when(jnp.logical_not(small))
    def _():
        lax.fori_loop(0, total // TQ, shifted_tile, 0)


def attend(bounds, q, k, v, kc, vc, id_row, id_col, heads, group):
    total = q.shape[1]
    head = pl.BlockSpec((group * HD, total), lambda g, b: (g, 0))
    whole = lambda shape: pl.BlockSpec(shape, lambda g, b: (0, 0))
    return pl.pallas_call(
        functools.partial(attend_kernel, group),
        grid_spec=pltpu.PrefetchScalarGridSpec(
            num_scalar_prefetch=1,
            grid=(heads // group,),
            in_specs=[head] * 5 + [whole(id_row.shape), whole(id_col.shape)],
            out_specs=[head, pl.BlockSpec((group, 8, total), lambda g, b: (g, 0, 0))],
            scratch_shapes=[pltpu.VMEM((group, total, HD), BF)] * 2
            + [pltpu.VMEM((group, HD + 16, total), BF)] * 2,
        ),
        out_shape=[
            jax.ShapeDtypeStruct((heads * HD, total), BF),
            jax.ShapeDtypeStruct((heads, 8, total), F32),
        ],
        cost_estimate=pl.CostEstimate(
            flops=16 * heads * HD * total * total, bytes_accessed=2**24, transcendentals=0
        ),
        name="attend",
    )(bounds, q, k, v, kc, vc, id_row, id_col)


def attend_back_kernel(group, bounds, q, k, v, kc, vc, o, lse, do_mine, do_other, id_row, id_col,
                       cos_ref, sin_ref, own_out, cln_out, ks, vs, kcs, vcs, qs, dos, dot_s,
                       dk_acc, dv_acc, dkc_acc, dvc_acc, dq_acc):
    total = q.shape[1]
    half_rows = total // 2
    scale = LOG2E * HD**-0.5
    lift = bounds[4, 0]
    core = bounds[4, 1]
    near = pl.ds(pl.multiple_of(core * half_rows, 128), half_rows)
    far = pl.ds(pl.multiple_of((1 - core) * half_rows, 128), half_rows)
    dot_s[:, near] = do_mine[...]
    dot_s[:, far] = do_other[...]
    for h in range(group):
        rows = slice(h * HD, (h + 1) * HD)
        ks[h] = jnp.transpose(k[rows, :])
        vs[h] = jnp.transpose(v[rows, :])
        kcs[h] = jnp.transpose(kc[rows, :])
        vcs[h] = jnp.transpose(vc[rows, :])
        qs[h] = jnp.transpose(q[rows, :])
        dos[h] = jnp.transpose(dot_s[rows, :])
    for ref in (dk_acc, dv_acc, dkc_acc, dvc_acc):
        ref[...] = jnp.zeros_like(ref)

    def one_tile(i, _):
        at = pl.ds(pl.multiple_of(i * TQ, TQ), TQ)
        q_ids = id_row[0:1, at]
        queries, grads, deltas, sums, q_rows, g_rows = [], [], [], [], [], []
        for h in range(group):
            rows = slice(h * HD, (h + 1) * HD)
            queries.append(q[rows, at])
            g = dot_s[rows, at]
            grads.append(g)
            deltas.append(jnp.sum(g.astype(F32) * o[rows, at].astype(F32), 0, keepdims=True))
            sums.append(lse[h, 0:1, at])
            q_rows.append(qs[h, at, :])
            g_rows.append(dos[h, at, :])

        def update(state, key_ref, val_ref, key_cols, dk, dv, keys, mask):
            out = []
            for h in range(group):
                s = dot(key_ref[h, keys, :], queries[h])
                p = jnp.exp2(s * scale - sums[h])
                if mask is not None:
                    p = jnp.where(mask, p, 0.0)
                dp = dot(val_ref[h, keys, :], grads[h])
                ds = (p * (dp - deltas[h])).astype(BF)
                dv[h, keys, :] += dot(p.astype(BF), g_rows[h])
                dk[h, keys, :] += dot(ds, q_rows[h])
                out.append(state[h] + dot(key_cols[h * HD : (h + 1) * HD, keys], ds))
            return tuple(out)

        def key_ids(keys):
            col = id_col[keys, :]
            return jnp.concatenate([col] * (TQ // 128), 1)

        def band(j, state):
            keys = pl.ds(pl.multiple_of(j * TM, TM), TM)
            return update(state, ks, vs, k, dk_acc, dv_acc, keys, key_ids(keys) == q_ids)

        def full(j, state):
            keys = pl.ds(pl.multiple_of(j * TK, TK), TK)
            return update(state, kcs, vcs, kc, dkc_acc, dvc_acc, keys, None)

        def edge(j, state):
            keys = pl.ds(pl.multiple_of(j * TM, TM), TM)
            mask = key_ids(keys) < q_ids + lift
            return update(state, kcs, vcs, kc, dkc_acc, dvc_acc, keys, mask)

        state = (jnp.zeros((HD, TQ), F32),) * group
        state = lax.fori_loop(bounds[2, i], bounds[3, i], band, state)
        state = lax.fori_loop(0, bounds[0, i], full, state)
        state = lax.fori_loop(bounds[0, i] * (TK // TM), bounds[1, i], edge, state)
        for h in range(group):
            dq_acc[h * HD : (h + 1) * HD, at] = state[h]
        return 0

    lax.fori_loop(0, total // TQ, one_tile, 0)

    half = HD // 2
    cos_t, sin_t = cos_ref[...], sin_ref[...]
    noisy = lift == 0

    def spread(out, value, base):
        rows = slice(base, base + value.shape[0])
        out[rows, near] = value[:, :half_rows].astype(BF)
        out[rows, far] = value[:, half_rows:].astype(BF)

    def back_turn(out, w, base):
        first, second = w[:half, :], w[half:, :]
        spread(out, first * cos_t + second * sin_t, base)
        spread(out, second * cos_t - first * sin_t, base + half)

    for h in range(group):
        back_turn(own_out, dq_acc[h * HD : (h + 1) * HD, :] * HD**-0.5, 3 * h * HD)
        band_k = jnp.where(noisy, dk_acc[h], dkc_acc[h])
        band_v = jnp.where(noisy, dv_acc[h], dvc_acc[h])
        back_turn(own_out, jnp.transpose(band_k) * HD**-0.5, (3 * h + 1) * HD)
        spread(own_out, jnp.transpose(band_v), (3 * h + 2) * HD)
        back_turn(cln_out, jnp.transpose(dkc_acc[h]) * HD**-0.5, 2 * h * HD)
        spread(cln_out, jnp.transpose(dvc_acc[h]), (2 * h + 1) * HD)


def attend_back(bounds, q, k, v, kc, vc, o, lse, do_mine, do_other, id_row, id_col, cos_t, sin_t,
                pair, group):
    total = q.shape[1]
    head = pl.BlockSpec((group * HD, total), lambda g, b: (pair, 0))
    halfhead = pl.BlockSpec((group * HD, total // 2), lambda g, b: (pair, 0))
    whole = lambda shape: pl.BlockSpec(shape, lambda g, b: (0, 0))
    rows16 = pltpu.VMEM((group, total, HD), BF)
    rows32 = pltpu.VMEM((group, total, HD), F32)
    outs = [(group * 3 * HD, total), (group * 2 * HD, total)]
    return pl.pallas_call(
        functools.partial(attend_back_kernel, group),
        grid_spec=pltpu.PrefetchScalarGridSpec(
            num_scalar_prefetch=1,
            grid=(1,),
            in_specs=[head] * 6
            + [pl.BlockSpec((group, 8, total), lambda g, b: (pair, 0, 0)), halfhead, halfhead]
            + [whole(id_row.shape), whole(id_col.shape), whole(cos_t.shape), whole(sin_t.shape)],
            out_specs=[whole(shape) for shape in outs],
            scratch_shapes=[rows16] * 6
            + [pltpu.VMEM((group * HD, total), BF)]
            + [rows32] * 4
            + [pltpu.VMEM((group * HD, total), F32)],
        ),
        out_shape=[jax.ShapeDtypeStruct(shape, BF) for shape in outs],
        cost_estimate=pl.CostEstimate(
            flops=20 * group * HD * total * total, bytes_accessed=8 * 2**20, transcendentals=0
        ),
        name="attend_back",
    )(bounds, q, k, v, kc, vc, o, lse, do_mine, do_other, id_row, id_col, cos_t, sin_t)


def finish_kernel(n, g, s, g_out, s_out, s_in, g_x, s_x, g_c, s_c, g_t, s_t, s_send, s_recv,
                  x_send, x_recv, c_send, c_recv, local):
    me = lax.axis_index("fsdp")
    seat = lax.axis_index("seq")
    core = lax.rem(seat, 2)
    across = {"seq": lax.rem(seat + 2, 4)}
    beside = {"seq": seat + 1 - 2 * core}
    mesh_id = pl.DeviceIdType.MESH
    barrier = pltpu.get_barrier_semaphore()
    peers = [{"fsdp": lax.rem(me + d, n)} for d in range(1, n)]
    for where in peers + [across, beside]:
        pl.semaphore_signal(barrier, inc=1, device_id=where, device_id_type=mesh_id)
    pl.semaphore_wait(barrier, n + 1)

    def push(src, dst, one, two, where):
        copy = pltpu.make_async_remote_copy(
            src_ref=src, dst_ref=dst, send_sem=one, recv_sem=two, device_id=where,
            device_id_type=mesh_id,
        )
        copy.start()
        return copy

    def settle(tmp, out, sem):
        copy = pltpu.make_async_copy(tmp, out, sem)
        copy.start()
        copy.wait()

    first = [
        push(s.at[lax.rem(me + d, n)], s_in.at[d - 1], s_send.at[d - 1], s_recv.at[d - 1],
             peers[d - 1])
        for d in range(1, n)
    ]
    far_g = push(g, g_x, x_send.at[0], x_recv.at[0], across)
    for copy in first:
        copy.wait()
    total = s[me]
    for d in range(n - 1):
        total = total + s_in[d]
    s_t[0] = total
    settle(s_t.at[0], s_x.at[0], local.at[0])
    far_s = push(s_x.at[0], s_x.at[1], x_send.at[1], x_recv.at[1], across)
    far_g.wait()
    g_t[...] = (g[...].astype(F32) + g_x[...].astype(F32)).astype(BF)
    settle(g_t, g_c.at[core], local.at[1])
    near_g = push(g_c.at[core], g_c.at[core], c_send.at[0], c_recv.at[0], beside)
    far_s.wait()
    s_t[1] = s_x[0] + s_x[1]
    settle(s_t.at[1], s_c.at[0], local.at[2])
    near_s = push(s_c.at[0], s_c.at[1], c_send.at[1], c_recv.at[1], beside)
    near_g.wait()
    span = g.shape[1]
    for c in range(2):
        g_out[:, c * span : (c + 1) * span] = g_c[c].astype(F32)
    near_s.wait()
    s_out[...] = s_c[0] + s_c[1]


def finish(g, s):
    n = s.shape[0]
    vm = pl.BlockSpec(memory_space=pltpu.VMEM)
    dma = pltpu.SemaphoreType.DMA
    return pl.pallas_call(
        functools.partial(finish_kernel, n),
        in_specs=[vm] * 2,
        out_specs=[vm] * 2,
        out_shape=[
            jax.ShapeDtypeStruct((g.shape[0], 2 * g.shape[1]), F32),
            jax.ShapeDtypeStruct(s.shape[1:], F32),
        ],
        scratch_shapes=[
            pltpu.VMEM((n - 1,) + s.shape[1:], F32),
            pltpu.VMEM(g.shape, BF),
            pltpu.VMEM((2,) + s.shape[1:], F32),
            pltpu.VMEM((2,) + g.shape, BF),
            pltpu.VMEM((2,) + s.shape[1:], F32),
            pltpu.VMEM(g.shape, BF),
            pltpu.VMEM((2,) + s.shape[1:], F32),
            dma((n - 1,)),
            dma((n - 1,)),
            dma((2,)),
            dma((2,)),
            dma((2,)),
            dma((2,)),
            dma((3,)),
        ],
        compiler_params=pltpu.CompilerParams(collective_id=1, has_side_effects=True),
        name="finish",
    )(g, s)


def assemble_kernel(span, n, core_ref, mine, other, d_mine, d_other, out_ref, up_ref, down_ref):
    first_core = core_ref[0] == 0
    pick = lambda one, two: (
        jnp.where(first_core, one, two).astype(F32), jnp.where(first_core, two, one).astype(F32)
    )
    pair = pick(mine[...].astype(F32), other[...].astype(F32))
    rows = pair[0].shape[0]
    half = (pair[0].shape[1] - span) // (2 * n)
    for c in range(2):
        out_ref[:, c * span : (c + 1) * span] = pair[c][:, :span]
    for i in range(n):
        up_ref[:, 4 * i * half : 4 * (i + 1) * half] = jnp.concatenate(
            [
                part[:, span + (j * n + i) * half : span + (j * n + i + 1) * half]
                for part in pair
                for j in range(2)
            ],
            1,
        )
    pair = pick(d_mine[...].astype(F32), d_other[...].astype(F32))
    width = down_ref.shape[1]
    for c in range(2):
        for j in range(2):
            at = (2 * c + j) * rows
            down_ref[at : at + rows, :] = pair[c][:, j * width : (j + 1) * width]


def assemble(core, mine, other, d_mine, d_other, span, n):
    rows, width = mine.shape
    vm = pl.BlockSpec(memory_space=pltpu.VMEM)
    return pl.pallas_call(
        functools.partial(assemble_kernel, span, n),
        in_specs=[pl.BlockSpec(memory_space=pltpu.SMEM)] + [vm] * 4,
        out_specs=[vm] * 3,
        out_shape=[
            jax.ShapeDtypeStruct((rows, 2 * span), F32),
            jax.ShapeDtypeStruct((rows, 2 * (width - span)), F32),
            jax.ShapeDtypeStruct((4 * rows, d_mine.shape[1] // 2), F32),
        ],
        name="assemble",
    )(core, mine, other, d_mine, d_other)


def on_device(
    tokens,
    block_ids,
    ln1_scale,
    ln1_bias,
    qkv_weight,
    qkv_bias,
    out_weight,
    out_bias,
    ln2_scale,
    ln2_bias,
    up_weight,
    up_bias,
    down_weight,
    down_bias,
    cotangent,
):
    tok = tokens[0]
    local_rows, width = tok.shape
    ids = block_ids[0].astype(jnp.int32)
    length = ids.shape[0]
    shard = ln1_scale.shape[0]
    heads = H // 2
    span = heads * HD
    me = lax.axis_index("seq")
    core = me % 2
    noisy = me < 2
    swap = [(0, 1), (1, 0), (2, 3), (3, 2)]
    other = lax.ppermute(tok, "seq", swap)
    clean_in = lax.ppermute(tok, "seq", [(2, 0), (3, 1)])
    cot_far = lax.ppermute(cotangent[0], "seq", swap)

    q_cols = lax.dynamic_slice_in_dim(qkv_weight, core * 3 * span, 3 * span, 1)
    small = jnp.concatenate(
        [
            ln1_scale.reshape(1, shard),
            ln1_bias.reshape(1, shard),
            out_bias.reshape(1, shard),
            ln2_scale.reshape(1, shard),
            ln2_bias.reshape(1, shard),
            down_bias.reshape(1, shard),
            qkv_bias.reshape(-1, shard),
            up_bias.reshape(-1, shard),
        ],
        0,
    )
    n_small = small.shape[0]
    small = jnp.pad(small, ((0, 128 - n_small), (0, 0))).T
    gathered = lax.all_gather(
        jnp.concatenate([q_cols, small], 1), "fsdp", axis=0, tiled=True
    )
    n_fsdp = width // shard
    vectors = gathered[:, 3 * span :].reshape(n_fsdp, shard, 128)[:, :, :n_small]
    vectors = jnp.transpose(vectors, (2, 0, 1)).astype(F32)
    flat = vectors[:6].reshape(6, width)
    qkv_b = jnp.transpose(vectors[6:9], (1, 0, 2)).reshape(-1)
    scale_one, shift_one, out_shift, scale_two, shift_two, down_shift = [flat[i] for i in range(6)]

    inner = up_bias.shape[0] // 2
    up_b = jnp.transpose(vectors[9:], (1, 0, 2)).reshape(n_fsdp, 2, inner)
    by_half = lambda a: jnp.swapaxes(a.reshape(-1, n_fsdp, 2, inner // 2), 1, 2)
    up_b = by_half(lax.dynamic_index_in_dim(up_b, core, 1, False)).reshape(-1)
    up_cols = by_half(
        lax.dynamic_index_in_dim(up_weight.reshape(shard, n_fsdp, 2, inner), core, 2, False)
    ).reshape(shard, n_fsdp * inner)
    down_rows = lax.dynamic_slice_in_dim(down_weight, core * inner, inner, 0)
    beside = lambda a: jnp.concatenate([a[: a.shape[0] // 2], a[a.shape[0] // 2 :]], 1)
    out_cols = lax.dynamic_slice_in_dim(out_weight, core * span, span, 1)
    ffn = lax.all_gather(
        jnp.concatenate([out_cols, up_cols, beside(down_rows)], 1), "fsdp", axis=0, tiled=True
    )
    in_order = lambda near, far, axis: jnp.where(
        core == 0, jnp.concatenate([near, far], axis), jnp.concatenate([far, near], axis)
    )

    frequency = jnp.exp(-jnp.log(10000.0) * jnp.arange(HD // 2, dtype=F32) / (HD // 2))
    angles = frequency[:, None] * jnp.arange(length, dtype=F32)[None, :]
    cos_t, sin_t = jnp.cos(angles), jnp.sin(angles)

    first = ids[::TQ][:, None]
    last = ids[TQ - 1 :: TQ][:, None]
    before = lambda edge: jnp.sum((ids[None, :] < edge).astype(jnp.int32), 1)
    start_first, end_first = before(first), before(first + 1)
    start_last, end_last = before(last), before(last + 1)
    lift = jnp.where(noisy, 0, 1)
    zero = jnp.zeros_like(start_first)

    def key_bounds(full, masked):
        ceil_m = lambda value: (value + masked - 1) // masked
        return jnp.stack(
            [
                jnp.where(noisy, start_first, end_first) // full,
                ceil_m(jnp.where(noisy, start_last, end_last)),
                jnp.where(noisy, start_first // masked, zero),
                jnp.where(noisy, ceil_m(end_last), zero),
                zero + jnp.where(jnp.arange(zero.shape[0]) == 0, lift, core),
            ]
        ).astype(jnp.int32)

    bounds, wide_bounds = key_bounds(TK, TM), key_bounds(FK, FK)
    id_row = jnp.broadcast_to(ids[None, :], (8, length))
    id_col = jnp.broadcast_to(ids[:, None], (length, 128))

    cot_both = jnp.concatenate([cotangent[0], cot_far], 0)
    clean_in, cot_both, cos_t, sin_t, bounds, wide_bounds, id_row, id_col = (
        lax.optimization_barrier(
            (clean_in, cot_both, cos_t, sin_t, bounds, wide_bounds, id_row, id_col)
        )
    )
    clean_far = lax.ppermute(clean_in, "seq", swap)

    vec = jnp.concatenate([scale_one[None], shift_one[None], jnp.zeros((6, width), F32)], 0)
    bias_own = lax.dynamic_slice_in_dim(qkv_b, core * 3 * span, 3 * span, 0)
    bias_own = jnp.transpose(bias_own.reshape(heads, 3, HD), (1, 0, 2)).reshape(3 * span, 1)
    q, k, v, kc, vc, a_own = project(
        jnp.stack([core, noisy.astype(core.dtype)]), tok, other, clean_in, clean_far, gathered, vec,
        bias_own, cos_t, sin_t, heads
    )
    o, lse = attend(wide_bounds, q, k, v, kc, vc, id_row, id_col, heads, 1)
    cut = lambda value, which: lax.dynamic_slice_in_dim(value, which * local_rows, local_rows, 1)
    o_mine = cut(o, core)
    o_in = lax.ppermute(cut(o, 1 - core), "seq", swap)
    o_mine, o_in, ffn = lax.optimization_barrier((o_mine, o_in, ffn))
    at = span + n_fsdp * inner
    out_near, up_own = ffn[:, :span], ffn[:, span:at]
    down_own = jnp.concatenate([ffn[:, at : at + width], ffn[:, at + width :]], 0)
    out_full = in_order(out_near, lax.ppermute(out_near, "seq", swap), 1)
    attended = in_order(o_mine, o_in, 0)

    rows_in = tok.astype(F32)
    hidden = rows_in + rows_contract(attended, out_full) + out_shift
    normed_two, inverse_two = normalize_parts(hidden)
    second_in = (normed_two * scale_two + shift_two).astype(BF)
    both_in = jnp.concatenate([second_in, lax.ppermute(second_in, "seq", swap)], 0)

    def join(product, rows):
        far = product(rows[local_rows:]).astype(BF)
        return product(rows[:local_rows]) + lax.ppermute(far, "seq", swap).astype(F32)

    pre_act = dot(both_in, up_own) + up_b
    root = (2 / math.pi) ** 0.5
    square = pre_act * pre_act
    bend = jnp.tanh(pre_act * (root + 0.044715 * root * square))
    rise = 0.5 + 0.5 * bend
    act_low = (pre_act * rise).astype(BF)
    curve = pre_act * (1 - bend * bend) * (0.5 * root + 1.5 * 0.044715 * root * square)
    slope = (rise + curve).astype(BF)
    grad_down_w = beside(rows_contract(act_low, cot_both).astype(BF))
    scatter = lambda grad: lax.psum_scatter(grad, "fsdp", scatter_dimension=0, tiled=True)
    act_low, slope, grad_down_w, cot_both = lax.optimization_barrier(
        (act_low, slope, grad_down_w, cot_both)
    )
    down_part = scatter(grad_down_w)
    result = hidden + join(lambda rows: dot(rows, down_own), act_low) + down_shift

    grad_top = cotangent[0].astype(F32)
    grad_down_b = jnp.sum(grad_top, 0)
    grad_pre = (right_transposed(cot_both, down_own) * slope.astype(F32)).astype(BF)
    grad_second = join(lambda rows: right_transposed(rows, up_own), grad_pre)
    grad_up_b = jnp.sum(grad_pre.astype(F32), 0)
    grad_up_w = rows_contract(both_in, grad_pre).astype(BF)
    grad_scale_two = jnp.sum(grad_second * normed_two, 0)
    grad_shift_two = jnp.sum(grad_second, 0)
    grad_hidden = grad_top + norm_backward(grad_second, normed_two, inverse_two, scale_two)

    grad_attn = grad_hidden.astype(BF)
    grad_out_w = dot(attended, grad_attn).astype(BF)
    grad_out_b = jnp.sum(grad_attn.astype(F32), 0)
    grad_o = right_transposed(out_full, grad_attn).astype(BF)
    cut_heads = lambda which: lax.dynamic_slice_in_dim(grad_o, which * span, span, 0)
    do_mine = cut_heads(core)
    do_in = lax.ppermute(cut_heads(1 - core), "seq", swap)
    cut_cols = lambda which: lax.dynamic_slice_in_dim(grad_out_w, which * span, span, 1)
    out_sum = (
        cut_cols(core).astype(F32) + lax.ppermute(cut_cols(1 - core), "seq", swap).astype(F32)
    ).astype(BF)
    do_mine, do_in, grad_up_w, out_sum = lax.optimization_barrier(
        (do_mine, do_in, grad_up_w, out_sum)
    )
    out_up_part = scatter(jnp.concatenate([out_sum, grad_up_w], 1))

    back_args = lambda mine: (
        bounds, q, k, v, kc, vc, o, lse, mine, do_in, id_row, id_col, cos_t, sin_t
    )
    hold = lax.optimization_barrier
    cross = [(0, 2), (1, 3), (2, 0), (3, 1)]
    to_clean = lambda send: lax.ppermute(send, "seq", [(0, 2), (1, 3)])
    pair_w = 2 * 3 * HD

    def joined(own, got):
        own = own.reshape(2, 3, HD, -1)
        key_value = own[:, 1:].astype(F32) + got.reshape(2, 2, HD, -1).astype(F32)
        return jnp.concatenate([own[:, :1], key_value.astype(BF)], 1).reshape(pair_w, -1)

    def weight_grad(own):
        return lax.dot_general(
            a_own, own, (((0,), (1,)), ((), ())), preferred_element_type=F32
        ).astype(BF)

    def back(own, first, count):
        cols = gathered[:, first * pair_w : (first + count) * pair_w]
        return lax.dot_general(
            own, cols, (((0,), (1,)), ((), ())), preferred_element_type=F32
        )

    own_0, send_0 = attend_back(*back_args(do_mine), 0, 2)
    send_0, do_mine = hold((send_0, do_mine))
    got_0 = to_clean(send_0)
    own_1, send_1 = attend_back(*back_args(do_mine), 1, 2)
    own_1, send_1, got_0, down_part = hold((own_1, send_1, got_0, down_part))
    got_1, down_far = to_clean(send_1), lax.ppermute(down_part, "seq", cross)
    own_0 = joined(own_0, got_0)
    grad_0, do_mine = hold((weight_grad(own_0), do_mine))
    own_2, send_2 = attend_back(*back_args(do_mine), 2, 2)
    own_2, send_2, got_1, down_far, out_up_part = hold(
        (own_2, send_2, got_1, down_far, out_up_part)
    )
    got_2 = to_clean(send_2)
    own_1 = joined(own_1, got_1)
    grad_01, own_1 = hold((jnp.concatenate([grad_0, weight_grad(own_1)], 1), own_1))
    exchange = lambda grad: lax.all_to_all(
        grad.reshape(n_fsdp, shard, grad.shape[1]), "fsdp", 0, 0
    )
    piece_sum = lambda pieces: functools.reduce(
        jnp.add, [pieces[d].astype(F32) for d in range(n_fsdp)]
    ).astype(BF)
    pieces_01 = exchange(grad_01)
    own_01 = jnp.concatenate([own_0, own_1], 0)
    first_01 = back(own_01, 0, 2)
    got_2, out_up_part, first_01 = hold((got_2, out_up_part, first_01))
    own_2 = joined(own_2, got_2)
    far_rows = (first_01[local_rows:] + back(own_2[:, local_rows:], 2, 1)).astype(BF)
    grad_2, far_rows = hold((weight_grad(own_2), far_rows))
    got_rows = lax.ppermute(far_rows, "seq", swap).astype(F32)
    grad_first = first_01[:local_rows] + back(own_2[:, :local_rows], 2, 1) + got_rows

    def chip_sum(part, far):
        total = (part.astype(F32) + far.astype(F32)).astype(BF)
        return total, lax.ppermute(total, "seq", swap)

    out_up_both = chip_sum(out_up_part, lax.ppermute(out_up_part, "seq", cross))
    out_g, up_g, down_g = assemble(
        core.reshape(1).astype(jnp.int32), *out_up_both, *chip_sum(down_part, down_far), span, n_fsdp
    )

    grad_2, pieces_01, out_g, up_g, down_g = hold((grad_2, pieces_01, out_g, up_g, down_g))
    pieces_2 = exchange(grad_2)
    sum_cols = lambda own: jnp.sum(own.astype(F32), 1)
    grad_qkv_b = jnp.concatenate([sum_cols(own_01), sum_cols(own_2)])
    normed_one, inverse_one = normalize_parts(rows_in)
    grad_scale_one = jnp.sum(grad_first * normed_one, 0)
    grad_shift_one = jnp.sum(grad_first, 0)
    grad_rows = grad_hidden + norm_backward(grad_first, normed_one, inverse_one, scale_one)

    qkv_b_wide = lax.dynamic_update_slice_in_dim(
        jnp.zeros((2 * 3 * span,), F32), grad_qkv_b, core * 3 * span, 0
    )
    up_b_wide = lax.dynamic_update_slice_in_dim(
        jnp.zeros((n_fsdp, 2, inner), F32),
        jnp.swapaxes(grad_up_b.reshape(2, n_fsdp, inner // 2), 0, 1).reshape(n_fsdp, 1, inner),
        core,
        1,
    )
    pieces = [
        piece.reshape(n_fsdp, -1)
        for piece in (
            grad_scale_one, grad_shift_one, qkv_b_wide, grad_out_b, grad_scale_two,
            grad_shift_two, up_b_wide, grad_down_b,
        )
    ]
    sizes = [piece.shape[1] for piece in pieces]
    packed = jnp.concatenate(pieces, 1)
    lines = -(-packed.shape[1] // 128)
    packed = jnp.pad(packed, ((0, 0), (0, lines * 128 - packed.shape[1])))
    packed = packed.reshape(n_fsdp, lines, 128)
    part_01 = piece_sum(pieces_01)
    grad_rows, out_g, up_g, down_g, packed, part_01, pieces_2 = hold(
        (grad_rows, out_g, up_g, down_g, packed, part_01, pieces_2)
    )
    qkv_part = jnp.concatenate([part_01, piece_sum(pieces_2)], 1)
    qkv_g, small_sum = finish(qkv_part, packed)
    small_sum = small_sum.reshape(-1)
    small_out, at = [], 0
    for size in sizes:
        small_out.append(small_sum[at : at + size])
        at += size
    return (
        result.astype(BF)[None],
        grad_rows[None],
        small_out[0],
        small_out[1],
        qkv_g,
        small_out[2],
        out_g,
        small_out[3],
        small_out[4],
        small_out[5],
        up_g,
        small_out[6],
        down_g,
        small_out[7],
    )


def solution(mesh):
    row, mat, vec = P("fsdp", "seq", None), P("fsdp", None), P("fsdp")
    in_specs = (row, mat, vec, vec, mat, vec, mat, vec, vec, vec, mat, vec, mat, vec, row)
    out_specs = (row, row, vec, vec, mat, vec, mat, vec, vec, vec, mat, vec, mat, vec)
    return jax.shard_map(
        on_device, mesh=mesh, in_specs=in_specs, out_specs=out_specs, check_vma=False
    )
```
